128 devices in a mesh: seg: 64 (over x, y, z), sub: 2 (over core).
Axes of the slice: x: 4, y: 4, z: 4, core: 2. Of those that a mesh axis runs over, the one named last changes fastest.
Arguments:
- start_field: float32 [3, 884736], P(None, ('seg', 'sub')), may hold values from -6 to 6
- element_loads: float32 [192, 32768], P(None, ('seg', 'sub')), may hold values from -6 to 6
- element_coefs: float32 [2, 32768], P(None, ('seg', 'sub')), may hold values from 0.2 to 5
- element_nodes: int32 [64, 32768], P(None, ('seg', 'sub')), may hold values from 0 to 7295, as said below
- move_list: int32 [3, 32768], P(None, ('seg', 'sub')), may hold values from 0 to 255, as said below
- face_nodes: int32 [2, 24576], P(None, ('seg', 'sub')), may hold values from 0 to 6911, as said below
- stiffness: float32 [2, 192, 192], replicated, as said below
Outputs:
- smoothed: float32 [3, 884736], P(None, ('seg', 'sub'))
- moved_loads: float32 [192, 32768], P(None, ('seg', 'sub'))
- moved_coefs: float32 [2, 32768], P(None, ('seg', 'sub'))
The draws below stay inside these ranges and needn't reach their ends.
Inputs may be any that keep to these rules, and one draw needn't show every extreme that they name: `move_list`: column e describes the record in slot e of its device before migration: row 0 its destination device p, row 1 its slot there, row 2 its place in the list that its device sends to p. A record that stays keeps its slot and has place 0. Every slot after migration receives exactly one record. A record leaves only for the device just before or after its own, with at most 16 records from one device to each and places below 16, or for a device two or more positions away, with at most 1 records from one device to one such device and places below 1; places are distinct for one source and destination. Both bounds are reached. `element_nodes`: column e lists the nodes of the element in slot e after migration in its device's numbering: values below 6912 are the device's own nodes, 6912 + s is entry s of face_nodes row 1 of the device before, 7104 + s entry s of face_nodes row 0 of the device after. The nodes of one element are distinct, every own node belongs to some element, the first device refers to no device before it and the last to none after it. `face_nodes`: for each device, row 0 lists own nodes that the device before refers to and row 1 those that the device after refers to; the 384 entries of one device are distinct. `stiffness`: both blocks are symmetric with positive diagonals and strictly diagonally dominant rows.
All inputs are finite; a program needn't handle non-finite values.
Results may differ from the reference program's by a relative error of at most 0.0001.
Values sent between devices are 32-bit elements; how exact they have to be, the bound alone decides.
No kernel may reach another device: no remote copies, remote signals or barrier semaphores. Data moves between devices by JAX's collectives and lax.ppermute only.
A program may use at most 128 MiB of HBM per device.

```python
import math
import jax
import jax.numpy as jnp
from jax import lax

ELEM_NODES = 64
DOFS = 192
ELEM_DEV = 256
NODE_DEV = 6912
FACE = 192
NEAR_CAP = 16
FAR_CAP = 1
DEGREE = 4
SWEEPS = 2
ELEMENTS = 32768
NODES = 884736


def draw_element_nodes(key, part):
    devices = ELEMENTS // ELEM_DEV
    key_order, key_mult, key_turn, key_shuffle = jax.random.split(jax.random.fold_in(key, 101), 4)
    orders = jax.vmap(lambda one_key: jax.random.permutation(one_key, NODE_DEV))(jax.random.split(key_order, devices)).astype(jnp.int32)
    element = jnp.arange(ELEM_DEV, dtype=jnp.int32)[None, None, :]
    offset = jnp.arange(ELEM_NODES, dtype=jnp.int32)[None, :, None]
    device = jnp.arange(devices, dtype=jnp.int32)[:, None, None]
    position = (27 * element + offset) % NODE_DEV
    own_nodes = jnp.take(orders, position[0], axis=1)
    rim_count = FACE // 16
    back_use = (offset < 16) & (element < rim_count) & (device > 0)
    back_node = NODE_DEV + 16 * element + offset
    ahead_use = (offset >= ELEM_NODES - 16) & (element >= ELEM_DEV - rim_count) & (device < devices - 1)
    ahead_node = NODE_DEV + FACE + 16 * (element - (ELEM_DEV - rim_count)) + offset - (ELEM_NODES - 16)
    window = jnp.where(back_use, back_node, jnp.where(ahead_use, ahead_node, own_nodes))
    multiplier = 2 * jax.random.randint(key_mult, (devices, 1, ELEM_DEV), 0, ELEM_NODES // 2) + 1
    rotation = jax.random.randint(key_turn, (devices, 1, ELEM_DEV), 0, ELEM_NODES)
    chosen = (offset * multiplier + rotation) % ELEM_NODES
    result = jnp.take_along_axis(window, chosen, axis=1)
    shuffle = jax.vmap(lambda one_key: jax.random.permutation(one_key, ELEM_DEV))(jax.random.split(key_shuffle, devices)).astype(jnp.int32)
    result = jnp.take_along_axis(result, shuffle[:, None, :], axis=2)
    return result.transpose(1, 0, 2).reshape(ELEM_NODES, ELEMENTS).astype(jnp.int32)


def draw_move_list(key, part):
    devices = ELEMENTS // ELEM_DEV
    key_near, key_peak, key_far, key_full, key_spot, key_amount = jax.random.split(jax.random.fold_in(key, 202), 6)
    levels = jax.random.randint(key_near, (devices - 1,), 0, 5)
    boundary = jnp.maximum(jnp.right_shift(jnp.full((devices - 1,), NEAR_CAP, jnp.int32), levels), 1)
    peak_index = jax.random.randint(key_peak, (), 0, devices - 1)
    boundary = boundary.at[peak_index].set(NEAR_CAP)
    middle = ELEM_DEV - 2 * NEAR_CAP
    layout = jax.vmap(lambda one_key: jax.random.permutation(one_key, middle))(jax.random.split(key_spot, devices)).astype(jnp.int32)
    position = jnp.argsort(layout, axis=1).astype(jnp.int32)
    device_row = jnp.arange(devices, dtype=jnp.int32)
    upper = device_row[:, None] < device_row[None, :]
    pick = jax.random.randint(key_far, (devices, devices), 0, 10)
    amount = jax.random.randint(key_amount, (devices, devices), 1, FAR_CAP + 1)
    pick_sym = jnp.where(upper, pick, pick.T)
    amount_sym = jnp.where(upper, amount, amount.T)
    counts = jnp.where(pick_sym == 0, amount_sym, 0)
    target = jax.random.randint(key_full, (), 0, devices)
    full_mark = (device_row[:, None] == target) | (device_row[None, :] == target)
    counts = jnp.where(full_mark, FAR_CAP, counts)
    slot = jnp.arange(ELEM_DEV, dtype=jnp.int32)[None, :]
    device = device_row[:, None]
    zero_one = jnp.zeros((1,), jnp.int32)
    tail_count = jnp.concatenate([boundary, zero_one])[device]
    head_count = jnp.concatenate([zero_one, boundary])[device]
    tail_move = slot >= ELEM_DEV - tail_count
    head_move = slot < head_count
    tail_place = slot - (ELEM_DEV - tail_count)
    in_middle = (slot >= NEAR_CAP) & (slot < ELEM_DEV - NEAR_CAP)
    middle_index = jnp.broadcast_to(jnp.clip(slot - NEAR_CAP, 0, middle - 1), (devices, ELEM_DEV))
    region = jnp.where(in_middle, jnp.take_along_axis(layout, middle_index, axis=1), devices * FAR_CAP)
    partner = region // FAR_CAP
    inner = region % FAR_CAP
    partner_safe = jnp.clip(partner, 0, devices - 1)
    far_move = in_middle & (partner < devices) & (jnp.abs(partner - device) >= 2) & (inner < counts[device, partner_safe])
    far_index = jnp.clip(device * FAR_CAP + inner, 0, middle - 1)
    far_slot = NEAR_CAP + position[partner_safe, far_index]
    target_device = jnp.where(tail_move, device + 1, jnp.where(head_move, device - 1, jnp.where(far_move, partner_safe, device)))
    target_slot = jnp.where(tail_move, tail_place, jnp.where(head_move, ELEM_DEV - head_count + slot, jnp.where(far_move, far_slot, slot)))
    list_place = jnp.where(tail_move, tail_place, jnp.where(head_move, slot, jnp.where(far_move, inner, 0)))
    stacked = jnp.stack([target_device * jnp.ones_like(slot), target_slot, list_place])
    return stacked.reshape(3, ELEMENTS).astype(jnp.int32)


def draw_face_nodes(key, part):
    devices = ELEMENTS // ELEM_DEV
    key_pick, key_mix = jax.random.split(jax.random.fold_in(key, 303), 2)
    picked = jax.vmap(lambda one_key: jax.random.permutation(one_key, NODE_DEV - 1)[:2 * FACE - 1])(jax.random.split(key_pick, devices))
    with_last = jnp.concatenate([picked.astype(jnp.int32), jnp.full((devices, 1), NODE_DEV - 1, jnp.int32)], axis=1)
    mixing = jax.vmap(lambda one_key: jax.random.permutation(one_key, 2 * FACE))(jax.random.split(key_mix, devices))
    mixed = jnp.take_along_axis(with_last, mixing.astype(jnp.int32), axis=1)
    return mixed.reshape(devices, 2, FACE).transpose(1, 0, 2).reshape(2, devices * FACE).astype(jnp.int32)


def draw_stiffness(key, part):
    key_size, key_sign, key_diag = jax.random.split(jax.random.fold_in(key, 404), 3)
    magnitude = jax.random.uniform(key_size, (2, DOFS, DOFS), jnp.float32, 0.5, 1.0)
    size_part = 0.5 * (magnitude + jnp.transpose(magnitude, (0, 2, 1)))
    sign_raw = jax.random.normal(key_sign, (2, DOFS), jnp.float32)
    sign_vector = jnp.where(sign_raw >= 0.0, 1.0, -1.0)
    block_sign = jnp.array([1.0, -1.0], jnp.float32)[:, None, None]
    sign_part = block_sign * sign_vector[:, :, None] * sign_vector[:, None, :]
    identity = jnp.eye(DOFS, dtype=jnp.float32)
    lift = jax.random.uniform(key_diag, (2, DOFS), jnp.float32, 0.0, 40.0)
    diag_part = (DOFS + lift)[:, :, None] * identity
    return ((size_part * sign_part * (1.0 - identity) + diag_part) / 232.0).astype(jnp.float32)


def shard_levels(stream_key, dims, cuts, smallest, top_value):
    def one(axis_at, blocks):
        heights = jax.random.uniform(jax.random.fold_in(jax.random.fold_in(stream_key, 6), axis_at), (blocks,), jnp.float32, smallest / len(cuts), top_value / len(cuts))
        return jnp.repeat(jnp.exp(heights), dims[axis_at] // blocks).reshape((-1,) + (1,) * (len(dims) - axis_at - 1))

    gain = one(*cuts[0])
    for cut in cuts[1:]:
        gain = gain * one(*cut)
    return gain


def scatter_about(key, extent, scale, limit, cuts=(), held_as=jnp.bfloat16):
    level = shard_levels(key, extent, cuts, -0.22, 0.18) if cuts else 1.0
    values = jax.random.normal(key, extent, jnp.float32) * scale * level
    return jnp.minimum(jnp.maximum(values, -limit), limit).astype(held_as)


def setup_inputs(seed: int = 0) -> dict:
    splits = jax.random.split(jax.random.key(seed), 8)
    start_field = scatter_about(splits[0], (3, NODES), 1.0, 6.0, ((1, 128),), jnp.float32)
    element_loads = scatter_about(splits[1], (DOFS, ELEMENTS), 1.0, 6.0, ((1, 128),), jnp.float32)
    element_coefs = jnp.clip(jnp.exp(math.log(5.0) - 3.218876 * jax.random.uniform(splits[2], (2, ELEMENTS), jnp.float32) ** shard_levels(splits[2], (2, ELEMENTS), ((1, 128),), -0.2, 0.2)), 0.2, 5.0)
    element_nodes = draw_element_nodes(jax.random.fold_in(splits[7], 71), 0)
    move_list = draw_move_list(jax.random.fold_in(splits[7], 71), 0)
    face_nodes = draw_face_nodes(jax.random.fold_in(splits[7], 71), 0)
    stiffness = draw_stiffness(jax.random.fold_in(splits[7], 71), 0)
    return {"start_field": start_field, "element_loads": element_loads, "element_coefs": element_coefs, "element_nodes": element_nodes, "move_list": move_list, "face_nodes": face_nodes, "stiffness": stiffness}


center = 1.125
half_width = 0.875


def reference(start_field, element_loads, element_coefs, element_nodes, move_list, face_nodes, stiffness):
    devices = ELEMENTS // ELEM_DEV
    per_element = element_nodes.shape[0]
    dof_count = element_loads.shape[0]
    components = dof_count // per_element
    destination = move_list[0] * ELEM_DEV + move_list[1]
    moved_loads = jnp.zeros_like(element_loads).at[:, destination].set(element_loads)
    moved_coefs = jnp.zeros_like(element_coefs).at[:, destination].set(element_coefs)
    owner_device = (jnp.arange(ELEMENTS, dtype=jnp.int32) // ELEM_DEV)[None, :]
    face_lists = face_nodes.reshape(2, devices, FACE)
    slot_back = jnp.clip(element_nodes - NODE_DEV, 0, FACE - 1)
    slot_ahead = jnp.clip(element_nodes - NODE_DEV - FACE, 0, FACE - 1)
    prev_device = jnp.clip(owner_device - 1, 0, devices - 1)
    next_device = jnp.clip(owner_device + 1, 0, devices - 1)
    from_prev = prev_device * NODE_DEV + face_lists[1][prev_device, slot_back]
    from_next = next_device * NODE_DEV + face_lists[0][next_device, slot_ahead]
    global_nodes = jnp.where(element_nodes < NODE_DEV, owner_device * NODE_DEV + element_nodes,
                             jnp.where(element_nodes < NODE_DEV + FACE, from_prev, from_next))
    flat_nodes = global_nodes.reshape(-1).astype(jnp.int32)

    def assemble(values):
        channels = values.shape[0] // per_element
        return jnp.zeros((channels, NODES), jnp.float32).at[:, flat_nodes].add(values.reshape(channels, -1))

    def operate(field):
        gathered = field[:, flat_nodes].reshape(dof_count, ELEMENTS)
        part_first = jnp.dot(stiffness[0], gathered, precision=lax.Precision.HIGHEST, preferred_element_type=jnp.float32)
        part_second = jnp.dot(stiffness[1], gathered, precision=lax.Precision.HIGHEST, preferred_element_type=jnp.float32)
        return assemble(part_first * moved_coefs[0] + part_second * moved_coefs[1])

    diagonals = jnp.diagonal(stiffness, axis1=1, axis2=2)
    element_diag = diagonals[0][:, None] * moved_coefs[0] + diagonals[1][:, None] * moved_coefs[1]
    right_side = assemble(moved_loads)
    diagonal = assemble(element_diag)
    field = start_field
    scaled_center = center / half_width
    for sweep_index in range(SWEEPS):
        residual = right_side - operate(field)
        update = residual / (center * diagonal)
        ratio = 1.0 / scaled_center
        for degree_step in range(DEGREE):
            field = field + update
            if degree_step + 1 < DEGREE:
                residual = residual - operate(update)
                ratio_next = 1.0 / (2.0 * scaled_center - ratio)
                update = ratio_next * ratio * update + (2.0 * ratio_next / half_width) * residual / diagonal
                ratio = ratio_next
    return field, moved_loads, moved_coefs
```

```python
import functools

import jax
import jax.numpy as jnp
from jax import lax
from jax.experimental import pallas as pl
from jax.experimental.pallas import tpu as pltpu
from jax.sharding import PartitionSpec as P

NEAR_CAP = 16
DEGREE = 4
SWEEPS = 2
DEVICES = 128
ELEM = 256
DOFS = 192
PER = 64
OWN = 6912
FACE = 192
BACK_ROW = 27
AHEAD_ROW = 28
OWN_CHUNKS = OWN // 128
CHUNKS = 58
NODE_BLOCK = 8

center = 1.125
half_width = 0.875

AXES = ("seg", "sub")
F32 = jnp.float32
BF16 = jnp.bfloat16


def fill_table(table, rows, chunks):
    for c in range(3):
        for k in range(chunks):
            table[c * CHUNKS + k] = jnp.broadcast_to(rows(c, k), (8, 128))


def lane_gather(table, index, chunks):
    lane = index & 127
    chunk = index >> 7
    found = [jnp.zeros((8, 128), F32)] * 3
    for k in range(chunks):
        here = chunk == k
        for c in range(3):
            picked = jnp.take_along_axis(table[c * CHUNKS + k], lane, axis=1)
            found[c] = jnp.where(here, picked, found[c])
    return found


def gather_elements(table, nodes_ref, out_ref):
    def block(b, carry):
        row = pl.multiple_of(b * 8, 8)
        for half in range(2):
            lanes = slice(half * 128, half * 128 + 128)
            found = lane_gather(table, nodes_ref[pl.ds(row, 8), lanes], CHUNKS)
            for c in range(3):
                out_ref[pl.ds(c * PER + row, 8), lanes] = found[c]
        return carry

    lax.fori_loop(0, PER // 8, block, 0)


def split(x):
    high = x.astype(BF16).astype(F32)
    return high, x - high


def one_hot_sum(node_rows, value_rows):
    low = node_rows & 255
    high = node_rows >> 8
    row_of = lax.broadcasted_iota(jnp.int32, (32, 256), 0)
    lane_of = lax.broadcasted_iota(jnp.int32, (256, 256), 0)
    parts = [part for rows in value_rows for part in split(rows)]
    left, right = [], []
    for k in range(node_rows.shape[0]):
        here = high[k : k + 1, :] == row_of
        left.append(
            jnp.concatenate(
                [jnp.where(here, part[k : k + 1, :], 0.0) for part in parts], axis=0
            ).astype(BF16)
        )
        right.append(jnp.where(low[k : k + 1, :] == lane_of, 1.0, 0.0).astype(BF16))
    left = jnp.concatenate(left, axis=1)
    right = jnp.concatenate(right, axis=1)
    return lax.dot_general(left, right, (((1,), (1,)), ((), ())), preferred_element_type=F32)


def scatter_elements(nodes_ref, value_refs, sums_ref):
    sums_ref[...] = jnp.zeros_like(sums_ref)

    def block(b, carry):
        row = pl.multiple_of(b * NODE_BLOCK, NODE_BLOCK)
        values = [
            ref[pl.ds(c * PER + row, NODE_BLOCK), :] for ref in value_refs for c in range(3)
        ]
        sums_ref[...] += one_hot_sum(nodes_ref[pl.ds(row, NODE_BLOCK), :], values)
        return carry

    lax.fori_loop(0, PER // NODE_BLOCK, block, 0)


def add_parts(sums, first, channels):
    return jnp.concatenate(
        [
            sums[64 * (first + c) : 64 * (first + c) + 32]
            + sums[64 * (first + c) + 32 : 64 * (first + c) + 64]
            for c in range(channels)
        ],
        axis=0,
    )


def face_messages(table, state, places, to_before, to_after, row):
    found = lane_gather(table, places, OWN_CHUNKS)
    for c in range(3):
        got = found[c]
        turned = pltpu.roll(got, 64, 1)
        to_before[row + c : row + c + 1, :] = jnp.concatenate([got[0:1], got[1:2]], axis=1)
        to_after[row + c : row + c + 1, :] = jnp.concatenate([got[2:3], turned[1:2]], axis=1)
        if state is not None:
            back = 32 * c + BACK_ROW
            ahead = 32 * c + AHEAD_ROW
            to_before[row + 3 + c : row + 4 + c, :] = state[back : back + 1, :]
            to_after[row + 3 + c : row + 4 + c, :] = state[ahead : ahead + 1, :]


def state_rows(ref):
    return lambda c, k: ref[32 * c + k // 2 : 32 * c + k // 2 + 1, (k % 2) * 128 : (k % 2) * 128 + 128]


def completed(partial, before, after, lists, row):
    nodes = lists[0:2, :]
    values = [
        jnp.concatenate(
            [before[row + 3 + c : row + 4 + c, :], after[row + 3 + c : row + 4 + c, :]], axis=0
        )
        for c in range(3)
    ]
    shared = add_parts(one_hot_sum(nodes, values), 0, 3)
    line = lax.broadcasted_iota(jnp.int32, (32, 256), 0)
    ghost = jnp.concatenate(
        [
            jnp.where(
                line == BACK_ROW,
                before[row + c : row + c + 1, :],
                jnp.where(line == AHEAD_ROW, after[row + c : row + c + 1, :], 0.0),
            )
            for c in range(3)
        ],
        axis=0,
    )
    return partial + shared + ghost


def pack_kernel(
    loads_ref,
    coefs_ref,
    move_ref,
    face_ref,
    field_ref,
    far_ref,
    to_before,
    to_after,
    lists_ref,
    places_ref,
    table,
):
    me = lax.axis_index(AXES)
    away = move_ref[0:1, :] - me
    place = move_ref[2:3, :]
    code = jnp.where(
        away == 1,
        DEVICES + place,
        jnp.where(away == -1, DEVICES + NEAR_CAP + place, jnp.where(away == 0, -1, move_ref[0:1, :])),
    )
    rows = DEVICES + 2 * NEAR_CAP
    chosen = jnp.where(code == lax.broadcasted_iota(jnp.int32, (rows, ELEM), 0), 1.0, 0.0)
    slot = (move_ref[1:2, :] + 1).astype(F32)
    records = jnp.concatenate(
        [loads_ref[...], coefs_ref[...], slot, jnp.zeros((61, ELEM), F32)], axis=0
    )
    packed = lax.dot_general(
        chosen,
        records,
        (((1,), (1,)), ((), ())),
        precision=lax.Precision.HIGHEST,
        preferred_element_type=F32,
    )
    far_ref[...] = packed[:DEVICES]
    to_after[0:NEAR_CAP, :] = packed[DEVICES : DEVICES + NEAR_CAP]
    to_before[0:NEAR_CAP, :] = packed[DEVICES + NEAR_CAP :]
    to_after[NEAR_CAP:, :] = jnp.zeros((8, 256), F32)
    to_before[NEAR_CAP:, :] = jnp.zeros((8, 256), F32)
    lists_ref[...] = jnp.full((8, 256), -1, jnp.int32)
    lists_ref[0:2, 0:FACE] = face_ref[...]
    places_ref[...] = jnp.zeros((8, 128), jnp.int32)
    places_ref[0:1, :] = face_ref[0:1, 0:128]
    places_ref[1:2, 0:64] = face_ref[0:1, 128:192]
    places_ref[1:2, 64:128] = face_ref[1:2, 128:192]
    places_ref[2:3, :] = face_ref[1:2, 0:128]
    fill_table(table, lambda c, k: field_ref[c : c + 1, 128 * k : 128 * k + 128], OWN_CHUNKS)
    face_messages(table, None, places_ref[...], to_before, to_after, NEAR_CAP)


def first_kernel(
    field_ref,
    before,
    after,
    nodes_ref,
    stiff_ref,
    state_ref,
    index_ref,
    high_ref,
    low_ref,
    products_ref,
    table,
    gathered,
):
    state_ref[...] = jnp.zeros_like(state_ref)
    for c in range(3):
        for h in range(BACK_ROW):
            state_ref[32 * c + h : 32 * c + h + 1, :] = field_ref[c : c + 1, 256 * h : 256 * h + 256]
        row = NEAR_CAP + c
        state_ref[32 * c + BACK_ROW : 32 * c + BACK_ROW + 1, :] = before[row : row + 1, :]
        state_ref[32 * c + AHEAD_ROW : 32 * c + AHEAD_ROW + 1, :] = after[row : row + 1, :]
    nodes = nodes_ref[...]
    index_ref[...] = jnp.where(nodes >= OWN + FACE, nodes + 64, nodes)
    fill_table(table, state_rows(state_ref), CHUNKS)
    gather_elements(table, index_ref, gathered)
    x_high, x_low = split(gathered[...])
    x_high = x_high.astype(BF16)
    x_low = x_low.astype(BF16)
    for i in range(2):
        block_high, block_low = split(stiff_ref[i])
        block_high = block_high.astype(BF16)
        block_low = block_low.astype(BF16)
        high_ref[i] = block_high
        low_ref[i] = block_low
        products_ref[i] = (
            jnp.dot(block_high, x_low, preferred_element_type=F32)
            + jnp.dot(block_low, x_high, preferred_element_type=F32)
            + jnp.dot(block_high, x_high, preferred_element_type=F32)
        )


def place_kernel(
    loads_ref,
    coefs_ref,
    move_ref,
    far_ref,
    before,
    after,
    stiff_ref,
    products_ref,
    nodes_ref,
    places_ref,
    moved_loads,
    moved_coefs,
    partial_ref,
    diagonal_ref,
    to_before,
    to_after,
    sums,
    first_values,
    diag_values,
    table,
):
    me = lax.axis_index(AXES)
    received = jnp.concatenate([far_ref[...], before[0:NEAR_CAP, :], after[0:NEAR_CAP, :]], axis=0)
    rows = DEVICES + 2 * NEAR_CAP
    slot = received[:, DOFS + 2 : DOFS + 3].astype(jnp.int32)
    chosen = jnp.where(slot == lax.broadcasted_iota(jnp.int32, (rows, ELEM), 1) + 1, 1.0, 0.0)
    arrived = lax.dot_general(
        received,
        chosen,
        (((0,), (0,)), ((), ())),
        precision=lax.Precision.HIGHEST,
        preferred_element_type=F32,
    )
    stays = move_ref[0:1, :] == me
    loads = jnp.where(stays, loads_ref[...], 0.0) + arrived[:DOFS]
    coefs = jnp.where(stays, coefs_ref[...], 0.0) + arrived[DOFS : DOFS + 2]
    moved_loads[...] = loads
    moved_coefs[...] = coefs
    first_values[...] = loads - (products_ref[0] * coefs[0:1, :] + products_ref[1] * coefs[1:2, :])
    eye = lax.broadcasted_iota(jnp.int32, (DOFS, DOFS), 0) == lax.broadcasted_iota(
        jnp.int32, (DOFS, DOFS), 1
    )
    first_diag = jnp.sum(jnp.where(eye, stiff_ref[0], 0.0), axis=1, keepdims=True)
    second_diag = jnp.sum(jnp.where(eye, stiff_ref[1], 0.0), axis=1, keepdims=True)
    diag_values[...] = first_diag * coefs[0:1, :] + second_diag * coefs[1:2, :]
    scatter_elements(nodes_ref, [first_values, diag_values], sums)
    total = sums[...]
    partial_ref[...] = add_parts(total, 0, 3)
    diagonal_ref[...] = add_parts(total, 3, 3)
    to_before[12:16, :] = jnp.zeros((4, 256), F32)
    to_after[12:16, :] = jnp.zeros((4, 256), F32)
    for i, ref in enumerate((partial_ref, diagonal_ref)):
        fill_table(table, state_rows(ref), OWN_CHUNKS)
        face_messages(table, ref, places_ref[...], to_before, to_after, 6 * i)


def apply_operator(
    update_ref, nodes_ref, coefs_ref, high_ref, low_ref, places_ref, partial_ref, to_before, to_after,
    table, gathered, sums,
):
    fill_table(table, state_rows(update_ref), CHUNKS)
    gather_elements(table, nodes_ref, gathered)
    x = gathered[...]
    total = jnp.zeros((DOFS, ELEM), F32)
    for i in range(2):
        x_high, x_low = split(x * coefs_ref[i : i + 1, :])
        x_high = x_high.astype(BF16)
        x_low = x_low.astype(BF16)
        total += (
            jnp.dot(high_ref[i], x_low, preferred_element_type=F32)
            + jnp.dot(low_ref[i], x_high, preferred_element_type=F32)
            + jnp.dot(high_ref[i], x_high, preferred_element_type=F32)
        )
    gathered[...] = total
    scatter_elements(nodes_ref, [gathered], sums)
    partial_ref[...] = add_parts(sums[...], 0, 3)
    to_before[6:8, :] = jnp.zeros((2, 256), F32)
    to_after[6:8, :] = jnp.zeros((2, 256), F32)
    fill_table(table, state_rows(partial_ref), OWN_CHUNKS)
    face_messages(table, partial_ref, places_ref[...], to_before, to_after, 0)


def start_kernel(
    step,
    partial_ref,
    diagonal_ref,
    before,
    after,
    lists_ref,
    field_ref,
    nodes_ref,
    coefs_ref,
    high_ref,
    low_ref,
    places_ref,
    residual_out,
    inverse_out,
    update_out,
    field_out,
    partial_out,
    to_before,
    to_after,
    table,
    gathered,
    sums,
):
    residual = completed(partial_ref[...], before, after, lists_ref, 0)
    diagonal = completed(diagonal_ref[...], before, after, lists_ref, 6)
    inverse = jnp.where(diagonal == 0.0, 0.0, 1.0 / diagonal)
    update = step[1] * (residual * inverse)
    residual_out[...] = residual
    inverse_out[...] = inverse
    update_out[...] = update
    field_out[...] = field_ref[...] + update
    apply_operator(
        update_out, nodes_ref, coefs_ref, high_ref, low_ref, places_ref, partial_out, to_before,
        to_after, table, gathered, sums,
    )


def step_kernel(
    step,
    partial_ref,
    before,
    after,
    lists_ref,
    residual_ref,
    inverse_ref,
    update_ref,
    field_ref,
    nodes_ref,
    coefs_ref,
    high_ref,
    low_ref,
    places_ref,
    residual_out,
    update_out,
    field_out,
    partial_out,
    to_before,
    to_after,
    table,
    gathered,
    sums,
):
    residual = residual_ref[...] - completed(partial_ref[...], before, after, lists_ref, 0)
    update = step[1] * (residual * inverse_ref[...])
    if step[0]:
        update = step[0] * update_ref[...] + update
    residual_out[...] = residual
    update_out[...] = update
    field_out[...] = field_ref[...] + update
    apply_operator(
        update_out, nodes_ref, coefs_ref, high_ref, low_ref, places_ref, partial_out, to_before,
        to_after, table, gathered, sums,
    )


def last_kernel(
    step, partial_ref, before, after, lists_ref, residual_ref, inverse_ref, update_ref, field_ref, out_ref
):
    residual = residual_ref[...] - completed(partial_ref[...], before, after, lists_ref, 0)
    update = step[1] * (residual * inverse_ref[...])
    if step[0]:
        update = step[0] * update_ref[...] + update
    field = field_ref[...] + update
    for c in range(3):
        for h in range(BACK_ROW):
            out_ref[c : c + 1, 256 * h : 256 * h + 256] = field[32 * c + h : 32 * c + h + 1, :]


def shaped(*shape, dtype=F32):
    return jax.ShapeDtypeStruct(shape, dtype)


def steps():
    scaled_center = center / half_width
    found = []
    for _ in range(SWEEPS):
        found.append((0.0, 1.0 / center))
        ratio = 1.0 / scaled_center
        for _ in range(DEGREE - 1):
            ratio_next = 1.0 / (2.0 * scaled_center - ratio)
            found.append((ratio_next * ratio, 2.0 * ratio_next / half_width))
            ratio = ratio_next
    return found


def exchange(to_before, to_after):
    devices = DEVICES
    from_before = lax.ppermute(to_after, AXES, [(i, i + 1) for i in range(devices - 1)])
    from_after = lax.ppermute(to_before, AXES, [(i + 1, i) for i in range(devices - 1)])
    return from_before, from_after


TABLE = pltpu.VMEM((3 * CHUNKS, 8, 128), F32)
ELEMENT_ROWS = pltpu.VMEM((DOFS, ELEM), F32)
STATE = shaped(96, 256)


def local(
    start_field, element_loads, element_coefs, element_nodes, move_list, face_nodes, stiffness
):
    far, to_before, to_after, lists, places = pl.pallas_call(
        pack_kernel,
        out_shape=(
            shaped(DEVICES, 256),
            shaped(24, 256),
            shaped(24, 256),
            shaped(8, 256, dtype=jnp.int32),
            shaped(8, 128, dtype=jnp.int32),
        ),
        scratch_shapes=[TABLE],
        name="pack",
    )(element_loads, element_coefs, move_list, face_nodes, start_field)
    before, after = exchange(to_before, to_after)
    far = lax.all_to_all(far, AXES, split_axis=0, concat_axis=0, tiled=True)
    field, nodes, high, low, products = pl.pallas_call(
        first_kernel,
        out_shape=(
            STATE,
            shaped(PER, ELEM, dtype=jnp.int32),
            shaped(2, DOFS, DOFS, dtype=BF16),
            shaped(2, DOFS, DOFS, dtype=BF16),
            shaped(2, DOFS, ELEM),
        ),
        scratch_shapes=[TABLE, ELEMENT_ROWS],
        name="first",
    )(start_field, before, after, element_nodes, stiffness)
    moved_loads, moved_coefs, partial, diagonal, to_before, to_after = pl.pallas_call(
        place_kernel,
        out_shape=(
            shaped(DOFS, ELEM),
            shaped(2, ELEM),
            STATE,
            STATE,
            shaped(16, 256),
            shaped(16, 256),
        ),
        scratch_shapes=[pltpu.VMEM((384, 256), F32), ELEMENT_ROWS, ELEMENT_ROWS, TABLE],
        name="place",
    )(
        element_loads, element_coefs, move_list, far, before, after, stiffness, products, nodes,
        places,
    )
    before, after = exchange(to_before, to_after)
    plan = steps()
    scratch = [TABLE, ELEMENT_ROWS, pltpu.VMEM((192, 256), F32)]
    message = shaped(8, 256)
    residual, inverse, update, field, partial, to_before, to_after = pl.pallas_call(
        functools.partial(start_kernel, plan[0]),
        out_shape=(STATE, STATE, STATE, STATE, STATE, message, message),
        scratch_shapes=scratch,
        name="start",
    )(partial, diagonal, before, after, lists, field, nodes, moved_coefs, high, low, places)
    for step in plan[1:-1]:
        before, after = exchange(to_before, to_after)
        residual, update, field, partial, to_before, to_after = pl.pallas_call(
            functools.partial(step_kernel, step),
            out_shape=(STATE, STATE, STATE, STATE, message, message),
            scratch_shapes=scratch,
            name="step",
        )(
            partial, before, after, lists, residual, inverse, update, field, nodes, moved_coefs,
            high, low, places,
        )
    before, after = exchange(to_before, to_after)
    field = pl.pallas_call(
        functools.partial(last_kernel, plan[-1]), out_shape=shaped(3, OWN), name="last"
    )(partial, before, after, lists, residual, inverse, update, field)
    return field, moved_loads, moved_coefs


def solution(mesh):
    split_columns = P(None, AXES)
    return jax.shard_map(
        local,
        mesh=mesh,
        in_specs=(split_columns,) * 6 + (P(),),
        out_specs=(split_columns,) * 3,
        check_vma=False,
    )
```

```python
import functools

import jax
import jax.numpy as jnp
from jax import lax
from jax.experimental import pallas as pl
from jax.experimental.pallas import tpu as pltpu
from jax.sharding import PartitionSpec as P

NEAR_CAP = 16
DEGREE = 4
SWEEPS = 2
DEVICES = 128
ELEM = 256
DOFS = 192
PER = 64
OWN = 6912
FACE = 192
OWN_ROWS = OWN // 256
OWN_CHUNKS = OWN // 128
SHARED_ROWS = 6
BLOCK = 32

center = 1.125
half_width = 0.875

AXES = ("seg", "sub")
F32 = jnp.float32
BF16 = jnp.bfloat16


def split(x):
    high = x.astype(BF16).astype(F32)
    return high, x - high


def iota(shape, dimension):
    return lax.broadcasted_iota(jnp.int32, shape, dimension)


def lane_pick(rows, lane):
    return jnp.take_along_axis(rows, lane, axis=1)


def gather_own(state_ref, nodes_ref, out_ref, extra_ref=None, extra_out=None):
    def block(b, carry):
        row = pl.multiple_of(b * 8, 8)
        for half in range(2):
            lanes = slice(half * 128, half * 128 + 128)
            index = nodes_ref[pl.ds(row, 8), lanes]
            lane = index & 127
            chunk = index >> 7
            found = [jnp.zeros((8, 128), F32)] * (3 if extra_ref is None else 4)
            for k in range(OWN_CHUNKS):
                here = chunk == k
                part = slice((k % 2) * 128, (k % 2) * 128 + 128)
                for c in range(len(found)):
                    source, line = (state_ref, 32 * c + k // 2) if c < 3 else (extra_ref, k // 2)
                    values = jnp.broadcast_to(source[line : line + 1, part], (8, 128))
                    found[c] = jnp.where(here, lane_pick(values, lane), found[c])
            for c in range(3):
                out_ref[pl.ds(c * PER + row, 8), lanes] = found[c]
            if extra_ref is not None:
                extra_out[pl.ds(row, 8), lanes] = found[3]
        return carry

    lax.fori_loop(0, PER // 8, block, 0)


def gather_shared(shared_ref, index_ref, rows_ref, first_row):
    tables = [
        [
            jnp.broadcast_to(shared_ref[8 * c + r : 8 * c + r + 1, :], (8, 128))
            for r in range(SHARED_ROWS)
        ]
        for c in range(3)
    ]
    for b in range(PER // 8):
        for half in range(2):
            lanes = slice(half * 128, half * 128 + 128)
            index = index_ref[8 * b : 8 * b + 8, lanes]
            lane = index & 127
            chunk = index >> 7
            masks = [chunk == r for r in range(first_row, SHARED_ROWS)]
            for c in range(3):
                rows = slice(c * PER + 8 * b, c * PER + 8 * b + 8)
                found = rows_ref[rows, lanes]
                for r in range(first_row, SHARED_ROWS):
                    found = jnp.where(masks[r - first_row], lane_pick(tables[c][r], lane), found)
                rows_ref[rows, lanes] = found


def scatter_elements(nodes_ref, hot_ref, values_ref, high_ref, low_ref, sums_ref, channels):
    high, low = split(values_ref[...])
    high_ref[...] = high
    low_ref[...] = low
    sums_ref[...] = jnp.zeros_like(sums_ref)
    lines = iota((32, 256), 0).astype(F32).astype(BF16)
    zero = jnp.zeros((), BF16)

    def block(b, carry):
        row = pl.multiple_of(b * BLOCK, BLOCK)
        line = (nodes_ref[pl.ds(row, BLOCK), :] >> 8).astype(F32)
        left = []
        for k in range(BLOCK):
            here = line[k : k + 1, :].astype(BF16) == lines
            left.append(
                jnp.concatenate(
                    [
                        jnp.where(
                            here,
                            jnp.broadcast_to(ref[pl.ds(c * PER + row + k, 1), :], (32, 256)).astype(
                                BF16
                            ),
                            zero,
                        )
                        for ref in (high_ref, low_ref)
                        for c in range(channels)
                    ],
                    axis=0,
                )
            )
        left = jnp.concatenate(left, axis=1)
        right = hot_ref[pl.ds(pl.multiple_of(row * 256, 256), BLOCK * 256), :]
        sums_ref[...] += jnp.dot(left, right, preferred_element_type=F32)
        return carry

    lax.fori_loop(0, PER // BLOCK, block, 0)


def add_parts(sums_ref, first, channels):
    top = 32 * first
    low = top + 32 * channels
    return sums_ref[top : top + 96, :] + sums_ref[low : low + 96, :]


def expand_own_faces(places, channels, parts):
    lines = iota((32, 128), 0)
    lanes = iota((256, 128), 0)
    rows = []
    for values in channels:
        rest = values
        for _ in range(parts):
            high, rest = split(rest)
            rows.append(high)
    left, right = [], []
    for k in range(3):
        here = (places[k : k + 1, :] >> 8) == lines
        left.append(
            jnp.concatenate([jnp.where(here, r[k : k + 1, :], 0.0) for r in rows], axis=0).astype(BF16)
        )
        right.append(jnp.where((places[k : k + 1, :] & 255) == lanes, 1.0, 0.0).astype(BF16))
    sums = lax.dot_general(
        jnp.concatenate(left, axis=1),
        jnp.concatenate(right, axis=1),
        (((1,), (1,)), ((), ())),
        preferred_element_type=F32,
    )
    out = []
    for i in range(len(channels)):
        total = sums[32 * parts * i : 32 * parts * i + 32]
        for q in range(1, parts):
            start = 32 * (parts * i + q)
            total = total + sums[start : start + 32]
        out.append(total)
    return jnp.concatenate(out, axis=0)


def take_shared(state_ref, places, out_ref, base, ghosts):
    found = [[None] * 3 for _ in range(3)]
    line = iota((8, 128), 0)
    for r in range(3):
        place = jnp.broadcast_to(places[r : r + 1, :], (8, 128))
        lane = place & 127
        chunk = place >> 7
        masks = [
            [chunk == 2 * (8 * t + line) + half for half in range(2)] for t in range(4)
        ]
        for c in range(3):
            got = jnp.zeros((8, 128), F32)
            for t in range(4):
                for half in range(2):
                    values = state_ref[
                        32 * c + 8 * t : 32 * c + 8 * t + 8, half * 128 : half * 128 + 128
                    ]
                    got = jnp.where(masks[t][half], lane_pick(values, lane), got)
            found[c][r] = jnp.sum(got, axis=0, keepdims=True)
    for c in range(3):
        top = 32 * c + OWN_ROWS
        if ghosts:
            others = [
                state_ref[top : top + 1, 0:128],
                state_ref[top : top + 1, 128:256],
                state_ref[top + 1 : top + 2, 0:128],
                jnp.zeros((2, 128), F32),
            ]
        else:
            others = [jnp.zeros((5, 128), F32)]
        out_ref[base + 8 * c : base + 8 * c + 8, 0:128] = jnp.concatenate(found[c] + others, axis=0)


def from_neighbours(near_ref, far_ref, base):
    first_core = lax.axis_index("sub") == 0
    left = iota((1, 128), 1) < 64
    out = []
    for c in range(3):
        rows = slice(base + 8 * c, base + 8 * c + 8)
        near = near_ref[rows, 0:128]
        far = far_ref[rows, 0:128]
        before = jnp.where(first_core, far, near)
        after = jnp.where(first_core, near, far)
        before_turned = pltpu.roll(before, 64, 1)
        after_turned = pltpu.roll(after, 64, 1)
        out += [
            before[5:6],
            jnp.where(left, before_turned[4:5], after_turned[4:5]),
            after[3:4],
            before[2:3],
            jnp.where(left, before_turned[1:2], after_turned[1:2]),
            after[0:1],
            jnp.zeros((2, 128), F32),
        ]
    return jnp.concatenate(out, axis=0)


def pack_kernel(
    loads_ref, coefs_ref, move_ref, face_ref, field_ref, far_ref, near_out, other_out, places_ref, state_ref
):
    me = lax.axis_index(AXES)
    first_core = lax.axis_index("sub") == 0
    near = jnp.where(first_core, me + 1, me - 1)
    other = jnp.where(first_core, me - 1, me + 1)
    target = move_ref[0:1, :]
    place = move_ref[2:3, :]
    code = jnp.where(
        target == me,
        -1,
        jnp.where(
            target == near,
            DEVICES + place,
            jnp.where(target == other, DEVICES + NEAR_CAP + place, target),
        ),
    )
    rows = DEVICES + 2 * NEAR_CAP
    chosen = jnp.where(code == iota((rows, ELEM), 0), 1.0, 0.0)
    slot = (move_ref[1:2, :] + 1).astype(F32)
    records = jnp.concatenate(
        [loads_ref[...], coefs_ref[...], slot, jnp.zeros((61, ELEM), F32)], axis=0
    )
    packed = lax.dot_general(
        chosen,
        records,
        (((1,), (1,)), ((), ())),
        precision=lax.Precision.HIGHEST,
        preferred_element_type=F32,
    )
    far_ref[...] = packed[:DEVICES]
    near_out[0:NEAR_CAP, :] = packed[DEVICES : DEVICES + NEAR_CAP]
    other_out[0:NEAR_CAP, :] = packed[DEVICES + NEAR_CAP :]
    near_out[NEAR_CAP:, :] = jnp.zeros((24, 256), F32)
    places_ref[...] = jnp.zeros((8, 128), jnp.int32)
    places_ref[0:1, :] = face_ref[0:1, 0:128]
    places_ref[1:2, 0:64] = face_ref[0:1, 128:192]
    places_ref[1:2, 64:128] = face_ref[1:2, 128:192]
    places_ref[2:3, :] = face_ref[1:2, 0:128]
    state_ref[...] = jnp.zeros_like(state_ref)
    for c in range(3):
        for h in range(OWN_ROWS):
            state_ref[32 * c + h : 32 * c + h + 1, :] = field_ref[c : c + 1, 256 * h : 256 * h + 256]
    take_shared(state_ref, places_ref[...], near_out, NEAR_CAP, False)
    other_out[NEAR_CAP:, :] = near_out[NEAR_CAP:, :]


def index_kernel(
    state_ref,
    places_ref,
    nodes_ref,
    stiff_ref,
    index_ref,
    shared_index_ref,
    unshared_ref,
    hot_ref,
    high_ref,
    low_ref,
    gathered_ref,
    positions,
    found,
):
    nodes = nodes_ref[...]
    ghost = nodes - OWN
    ahead = ghost - FACE
    shared = jnp.where(ahead < 0, ghost, jnp.where(ahead < 128, ahead + 256, ahead + 64))
    index_ref[...] = jnp.where(ghost < 0, nodes, OWN + shared)
    places = places_ref[...]
    numbers = (128 * iota((3, 128), 0) + iota((3, 128), 1) + 1).astype(F32)
    positions[...] = expand_own_faces(places, [numbers], 2)
    line = iota((32, 256), 0)
    unshared_ref[...] = jnp.where((positions[...] == 0.0) & (line < OWN_ROWS), 1.0, 0.0)
    gather_own(state_ref, index_ref, gathered_ref, positions, found)
    shared_index_ref[...] = jnp.where(
        ghost < 0, found[...].astype(jnp.int32) - 1, shared + 3 * 128
    )
    for i in range(2):
        high, low = split(stiff_ref[i])
        high_ref[DOFS * i : DOFS * i + DOFS, :] = high.astype(BF16)
        low_ref[DOFS * i : DOFS * i + DOFS, :] = low.astype(BF16)
    found[...] = (index_ref[...] & 255).astype(F32)
    lanes = iota((16, 256), 1).astype(F32)

    for half in range(2):
        turned = found[:, half * 128 : half * 128 + 128].T
        for b in range(8):
            columns = turned[16 * b : 16 * b + 16]
            for n in range(PER):
                hot_ref[256 * n + half * 128 + 16 * b : 256 * n + half * 128 + 16 * b + 16, :] = (
                    jnp.where(columns[:, n : n + 1] == lanes, 1.0, 0.0).astype(BF16)
                )


def multiply_blocks(high_ref, low_ref, rows_ref):
    high, low = split(rows_ref[...])
    high = high.astype(BF16)
    low = low.astype(BF16)
    return (
        jnp.dot(low_ref[...], high, preferred_element_type=F32)
        + jnp.dot(high_ref[...], low, preferred_element_type=F32)
        + jnp.dot(high_ref[...], high, preferred_element_type=F32)
    )


def place_kernel(
    loads_ref,
    coefs_ref,
    move_ref,
    far_ref,
    near_in,
    other_in,
    field_message,
    stiff_ref,
    gathered_in,
    nodes_ref,
    shared_index_ref,
    places_ref,
    hot_ref,
    high_ref,
    low_ref,
    moved_loads,
    moved_coefs,
    partial_ref,
    diagonal_ref,
    shared_field,
    message,
    gathered,
    values,
    value_high,
    value_low,
    sums,
):
    shared_field[...] = field_message[NEAR_CAP:, 0:128] + from_neighbours(near_in, other_in, NEAR_CAP)
    gathered[...] = gathered_in[...]
    gather_shared(shared_field, shared_index_ref, gathered, 3)
    products = multiply_blocks(high_ref, low_ref, gathered)
    me = lax.axis_index(AXES)
    received = jnp.concatenate(
        [far_ref[...], near_in[0:NEAR_CAP, :], other_in[0:NEAR_CAP, :]], axis=0
    )
    rows = DEVICES + 2 * NEAR_CAP
    slot = received[:, DOFS + 2 : DOFS + 3].astype(jnp.int32)
    chosen = jnp.where(slot == iota((rows, ELEM), 1) + 1, 1.0, 0.0)
    arrived = lax.dot_general(
        received,
        chosen,
        (((0,), (0,)), ((), ())),
        precision=lax.Precision.HIGHEST,
        preferred_element_type=F32,
    )
    stays = move_ref[0:1, :] == me
    loads = jnp.where(stays, loads_ref[...], 0.0) + arrived[:DOFS]
    coefs = jnp.where(stays, coefs_ref[...], 0.0) + arrived[DOFS : DOFS + 2]
    moved_loads[...] = loads
    moved_coefs[...] = coefs
    values[0:DOFS, :] = loads - (products[:DOFS] * coefs[0:1, :] + products[DOFS:] * coefs[1:2, :])
    eye = iota((DOFS, DOFS), 0) == iota((DOFS, DOFS), 1)
    first_diag = jnp.sum(jnp.where(eye, stiff_ref[0], 0.0), axis=1, keepdims=True)
    second_diag = jnp.sum(jnp.where(eye, stiff_ref[1], 0.0), axis=1, keepdims=True)
    values[DOFS:, :] = first_diag * coefs[0:1, :] + second_diag * coefs[1:2, :]
    scatter_elements(nodes_ref, hot_ref, values, value_high, value_low, sums, 6)
    partial_ref[...] = add_parts(sums, 0, 6)
    diagonal_ref[...] = add_parts(sums, 3, 6)
    take_shared(partial_ref, places_ref[...], message, 0, True)
    take_shared(diagonal_ref, places_ref[...], message, 24, True)


def apply_operator(
    shared_update, gathered_in, shared_index_ref, nodes_ref, coefs_ref, places_ref, hot_ref, high_ref,
    low_ref, partial_ref, message, gathered, value_high, value_low, sums,
):
    gathered[...] = gathered_in[...]
    gather_shared(shared_update, shared_index_ref, gathered, 0)
    products = multiply_blocks(high_ref, low_ref, gathered)
    gathered[...] = products[:DOFS] * coefs_ref[0:1, :] + products[DOFS:] * coefs_ref[1:2, :]
    scatter_elements(nodes_ref, hot_ref, gathered, value_high, value_low, sums, 3)
    partial_ref[...] = add_parts(sums, 0, 3)
    take_shared(partial_ref, places_ref[...], message, 0, True)


def inverse_of(diagonal):
    return jnp.where(diagonal == 0.0, 0.0, 1.0 / diagonal)


def begin_unshared(
    step, partial_ref, diagonal_ref, unshared_ref, field_ref, nodes_ref, inverse_out, update_out,
    field_out, gathered_out,
):
    unshared = jnp.concatenate([unshared_ref[...]] * 3, axis=0)
    inverse = jnp.where(unshared > 0.0, inverse_of(diagonal_ref[...]), 0.0)
    update = step[1] * (partial_ref[...] * inverse)
    inverse_out[...] = inverse
    update_out[...] = update
    field_out[...] = field_ref[...] + update
    gather_own(update_out, nodes_ref, gathered_out)


def begin_shared(
    step, message_in, near_in, other_in, shared_field, gathered_in, shared_index_ref, nodes_ref,
    coefs_ref, places_ref, hot_ref, high_ref, low_ref, residual_out, inverse_out, update_out,
    field_out, partial_ref, message, gathered, value_high, value_low, sums,
):
    residual = message_in[0:24, :] + from_neighbours(near_in, other_in, 0)
    inverse = inverse_of(message_in[24:48, :] + from_neighbours(near_in, other_in, 24))
    update = step[1] * (residual * inverse)
    residual_out[...] = residual
    inverse_out[...] = inverse
    update_out[...] = update
    field_out[...] = shared_field[...] + update
    apply_operator(
        update_out, gathered_in, shared_index_ref, nodes_ref, coefs_ref, places_ref, hot_ref,
        high_ref, low_ref, partial_ref, message, gathered, value_high, value_low, sums,
    )


def next_update(step, residual, inverse, update):
    changed = step[1] * (residual * inverse)
    return step[0] * update + changed if step[0] else changed


def step_unshared(
    step, partial_ref, residual_ref, inverse_ref, update_ref, field_ref, nodes_ref, residual_out,
    update_out, field_out, gathered_out,
):
    residual = residual_ref[...] - partial_ref[...]
    update = next_update(step, residual, inverse_ref[...], update_ref[...])
    residual_out[...] = residual
    update_out[...] = update
    field_out[...] = field_ref[...] + update
    gather_own(update_out, nodes_ref, gathered_out)


def step_shared(
    step, message_in, near_in, other_in, residual_ref, inverse_ref, update_ref, field_ref,
    gathered_in, shared_index_ref, nodes_ref, coefs_ref, places_ref, hot_ref, high_ref, low_ref,
    residual_out, update_out, field_out, partial_ref, message, gathered, value_high, value_low, sums,
):
    residual = residual_ref[...] - (message_in[...] + from_neighbours(near_in, other_in, 0))
    update = next_update(step, residual, inverse_ref[...], update_ref[...])
    residual_out[...] = residual
    update_out[...] = update
    field_out[...] = field_ref[...] + update
    apply_operator(
        update_out, gathered_in, shared_index_ref, nodes_ref, coefs_ref, places_ref, hot_ref,
        high_ref, low_ref, partial_ref, message, gathered, value_high, value_low, sums,
    )


def last_unshared(step, partial_ref, residual_ref, inverse_ref, update_ref, field_ref, field_out):
    residual = residual_ref[...] - partial_ref[...]
    field_out[...] = field_ref[...] + next_update(step, residual, inverse_ref[...], update_ref[...])


def last_shared(
    step, message_in, near_in, other_in, residual_ref, inverse_ref, update_ref, shared_field,
    field_ref, unshared_ref, places_ref, out_ref,
):
    residual = residual_ref[...] - (message_in[...] + from_neighbours(near_in, other_in, 0))
    shared = shared_field[...] + next_update(step, residual, inverse_ref[...], update_ref[...])
    faces = expand_own_faces(places_ref[...], [shared[8 * c : 8 * c + 3] for c in range(3)], 3)
    unshared = jnp.concatenate([unshared_ref[...]] * 3, axis=0)
    field = jnp.where(unshared > 0.0, field_ref[...], faces)
    for c in range(3):
        for h in range(OWN_ROWS):
            out_ref[c : c + 1, 256 * h : 256 * h + 256] = field[32 * c + h : 32 * c + h + 1, :]


def shaped(*shape, dtype=F32):
    return jax.ShapeDtypeStruct(shape, dtype)


def steps():
    scaled_center = center / half_width
    found = []
    for _ in range(SWEEPS):
        found.append((0.0, 1.0 / center))
        ratio = 1.0 / scaled_center
        for _ in range(DEGREE - 1):
            ratio_next = 1.0 / (2.0 * scaled_center - ratio)
            found.append((ratio_next * ratio, 2.0 * ratio_next / half_width))
            ratio = ratio_next
    return found


NEAR_PAIRS = [(i, i ^ 1) for i in range(DEVICES)]
OTHER_PAIRS = [
    pair for i in range(1, DEVICES - 1, 2) for pair in ((i, i + 1), (i + 1, i))
]


def exchange(near_message, other_message):
    other = lax.ppermute(other_message, AXES, OTHER_PAIRS)
    near = lax.ppermute(near_message, AXES, NEAR_PAIRS)
    return near, other


def call(kernel, name, outs, scratch=(), limit=6):
    return pl.pallas_call(
        kernel,
        out_shape=outs,
        scratch_shapes=list(scratch),
        compiler_params=pltpu.CompilerParams(vmem_limit_bytes=limit << 20),
        name=name,
    )


STATE = shaped(96, 256)
SHARED = shaped(24, 128)
ELEMENT_ROWS = shaped(DOFS, ELEM)


def rows(count):
    return pltpu.VMEM((count, ELEM), F32)


def local(
    start_field, element_loads, element_coefs, element_nodes, move_list, face_nodes, stiffness
):
    integers = functools.partial(shaped, dtype=jnp.int32)
    far, near, other, places, field = call(
        pack_kernel,
        "pack",
        (shaped(DEVICES, 256), shaped(40, 256), shaped(40, 256), integers(8, 128), STATE),
    )(element_loads, element_coefs, move_list, face_nodes, start_field)
    field_message = near
    near, other = exchange(near, other)
    far = lax.all_to_all(far, AXES, split_axis=0, concat_axis=0, tiled=True)
    nodes, shared_index, unshared, hot, high, low, gathered = call(
        index_kernel,
        "index",
        (
            integers(PER, ELEM),
            integers(PER, ELEM),
            shaped(32, 256),
            shaped(PER * ELEM, 256, dtype=BF16),
            shaped(2 * DOFS, DOFS, dtype=BF16),
            shaped(2 * DOFS, DOFS, dtype=BF16),
            ELEMENT_ROWS,
        ),
        [rows(32), rows(PER)],
        16,
    )(field, places, element_nodes, stiffness)
    moved_loads, moved_coefs, partial, diagonal, shared_field, message = call(
        place_kernel,
        "place",
        (ELEMENT_ROWS, shaped(2, ELEM), STATE, STATE, SHARED, shaped(48, 128)),
        [rows(DOFS), rows(2 * DOFS), rows(2 * DOFS), rows(2 * DOFS), rows(384)],
        20,
    )(
        element_loads, element_coefs, move_list, far, near, other, field_message, stiffness,
        gathered, nodes, shared_index, places, hot, high, low,
    )
    near, other = exchange(message, message)
    plan = steps()
    fixed = (shared_index, nodes, moved_coefs, places, hot, high, low)
    scratch = [rows(DOFS)] * 3 + [rows(192)]
    residual = partial
    inverse, update, field, gathered = call(
        functools.partial(begin_unshared, plan[0]),
        "begin_unshared",
        (STATE, STATE, STATE, ELEMENT_ROWS),
    )(partial, diagonal, unshared, field, nodes)
    shared_residual, shared_inverse, shared_update, shared_field, partial, message = call(
        functools.partial(begin_shared, plan[0]),
        "begin_shared",
        (SHARED, SHARED, SHARED, SHARED, STATE, SHARED),
        scratch,
        16,
    )(message, near, other, shared_field, gathered, *fixed)
    for step in plan[1:-1]:
        near, other = exchange(message, message)
        residual, update, field, gathered = call(
            functools.partial(step_unshared, step),
            "unshared",
            (STATE, STATE, STATE, ELEMENT_ROWS),
        )(partial, residual, inverse, update, field, nodes)
        shared_residual, shared_update, shared_field, partial, message = call(
            functools.partial(step_shared, step),
            "shared",
            (SHARED, SHARED, SHARED, STATE, SHARED),
            scratch,
            16,
        )(
            message, near, other, shared_residual, shared_inverse, shared_update, shared_field,
            gathered, *fixed,
        )
    near, other = exchange(message, message)
    field = call(functools.partial(last_unshared, plan[-1]), "last_unshared", STATE)(
        partial, residual, inverse, update, field
    )
    field = call(functools.partial(last_shared, plan[-1]), "last_shared", shaped(3, OWN))(
        message, near, other, shared_residual, shared_inverse, shared_update, shared_field, field,
        unshared, places,
    )
    return field, moved_loads, moved_coefs


def solution(mesh):
    split_columns = P(None, AXES)
    return jax.shard_map(
        local,
        mesh=mesh,
        in_specs=(split_columns,) * 6 + (P(),),
        out_specs=(split_columns,) * 3,
        check_vma=False,
    )
```

```python
import functools

import jax
import jax.numpy as jnp
from jax import lax
from jax.experimental import pallas as pl
from jax.experimental.pallas import tpu as pltpu
from jax.sharding import PartitionSpec as P

NEAR_CAP = 16
DEGREE = 4
SWEEPS = 2
DEVICES = 128
ELEM = 256
DOFS = 192
PER = 64
OWN = 6912
FACE = 192
OWN_ROWS = OWN // 256
OWN_CHUNKS = OWN // 128
SHARED_ROWS = 6
BLOCK = 32

center = 1.125
half_width = 0.875

AXES = ("seg", "sub")
F32 = jnp.float32
BF16 = jnp.bfloat16


def split(x):
    high = x.astype(BF16).astype(F32)
    return high, x - high


def iota(shape, dimension):
    return lax.broadcasted_iota(jnp.int32, shape, dimension)


def lane_pick(rows, lane):
    return jnp.take_along_axis(rows, lane, axis=1)


def gather_own(state_ref, nodes_ref, out_ref, extra_ref=None, extra_out=None):
    def block(b, carry):
        row = pl.multiple_of(b * 8, 8)
        for half in range(2):
            lanes = slice(half * 128, half * 128 + 128)
            index = nodes_ref[pl.ds(row, 8), lanes]
            lane = index & 127
            chunk = index >> 7
            found = [jnp.zeros((8, 128), F32)] * (3 if extra_ref is None else 4)
            for k in range(OWN_CHUNKS):
                here = chunk == k
                part = slice((k % 2) * 128, (k % 2) * 128 + 128)
                for c in range(len(found)):
                    source, line = (state_ref, 32 * c + k // 2) if c < 3 else (extra_ref, k // 2)
                    values = jnp.broadcast_to(source[line : line + 1, part], (8, 128))
                    found[c] = jnp.where(here, lane_pick(values, lane), found[c])
            for c in range(3):
                out_ref[pl.ds(c * PER + row, 8), lanes] = found[c]
            if extra_ref is not None:
                extra_out[pl.ds(row, 8), lanes] = found[3]
        return carry

    lax.fori_loop(0, PER // 8, block, 0)


def gather_shared(shared_ref, index_ref, rows_ref, first_row):
    tables = [
        [
            jnp.broadcast_to(shared_ref[8 * c + r : 8 * c + r + 1, :], (8, 128))
            for r in range(SHARED_ROWS)
        ]
        for c in range(3)
    ]
    for b in range(PER // 8):
        for half in range(2):
            lanes = slice(half * 128, half * 128 + 128)
            index = index_ref[8 * b : 8 * b + 8, lanes]
            lane = index & 127
            chunk = index >> 7
            masks = [chunk == r for r in range(first_row, SHARED_ROWS)]
            for c in range(3):
                rows = slice(c * PER + 8 * b, c * PER + 8 * b + 8)
                found = rows_ref[rows, lanes]
                for r in range(first_row, SHARED_ROWS):
                    found = jnp.where(masks[r - first_row], lane_pick(tables[c][r], lane), found)
                rows_ref[rows, lanes] = found


def scatter_elements(nodes_ref, hot_ref, values_ref, high_ref, low_ref, sums_ref, channels):
    high, low = split(values_ref[...])
    high_ref[...] = high
    low_ref[...] = low
    sums_ref[...] = jnp.zeros_like(sums_ref)
    lines = iota((32, 256), 0).astype(F32).astype(BF16)
    zero = jnp.zeros((), BF16)

    def block(b, carry):
        row = pl.multiple_of(b * BLOCK, BLOCK)
        line = (nodes_ref[pl.ds(row, BLOCK), :] >> 8).astype(F32)
        left = []
        for k in range(BLOCK):
            here = line[k : k + 1, :].astype(BF16) == lines
            left.append(
                jnp.concatenate(
                    [
                        jnp.where(
                            here,
                            jnp.broadcast_to(ref[pl.ds(c * PER + row + k, 1), :], (32, 256)).astype(
                                BF16
                            ),
                            zero,
                        )
                        for ref in (high_ref, low_ref)
                        for c in range(channels)
                    ],
                    axis=0,
                )
            )
        left = jnp.concatenate(left, axis=1)
        right = hot_ref[pl.ds(pl.multiple_of(row * 256, 256), BLOCK * 256), :]
        sums_ref[...] += jnp.dot(left, right, preferred_element_type=F32)
        return carry

    lax.fori_loop(0, PER // BLOCK, block, 0)


def add_parts(sums_ref, first, channels):
    top = 32 * first
    low = top + 32 * channels
    return sums_ref[top : top + 96, :] + sums_ref[low : low + 96, :]


def expand_own_faces(places, channels, parts):
    lines = iota((32, 128), 0)
    lanes = iota((256, 128), 0)
    rows = []
    for values in channels:
        rest = values
        for _ in range(parts):
            high, rest = split(rest)
            rows.append(high)
    left, right = [], []
    for k in range(3):
        here = (places[k : k + 1, :] >> 8) == lines
        left.append(
            jnp.concatenate([jnp.where(here, r[k : k + 1, :], 0.0) for r in rows], axis=0).astype(BF16)
        )
        right.append(jnp.where((places[k : k + 1, :] & 255) == lanes, 1.0, 0.0).astype(BF16))
    sums = lax.dot_general(
        jnp.concatenate(left, axis=1),
        jnp.concatenate(right, axis=1),
        (((1,), (1,)), ((), ())),
        preferred_element_type=F32,
    )
    out = []
    for i in range(len(channels)):
        total = sums[32 * parts * i : 32 * parts * i + 32]
        for q in range(1, parts):
            start = 32 * (parts * i + q)
            total = total + sums[start : start + 32]
        out.append(total)
    return jnp.concatenate(out, axis=0)


def take_shared(state_ref, places, out_ref, base, ghosts):
    found = [[None] * 3 for _ in range(3)]
    line = iota((8, 128), 0)
    for r in range(3):
        place = jnp.broadcast_to(places[r : r + 1, :], (8, 128))
        lane = place & 127
        chunk = place >> 7
        masks = [
            [chunk == 2 * (8 * t + line) + half for half in range(2)] for t in range(4)
        ]
        for c in range(3):
            got = jnp.zeros((8, 128), F32)
            for t in range(4):
                for half in range(2):
                    values = state_ref[
                        32 * c + 8 * t : 32 * c + 8 * t + 8, half * 128 : half * 128 + 128
                    ]
                    got = jnp.where(masks[t][half], lane_pick(values, lane), got)
            found[c][r] = jnp.sum(got, axis=0, keepdims=True)
    for c in range(3):
        top = 32 * c + OWN_ROWS
        if ghosts:
            others = [
                state_ref[top : top + 1, 0:128],
                state_ref[top : top + 1, 128:256],
                state_ref[top + 1 : top + 2, 0:128],
                jnp.zeros((2, 128), F32),
            ]
        else:
            others = [jnp.zeros((5, 128), F32)]
        out_ref[base + 8 * c : base + 8 * c + 8, 0:128] = jnp.concatenate(found[c] + others, axis=0)


def from_neighbours(near_ref, far_ref, base):
    first_core = lax.axis_index("sub") == 0
    left = iota((1, 128), 1) < 64
    out = []
    for c in range(3):
        rows = slice(base + 8 * c, base + 8 * c + 8)
        near = near_ref[rows, 0:128]
        far = far_ref[rows, 0:128]
        before = jnp.where(first_core, far, near)
        after = jnp.where(first_core, near, far)
        before_turned = pltpu.roll(before, 64, 1)
        after_turned = pltpu.roll(after, 64, 1)
        out += [
            before[5:6],
            jnp.where(left, before_turned[4:5], after_turned[4:5]),
            after[3:4],
            before[2:3],
            jnp.where(left, before_turned[1:2], after_turned[1:2]),
            after[0:1],
            jnp.zeros((2, 128), F32),
        ]
    return jnp.concatenate(out, axis=0)


def pack_kernel(
    loads_hbm, coefs_hbm, move_hbm, face_hbm, field_hbm, nodes_hbm, stiff_hbm, far_ref, near_out,
    other_out, places_ref, state_ref, loads_ref, coefs_ref, move_ref, nodes_ref, stiff_ref,
    face_ref, field_ref, sems,
):
    pairs = (
        (move_hbm, move_ref),
        (coefs_hbm, coefs_ref),
        (loads_hbm, loads_ref),
        (face_hbm, face_ref),
        (field_hbm, field_ref),
        (nodes_hbm, nodes_ref),
        (stiff_hbm, stiff_ref),
    )
    copies = [
        pltpu.make_async_copy(source, target, sems.at[i]) for i, (source, target) in enumerate(pairs)
    ]
    for copy in copies:
        copy.start()
    for copy in copies:
        copy.wait()
    me = lax.axis_index(AXES)
    first_core = lax.axis_index("sub") == 0
    near = jnp.where(first_core, me + 1, me - 1)
    other = jnp.where(first_core, me - 1, me + 1)
    target = move_ref[0:1, :]
    place = move_ref[2:3, :]
    code = jnp.where(
        target == me,
        -1,
        jnp.where(
            target == near,
            DEVICES + place,
            jnp.where(target == other, DEVICES + NEAR_CAP + place, target),
        ),
    )
    rows = DEVICES + 2 * NEAR_CAP
    chosen = jnp.where(code == iota((rows, ELEM), 0), 1.0, 0.0)
    slot = (move_ref[1:2, :] + 1).astype(F32)
    records = jnp.concatenate(
        [loads_ref[...], coefs_ref[...], slot, jnp.zeros((61, ELEM), F32)], axis=0
    )
    packed = lax.dot_general(
        chosen,
        records,
        (((1,), (1,)), ((), ())),
        precision=lax.Precision.HIGHEST,
        preferred_element_type=F32,
    )
    far_ref[:, 0, :] = packed[:DEVICES]
    near_out[0:NEAR_CAP, :] = packed[DEVICES : DEVICES + NEAR_CAP]
    other_out[0:NEAR_CAP, :] = packed[DEVICES + NEAR_CAP :]
    near_out[NEAR_CAP:, :] = jnp.zeros((24, 256), F32)
    places_ref[...] = jnp.zeros((8, 128), jnp.int32)
    places_ref[0:1, :] = face_ref[0:1, 0:128]
    places_ref[1:2, 0:64] = face_ref[0:1, 128:192]
    places_ref[1:2, 64:128] = face_ref[1:2, 128:192]
    places_ref[2:3, :] = face_ref[1:2, 0:128]
    state_ref[...] = jnp.zeros_like(state_ref)
    for c in range(3):
        for h in range(OWN_ROWS):
            state_ref[32 * c + h : 32 * c + h + 1, :] = field_ref[c : c + 1, 256 * h : 256 * h + 256]
    take_shared(state_ref, places_ref[...], near_out, NEAR_CAP, False)
    other_out[NEAR_CAP:, :] = near_out[NEAR_CAP:, :]


def index_kernel(
    state_ref,
    places_ref,
    nodes_ref,
    stiff_ref,
    index_ref,
    shared_index_ref,
    unshared_ref,
    high_ref,
    low_ref,
    gathered_ref,
    positions,
    found,
):
    nodes = nodes_ref[...]
    ghost = nodes - OWN
    ahead = ghost - FACE
    shared = jnp.where(ahead < 0, ghost, jnp.where(ahead < 128, ahead + 256, ahead + 64))
    index_ref[...] = jnp.where(ghost < 0, nodes, OWN + shared)
    places = places_ref[...]
    numbers = (128 * iota((3, 128), 0) + iota((3, 128), 1) + 1).astype(F32)
    positions[...] = expand_own_faces(places, [numbers], 2)
    line = iota((32, 256), 0)
    unshared_ref[...] = jnp.where((positions[...] == 0.0) & (line < OWN_ROWS), 1.0, 0.0)
    gather_own(state_ref, index_ref, gathered_ref, positions, found)
    shared_index_ref[...] = jnp.where(
        ghost < 0, found[...].astype(jnp.int32) - 1, shared + 3 * 128
    )
    for i in range(2):
        high, low = split(stiff_ref[i])
        high_ref[DOFS * i : DOFS * i + DOFS, :] = high.astype(BF16)
        low_ref[DOFS * i : DOFS * i + DOFS, :] = low.astype(BF16)


def build_hot(nodes_ref, hot_ref):
    low = (nodes_ref[...] & 255).astype(F32)
    lanes = iota((16, 256), 1).astype(F32).astype(BF16)
    one = jnp.ones((), BF16)
    zero = jnp.zeros((), BF16)
    for half in range(2):
        turned = low[:, half * 128 : half * 128 + 128].T.astype(BF16)
        for b in range(8):
            columns = turned[16 * b : 16 * b + 16]
            for n in range(PER):
                top = 256 * n + half * 128 + 16 * b
                column = jnp.broadcast_to(columns[:, n : n + 1], (16, 256))
                hot_ref[top : top + 16, :] = jnp.where(column == lanes, one, zero)


def multiply_blocks(high_ref, low_ref, rows_ref):
    high, low = split(rows_ref[...])
    high = high.astype(BF16)
    low = low.astype(BF16)
    return (
        jnp.dot(low_ref[...], high, preferred_element_type=F32)
        + jnp.dot(high_ref[...], low, preferred_element_type=F32)
        + jnp.dot(high_ref[...], high, preferred_element_type=F32)
    )


def place_kernel(
    loads_ref,
    coefs_ref,
    move_ref,
    far_ref,
    near_in,
    other_in,
    field_message,
    stiff_ref,
    gathered_in,
    nodes_ref,
    shared_index_ref,
    places_ref,
    high_ref,
    low_ref,
    hot_ref,
    moved_loads,
    moved_coefs,
    coefs_out,
    partial_ref,
    diagonal_ref,
    shared_field,
    message,
    gathered,
    values,
    value_high,
    value_low,
    sums,
):
    shared_field[...] = field_message[NEAR_CAP:, 0:128] + from_neighbours(near_in, other_in, NEAR_CAP)
    gathered[...] = gathered_in[...]
    gather_shared(shared_field, shared_index_ref, gathered, 3)
    products = multiply_blocks(high_ref, low_ref, gathered)
    me = lax.axis_index(AXES)
    received = jnp.concatenate(
        [far_ref[:, 0, :], near_in[0:NEAR_CAP, :], other_in[0:NEAR_CAP, :]], axis=0
    )
    rows = DEVICES + 2 * NEAR_CAP
    slot = received[:, DOFS + 2 : DOFS + 3].astype(jnp.int32)
    chosen = jnp.where(slot == iota((rows, ELEM), 1) + 1, 1.0, 0.0)
    arrived = lax.dot_general(
        received,
        chosen,
        (((0,), (0,)), ((), ())),
        precision=lax.Precision.HIGHEST,
        preferred_element_type=F32,
    )
    stays = move_ref[0:1, :] == me
    loads = jnp.where(stays, loads_ref[...], 0.0) + arrived[:DOFS]
    coefs = jnp.where(stays, coefs_ref[...], 0.0) + arrived[DOFS : DOFS + 2]
    moved_loads[...] = loads
    moved_coefs[...] = coefs
    coefs_out[...] = coefs
    values[0:DOFS, :] = loads - (products[:DOFS] * coefs[0:1, :] + products[DOFS:] * coefs[1:2, :])
    eye = iota((DOFS, DOFS), 0) == iota((DOFS, DOFS), 1)
    first_diag = jnp.sum(jnp.where(eye, stiff_ref[0], 0.0), axis=1, keepdims=True)
    second_diag = jnp.sum(jnp.where(eye, stiff_ref[1], 0.0), axis=1, keepdims=True)
    values[DOFS:, :] = first_diag * coefs[0:1, :] + second_diag * coefs[1:2, :]
    build_hot(nodes_ref, hot_ref)
    scatter_elements(nodes_ref, hot_ref, values, value_high, value_low, sums, 6)
    partial_ref[...] = add_parts(sums, 0, 6)
    diagonal_ref[...] = add_parts(sums, 3, 6)
    take_shared(partial_ref, places_ref[...], message, 0, True)
    take_shared(diagonal_ref, places_ref[...], message, 24, True)


def apply_operator(
    shared_update, gathered_in, shared_index_ref, nodes_ref, coefs_ref, places_ref, hot_ref, high_ref,
    low_ref, partial_ref, message, gathered, value_high, value_low, sums,
):
    gathered[...] = gathered_in[...]
    gather_shared(shared_update, shared_index_ref, gathered, 0)
    products = multiply_blocks(high_ref, low_ref, gathered)
    gathered[...] = products[:DOFS] * coefs_ref[0:1, :] + products[DOFS:] * coefs_ref[1:2, :]
    scatter_elements(nodes_ref, hot_ref, gathered, value_high, value_low, sums, 3)
    partial_ref[...] = add_parts(sums, 0, 3)
    take_shared(partial_ref, places_ref[...], message, 0, True)


def inverse_of(diagonal):
    return jnp.where(diagonal == 0.0, 0.0, 1.0 / diagonal)


def begin_unshared(
    step, partial_ref, diagonal_ref, unshared_ref, field_ref, nodes_ref, inverse_out, update_out,
    field_out, gathered_out,
):
    unshared = jnp.concatenate([unshared_ref[...]] * 3, axis=0)
    inverse = jnp.where(unshared > 0.0, inverse_of(diagonal_ref[...]), 0.0)
    update = step[1] * (partial_ref[...] * inverse)
    inverse_out[...] = inverse
    update_out[...] = update
    field_out[...] = field_ref[...] + update
    gather_own(update_out, nodes_ref, gathered_out)


def begin_shared(
    step, message_in, near_in, other_in, shared_field, gathered_in, shared_index_ref, nodes_ref,
    coefs_ref, places_ref, hot_ref, high_ref, low_ref, residual_out, inverse_out, update_out,
    field_out, partial_ref, message, gathered, value_high, value_low, sums,
):
    residual = message_in[0:24, :] + from_neighbours(near_in, other_in, 0)
    inverse = inverse_of(message_in[24:48, :] + from_neighbours(near_in, other_in, 24))
    update = step[1] * (residual * inverse)
    residual_out[...] = residual
    inverse_out[...] = inverse
    update_out[...] = update
    field_out[...] = shared_field[...] + update
    apply_operator(
        update_out, gathered_in, shared_index_ref, nodes_ref, coefs_ref, places_ref, hot_ref,
        high_ref, low_ref, partial_ref, message, gathered, value_high, value_low, sums,
    )


def next_update(step, residual, inverse, update):
    changed = step[1] * (residual * inverse)
    return step[0] * update + changed if step[0] else changed


def step_unshared(
    step, partial_ref, residual_ref, inverse_ref, update_ref, field_ref, nodes_ref, residual_out,
    update_out, field_out, gathered_out,
):
    residual = residual_ref[...] - partial_ref[...]
    update = next_update(step, residual, inverse_ref[...], update_ref[...])
    residual_out[...] = residual
    update_out[...] = update
    field_out[...] = field_ref[...] + update
    gather_own(update_out, nodes_ref, gathered_out)


def step_shared(
    step, message_in, near_in, other_in, residual_ref, inverse_ref, update_ref, field_ref,
    gathered_in, shared_index_ref, nodes_ref, coefs_ref, places_ref, hot_ref, high_ref, low_ref,
    residual_out, update_out, field_out, partial_ref, message, gathered, value_high, value_low, sums,
):
    residual = residual_ref[...] - (message_in[...] + from_neighbours(near_in, other_in, 0))
    update = next_update(step, residual, inverse_ref[...], update_ref[...])
    residual_out[...] = residual
    update_out[...] = update
    field_out[...] = field_ref[...] + update
    apply_operator(
        update_out, gathered_in, shared_index_ref, nodes_ref, coefs_ref, places_ref, hot_ref,
        high_ref, low_ref, partial_ref, message, gathered, value_high, value_low, sums,
    )


def last_unshared(step, partial_ref, residual_ref, inverse_ref, update_ref, field_ref, field_out):
    residual = residual_ref[...] - partial_ref[...]
    field_out[...] = field_ref[...] + next_update(step, residual, inverse_ref[...], update_ref[...])


def last_shared(
    step, message_in, near_in, other_in, residual_ref, inverse_ref, update_ref, shared_field,
    field_ref, unshared_ref, places_ref, out_ref,
):
    residual = residual_ref[...] - (message_in[...] + from_neighbours(near_in, other_in, 0))
    shared = shared_field[...] + next_update(step, residual, inverse_ref[...], update_ref[...])
    faces = expand_own_faces(places_ref[...], [shared[8 * c : 8 * c + 3] for c in range(3)], 3)
    unshared = jnp.concatenate([unshared_ref[...]] * 3, axis=0)
    field = jnp.where(unshared > 0.0, field_ref[...], faces)
    for c in range(3):
        for h in range(OWN_ROWS):
            out_ref[c : c + 1, 256 * h : 256 * h + 256] = field[32 * c + h : 32 * c + h + 1, :]


def shaped(*shape, dtype=F32):
    return jax.ShapeDtypeStruct(shape, dtype)


def steps():
    scaled_center = center / half_width
    found = []
    for _ in range(SWEEPS):
        found.append((0.0, 1.0 / center))
        ratio = 1.0 / scaled_center
        for _ in range(DEGREE - 1):
            ratio_next = 1.0 / (2.0 * scaled_center - ratio)
            found.append((ratio_next * ratio, 2.0 * ratio_next / half_width))
            ratio = ratio_next
    return found


NEAR_PAIRS = [(i, i ^ 1) for i in range(DEVICES)]
OTHER_PAIRS = [
    pair for i in range(1, DEVICES - 1, 2) for pair in ((i, i + 1), (i + 1, i))
]


def exchange(near_message, other_message):
    other = lax.ppermute(other_message, AXES, OTHER_PAIRS)
    near = lax.ppermute(near_message, AXES, NEAR_PAIRS)
    return near, other


def call(kernel, name, outs, scratch=(), **options):
    return pl.pallas_call(
        kernel,
        out_shape=outs,
        scratch_shapes=list(scratch),
        compiler_params=pltpu.CompilerParams(vmem_limit_bytes=20 << 20),
        name=name,
        **options,
    )


STATE = shaped(96, 256)
SHARED = shaped(24, 128)
ELEMENT_ROWS = shaped(DOFS, ELEM)


def rows(count):
    return pltpu.VMEM((count, ELEM), F32)


def local(
    start_field, element_loads, element_coefs, element_nodes, move_list, face_nodes, stiffness
):
    integers = functools.partial(shaped, dtype=jnp.int32)
    far, near, other, places, field, loads, coefs, moves, nodes, stiff = call(
        pack_kernel,
        "pack",
        (
            shaped(DEVICES, 1, 256),
            shaped(40, 256),
            shaped(40, 256),
            integers(8, 128),
            STATE,
            ELEMENT_ROWS,
            shaped(2, ELEM),
            integers(3, ELEM),
            integers(PER, ELEM),
            shaped(2, DOFS, DOFS),
        ),
        [
            pltpu.VMEM((2, FACE), jnp.int32),
            pltpu.VMEM((3, OWN), F32),
            pltpu.SemaphoreType.DMA((7,)),
        ],
        in_specs=[pl.BlockSpec(memory_space=pltpu.HBM)] * 7,
    )(*[pltpu.with_memory_space_constraint(x, pltpu.HBM) for x in (element_loads, element_coefs, move_list, face_nodes, start_field, element_nodes, stiffness)])
    field_message = near
    near, other = exchange(near, other)
    far = lax.all_to_all(far, AXES, split_axis=0, concat_axis=0, tiled=True)
    nodes, shared_index, unshared, high, low, gathered = call(
        index_kernel,
        "index",
        (
            integers(PER, ELEM),
            integers(PER, ELEM),
            shaped(32, 256),
            shaped(2 * DOFS, DOFS, dtype=BF16),
            shaped(2 * DOFS, DOFS, dtype=BF16),
            ELEMENT_ROWS,
        ),
        [rows(32), rows(PER)],
    )(field, places, nodes, stiff)
    hot, moved_loads, moved_coefs, coefs, partial, diagonal, shared_field, message = call(
        place_kernel,
        "place",
        (
            shaped(PER * ELEM, 256, dtype=BF16),
            ELEMENT_ROWS,
            shaped(2, ELEM),
            shaped(2, ELEM),
            STATE,
            STATE,
            SHARED,
            shaped(48, 128),
        ),
        [rows(DOFS), rows(2 * DOFS), rows(2 * DOFS), rows(2 * DOFS), rows(384)],
    )(
        loads, coefs, moves, far, near, other, field_message, stiff,
        gathered, nodes, shared_index, places, high, low,
    )
    near, other = exchange(message, message)
    plan = steps()
    fixed = (shared_index, nodes, coefs, places, hot, high, low)
    scratch = [rows(DOFS)] * 3 + [rows(192)]
    residual = partial
    inverse, update, field, gathered = call(
        functools.partial(begin_unshared, plan[0]),
        "begin_unshared",
        (STATE, STATE, STATE, ELEMENT_ROWS),
    )(partial, diagonal, unshared, field, nodes)
    shared_residual, shared_inverse, shared_update, shared_field, partial, message = call(
        functools.partial(begin_shared, plan[0]),
        "begin_shared",
        (SHARED, SHARED, SHARED, SHARED, STATE, SHARED),
        scratch,
    )(message, near, other, shared_field, gathered, *fixed)
    for step in plan[1:-1]:
        near, other = exchange(message, message)
        residual, update, field, gathered = call(
            functools.partial(step_unshared, step),
            "unshared",
            (STATE, STATE, STATE, ELEMENT_ROWS),
        )(partial, residual, inverse, update, field, nodes)
        shared_residual, shared_update, shared_field, partial, message = call(
            functools.partial(step_shared, step),
            "shared",
            (SHARED, SHARED, SHARED, STATE, SHARED),
            scratch,
        )(
            message, near, other, shared_residual, shared_inverse, shared_update, shared_field,
            gathered, *fixed,
        )
    near, other = exchange(message, message)
    field = call(functools.partial(last_unshared, plan[-1]), "last_unshared", STATE)(
        partial, residual, inverse, update, field
    )
    field = call(functools.partial(last_shared, plan[-1]), "last_shared", shaped(3, OWN))(
        message, near, other, shared_residual, shared_inverse, shared_update, shared_field, field,
        unshared, places,
    )
    return field, moved_loads, moved_coefs


def solution(mesh):
    split_columns = P(None, AXES)
    return jax.shard_map(
        local,
        mesh=mesh,
        in_specs=(split_columns,) * 6 + (P(),),
        out_specs=(split_columns,) * 3,
        check_vma=False,
    )
```

```python
import functools

import jax
import jax.numpy as jnp
from jax import lax
from jax.experimental import pallas as pl
from jax.experimental.pallas import tpu as pltpu
from jax.sharding import PartitionSpec as P

NEAR_CAP = 16
DEGREE = 4
SWEEPS = 2
DEVICES = 128
ELEM = 256
DOFS = 192
PER = 64
OWN = 6912
FACE = 192
OWN_ROWS = OWN // 256
OWN_CHUNKS = OWN // 128
SHARED_ROWS = 6
BLOCK = 32

center = 1.125
half_width = 0.875

AXES = ("seg", "sub")
F32 = jnp.float32
BF16 = jnp.bfloat16


def split(x):
    high = x.astype(BF16).astype(F32)
    return high, x - high


def iota(shape, dimension):
    return lax.broadcasted_iota(jnp.int32, shape, dimension)


def lane_pick(rows, lane):
    return jnp.take_along_axis(rows, lane, axis=1)


def gather_own(state_ref, nodes_ref, out_ref, extra_ref=None, extra_out=None):
    def block(b, carry):
        row = pl.multiple_of(b * 8, 8)
        for half in range(2):
            lanes = slice(half * 128, half * 128 + 128)
            index = nodes_ref[pl.ds(row, 8), lanes]
            lane = index & 127
            chunk = index >> 7
            found = [jnp.zeros((8, 128), F32)] * (3 if extra_ref is None else 4)
            for k in range(OWN_CHUNKS):
                here = chunk == k
                part = slice((k % 2) * 128, (k % 2) * 128 + 128)
                for c in range(len(found)):
                    source, line = (state_ref, 32 * c + k // 2) if c < 3 else (extra_ref, k // 2)
                    values = jnp.broadcast_to(source[line : line + 1, part], (8, 128))
                    found[c] = jnp.where(here, lane_pick(values, lane), found[c])
            for c in range(3):
                out_ref[pl.ds(c * PER + row, 8), lanes] = found[c]
            if extra_ref is not None:
                extra_out[pl.ds(row, 8), lanes] = found[3]
        return carry

    lax.fori_loop(0, PER // 8, block, 0)


def gather_mixed(state_ref, nodes_ref, hot_ref, out_ref):
    table = jnp.concatenate(split(state_ref[...]), axis=0).astype(BF16)
    line = iota((32, 256), 0)
    half_rows = PER // 2

    def block(b, carry):
        row = pl.multiple_of(b * 8, 8)
        for half in range(2):
            lanes = slice(half * 128, half * 128 + 128)
            index = nodes_ref[pl.ds(row, 8), lanes]
            lane = index & 127
            chunk = index >> 7
            found = [jnp.zeros((8, 128), F32)] * 3
            for k in range(OWN_CHUNKS):
                here = chunk == k
                part = slice((k % 2) * 128, (k % 2) * 128 + 128)
                for c in range(3):
                    source = 32 * c + k // 2
                    values = jnp.broadcast_to(state_ref[source : source + 1, part], (8, 128))
                    found[c] = jnp.where(here, lane_pick(values, lane), found[c])
            for c in range(3):
                out_ref[pl.ds(c * PER + row, 8), lanes] = found[c]
        other = pl.multiple_of(b * 8 + half_rows, 8)
        lines = nodes_ref[pl.ds(other, 8), :] >> 8
        for k in range(8):
            hot = hot_ref[pl.ds(pl.multiple_of((other + k) * 256, 256), 256), :]
            got = lax.dot_general(
                table, hot, (((1,), (1,)), ((), ())), preferred_element_type=F32
            )
            here = lines[k : k + 1, :] == line
            for c in range(3):
                both = got[32 * c : 32 * c + 32] + got[96 + 32 * c : 128 + 32 * c]
                out_ref[pl.ds(c * PER + other + k, 1), :] = jnp.sum(
                    jnp.where(here, both, 0.0), axis=0, keepdims=True
                )
        return carry

    lax.fori_loop(0, half_rows // 8, block, 0)


def gather_shared(shared_ref, index_ref, rows_ref, out_ref, first_row):
    tables = [
        [
            jnp.broadcast_to(shared_ref[8 * c + r : 8 * c + r + 1, :], (8, 128))
            for r in range(SHARED_ROWS)
        ]
        for c in range(3)
    ]
    for b in range(PER // 8):
        for half in range(2):
            lanes = slice(half * 128, half * 128 + 128)
            index = index_ref[8 * b : 8 * b + 8, lanes]
            lane = index & 127
            chunk = index >> 7
            masks = [chunk == r for r in range(first_row, SHARED_ROWS)]
            for c in range(3):
                rows = slice(c * PER + 8 * b, c * PER + 8 * b + 8)
                found = rows_ref[rows, lanes]
                for r in range(first_row, SHARED_ROWS):
                    found = jnp.where(masks[r - first_row], lane_pick(tables[c][r], lane), found)
                out_ref[rows, lanes] = found


def scatter_elements(nodes_ref, hot_ref, values_ref, high_ref, low_ref, sums_ref, channels):
    high, low = split(values_ref[...])
    high_ref[...] = high
    low_ref[...] = low
    sums_ref[...] = jnp.zeros_like(sums_ref)
    lines = iota((32, 256), 0).astype(F32).astype(BF16)
    zero = jnp.zeros((), BF16)

    def block(b, carry):
        row = pl.multiple_of(b * BLOCK, BLOCK)
        line = (nodes_ref[pl.ds(row, BLOCK), :] >> 8).astype(F32)
        left = []
        for k in range(BLOCK):
            here = line[k : k + 1, :].astype(BF16) == lines
            left.append(
                jnp.concatenate(
                    [
                        jnp.where(
                            here,
                            jnp.broadcast_to(ref[pl.ds(c * PER + row + k, 1), :], (32, 256)).astype(
                                BF16
                            ),
                            zero,
                        )
                        for ref in (high_ref, low_ref)
                        for c in range(channels)
                    ],
                    axis=0,
                )
            )
        left = jnp.concatenate(left, axis=1)
        right = hot_ref[pl.ds(pl.multiple_of(row * 256, 256), BLOCK * 256), :]
        sums_ref[...] += jnp.dot(left, right, preferred_element_type=F32)
        return carry

    lax.fori_loop(0, PER // BLOCK, block, 0)


def scatter_shared(index_ref, hot_ref, values_ref, high_ref, low_ref, sums_ref, out_ref):
    high, low = split(values_ref[...])
    high_ref[...] = high
    low_ref[...] = low
    sums_ref[...] = jnp.zeros_like(sums_ref)
    lines = iota((8, 256), 0)

    def block(b, carry):
        row = pl.multiple_of(b * BLOCK, BLOCK)
        line = index_ref[pl.ds(row, BLOCK), :] >> 7
        left = []
        for k in range(BLOCK):
            here = line[k : k + 1, :] == lines
            left.append(
                jnp.concatenate(
                    [
                        jnp.where(
                            here,
                            jnp.broadcast_to(ref[pl.ds(c * PER + row + k, 1), :], (8, 256)),
                            0.0,
                        )
                        for ref in (high_ref, low_ref)
                        for c in range(3)
                    ],
                    axis=0,
                ).astype(BF16)
            )
        left = jnp.concatenate(left, axis=1)
        right = hot_ref[pl.ds(pl.multiple_of(row * 256, 256), BLOCK * 256), :]
        sums_ref[...] += jnp.dot(left, right, preferred_element_type=F32)
        return carry

    lax.fori_loop(0, PER // BLOCK, block, 0)
    out_ref[...] = sums_ref[0:24, :] + sums_ref[24:48, :]


def add_parts(sums_ref, first, channels):
    top = 32 * first
    low = top + 32 * channels
    return sums_ref[top : top + 96, :] + sums_ref[low : low + 96, :]


def expand_own_faces(places, channels, parts):
    lines = iota((32, 128), 0)
    lanes = iota((256, 128), 0)
    rows = []
    for values in channels:
        rest = values
        for _ in range(parts):
            high, rest = split(rest)
            rows.append(high)
    left, right = [], []
    for k in range(3):
        here = (places[k : k + 1, :] >> 8) == lines
        left.append(
            jnp.concatenate([jnp.where(here, r[k : k + 1, :], 0.0) for r in rows], axis=0).astype(BF16)
        )
        right.append(jnp.where((places[k : k + 1, :] & 255) == lanes, 1.0, 0.0).astype(BF16))
    sums = lax.dot_general(
        jnp.concatenate(left, axis=1),
        jnp.concatenate(right, axis=1),
        (((1,), (1,)), ((), ())),
        preferred_element_type=F32,
    )
    out = []
    for i in range(len(channels)):
        total = sums[32 * parts * i : 32 * parts * i + 32]
        for q in range(1, parts):
            start = 32 * (parts * i + q)
            total = total + sums[start : start + 32]
        out.append(total)
    return jnp.concatenate(out, axis=0)


def take_shared(state_ref, places, out_ref, base, ghosts):
    found = [[None] * 3 for _ in range(3)]
    line = iota((8, 128), 0)
    for r in range(3):
        place = jnp.broadcast_to(places[r : r + 1, :], (8, 128))
        lane = place & 127
        chunk = place >> 7
        masks = [
            [chunk == 2 * (8 * t + line) + half for half in range(2)] for t in range(4)
        ]
        for c in range(3):
            got = jnp.zeros((8, 128), F32)
            for t in range(4):
                for half in range(2):
                    values = state_ref[
                        32 * c + 8 * t : 32 * c + 8 * t + 8, half * 128 : half * 128 + 128
                    ]
                    got = jnp.where(masks[t][half], lane_pick(values, lane), got)
            found[c][r] = jnp.sum(got, axis=0, keepdims=True)
    for c in range(3):
        top = 32 * c + OWN_ROWS
        if ghosts:
            others = [
                state_ref[top : top + 1, 0:128],
                state_ref[top : top + 1, 128:256],
                state_ref[top + 1 : top + 2, 0:128],
                jnp.zeros((2, 128), F32),
            ]
        else:
            others = [jnp.zeros((5, 128), F32)]
        out_ref[base + 8 * c : base + 8 * c + 8, 0:128] = jnp.concatenate(found[c] + others, axis=0)


def from_neighbours(near_ref, far_ref, base):
    first_core = lax.axis_index("sub") == 0
    left = iota((1, 128), 1) < 64
    out = []
    for c in range(3):
        rows = slice(base + 8 * c, base + 8 * c + 8)
        near = near_ref[rows, 0:128]
        far = far_ref[rows, 0:128]
        before = jnp.where(first_core, far, near)
        after = jnp.where(first_core, near, far)
        before_turned = pltpu.roll(before, 64, 1)
        after_turned = pltpu.roll(after, 64, 1)
        out += [
            before[5:6],
            jnp.where(left, before_turned[4:5], after_turned[4:5]),
            after[3:4],
            before[2:3],
            jnp.where(left, before_turned[1:2], after_turned[1:2]),
            after[0:1],
            jnp.zeros((2, 128), F32),
        ]
    return jnp.concatenate(out, axis=0)


def pack_kernel(
    loads_hbm, coefs_hbm, move_hbm, face_hbm, field_hbm, nodes_hbm, stiff_hbm, far_ref, near_out,
    other_out, places_ref, state_ref, loads_ref, coefs_ref, move_ref, nodes_ref, stiff_ref,
    face_ref, field_ref, sems,
):
    pairs = (
        (move_hbm, move_ref),
        (coefs_hbm, coefs_ref),
        (loads_hbm, loads_ref),
        (face_hbm, face_ref),
        (field_hbm, field_ref),
        (nodes_hbm, nodes_ref),
        (stiff_hbm, stiff_ref),
    )
    copies = [
        pltpu.make_async_copy(source, target, sems.at[i]) for i, (source, target) in enumerate(pairs)
    ]
    for copy in copies:
        copy.start()
    for copy in copies[:3]:
        copy.wait()
    me = lax.axis_index(AXES)
    first_core = lax.axis_index("sub") == 0
    near = jnp.where(first_core, me + 1, me - 1)
    other = jnp.where(first_core, me - 1, me + 1)
    target = move_ref[0:1, :]
    place = move_ref[2:3, :]
    code = jnp.where(
        target == me,
        -1,
        jnp.where(
            target == near,
            DEVICES + place,
            jnp.where(target == other, DEVICES + NEAR_CAP + place, target),
        ),
    )
    rows = DEVICES + 2 * NEAR_CAP
    chosen = jnp.where(code == iota((rows, ELEM), 0), 1.0, 0.0)
    slot = (move_ref[1:2, :] + 1).astype(F32)
    records = jnp.concatenate(
        [loads_ref[...], coefs_ref[...], slot, jnp.zeros((61, ELEM), F32)], axis=0
    )
    packed = lax.dot_general(
        chosen,
        records,
        (((1,), (1,)), ((), ())),
        precision=lax.Precision.HIGHEST,
        preferred_element_type=F32,
    )
    far_ref[:, 0, :] = packed[:DEVICES]
    near_out[0:NEAR_CAP, :] = packed[DEVICES : DEVICES + NEAR_CAP]
    other_out[0:NEAR_CAP, :] = packed[DEVICES + NEAR_CAP :]
    near_out[NEAR_CAP:, :] = jnp.zeros((24, 256), F32)
    for copy in copies[3:]:
        copy.wait()
    places_ref[...] = jnp.zeros((8, 128), jnp.int32)
    places_ref[0:1, :] = face_ref[0:1, 0:128]
    places_ref[1:2, 0:64] = face_ref[0:1, 128:192]
    places_ref[1:2, 64:128] = face_ref[1:2, 128:192]
    places_ref[2:3, :] = face_ref[1:2, 0:128]
    state_ref[...] = jnp.zeros_like(state_ref)
    for c in range(3):
        for h in range(OWN_ROWS):
            state_ref[32 * c + h : 32 * c + h + 1, :] = field_ref[c : c + 1, 256 * h : 256 * h + 256]
    take_shared(state_ref, places_ref[...], near_out, NEAR_CAP, False)
    other_out[NEAR_CAP:, :] = near_out[NEAR_CAP:, :]


def index_kernel(
    state_ref,
    places_ref,
    nodes_ref,
    stiff_ref,
    index_ref,
    shared_index_ref,
    unshared_ref,
    high_ref,
    low_ref,
    gathered_ref,
    positions,
    found,
):
    nodes = nodes_ref[...]
    ghost = nodes - OWN
    ahead = ghost - FACE
    shared = jnp.where(ahead < 0, ghost, jnp.where(ahead < 128, ahead + 256, ahead + 64))
    index_ref[...] = jnp.where(ghost < 0, nodes, OWN + shared)
    places = places_ref[...]
    numbers = (128 * iota((3, 128), 0) + iota((3, 128), 1) + 1).astype(F32)
    positions[...] = expand_own_faces(places, [numbers], 2)
    line = iota((32, 256), 0)
    unshared_ref[...] = jnp.where((positions[...] == 0.0) & (line < OWN_ROWS), 1.0, 0.0)
    gather_own(state_ref, index_ref, gathered_ref, positions, found)
    shared_index_ref[...] = jnp.where(
        ghost < 0, found[...].astype(jnp.int32) - 1, shared + 3 * 128
    )
    for i in range(2):
        high, low = split(stiff_ref[i])
        high_ref[DOFS * i : DOFS * i + DOFS, :] = high.astype(BF16)
        low_ref[DOFS * i : DOFS * i + DOFS, :] = low.astype(BF16)


def build_hot(index_ref, hot_ref, width):
    low = (index_ref[...] & (width - 1)).astype(F32)
    lanes = iota((16, width), 1).astype(F32).astype(BF16)
    one = jnp.ones((), BF16)
    zero = jnp.zeros((), BF16)
    for half in range(2):
        turned = low[:, half * 128 : half * 128 + 128].T.astype(BF16)
        for b in range(8):
            columns = turned[16 * b : 16 * b + 16]
            for n in range(PER):
                top = 256 * n + half * 128 + 16 * b
                column = jnp.broadcast_to(columns[:, n : n + 1], (16, width))
                hot_ref[top : top + 16, :] = jnp.where(column == lanes, one, zero)


def multiply_blocks(high_ref, low_ref, rows_ref):
    high, low = split(rows_ref[...])
    high = high.astype(BF16)
    low = low.astype(BF16)
    return (
        jnp.dot(low_ref[...], high, preferred_element_type=F32)
        + jnp.dot(high_ref[...], low, preferred_element_type=F32)
        + jnp.dot(high_ref[...], high, preferred_element_type=F32)
    )


def place_kernel(
    loads_ref,
    coefs_ref,
    move_ref,
    far_ref,
    near_in,
    other_in,
    field_message,
    stiff_ref,
    gathered_in,
    nodes_ref,
    shared_index_ref,
    places_ref,
    high_ref,
    low_ref,
    hot_ref,
    moved_loads,
    moved_coefs,
    coefs_out,
    partial_ref,
    diagonal_ref,
    shared_field,
    message,
    gathered,
    values,
    value_high,
    value_low,
    sums,
):
    shared_field[...] = field_message[NEAR_CAP:, 0:128] + from_neighbours(near_in, other_in, NEAR_CAP)
    gather_shared(shared_field, shared_index_ref, gathered_in, gathered, 3)
    products = multiply_blocks(high_ref, low_ref, gathered)
    me = lax.axis_index(AXES)
    received = jnp.concatenate(
        [far_ref[:, 0, :], near_in[0:NEAR_CAP, :], other_in[0:NEAR_CAP, :]], axis=0
    )
    rows = DEVICES + 2 * NEAR_CAP
    slot = received[:, DOFS + 2 : DOFS + 3].astype(jnp.int32)
    chosen = jnp.where(slot == iota((rows, ELEM), 1) + 1, 1.0, 0.0)
    arrived = lax.dot_general(
        received,
        chosen,
        (((0,), (0,)), ((), ())),
        precision=lax.Precision.HIGHEST,
        preferred_element_type=F32,
    )
    stays = move_ref[0:1, :] == me
    loads = jnp.where(stays, loads_ref[...], 0.0) + arrived[:DOFS]
    coefs = jnp.where(stays, coefs_ref[...], 0.0) + arrived[DOFS : DOFS + 2]
    moved_loads[...] = loads
    moved_coefs[...] = coefs
    coefs_out[...] = coefs
    values[0:DOFS, :] = loads - (products[:DOFS] * coefs[0:1, :] + products[DOFS:] * coefs[1:2, :])
    eye = iota((DOFS, DOFS), 0) == iota((DOFS, DOFS), 1)
    first_diag = jnp.sum(jnp.where(eye, stiff_ref[0], 0.0), axis=1, keepdims=True)
    second_diag = jnp.sum(jnp.where(eye, stiff_ref[1], 0.0), axis=1, keepdims=True)
    values[DOFS:, :] = first_diag * coefs[0:1, :] + second_diag * coefs[1:2, :]
    build_hot(nodes_ref, hot_ref, 256)
    scatter_elements(nodes_ref, hot_ref, values, value_high, value_low, sums, 6)
    partial_ref[...] = add_parts(sums, 0, 6)
    diagonal_ref[...] = add_parts(sums, 3, 6)
    take_shared(partial_ref, places_ref[...], message, 0, True)
    take_shared(diagonal_ref, places_ref[...], message, 24, True)


def apply_operator(
    shared_update, gathered_in, shared_index_ref, coefs_ref, hot_ref, high_ref, low_ref, values_ref,
    message, gathered, value_high, value_low, sums,
):
    gather_shared(shared_update, shared_index_ref, gathered_in, gathered, 0)
    products = multiply_blocks(high_ref, low_ref, gathered)
    values_ref[...] = products[:DOFS] * coefs_ref[0:1, :] + products[DOFS:] * coefs_ref[1:2, :]
    scatter_shared(shared_index_ref, hot_ref, values_ref, value_high, value_low, sums, message)


def inverse_of(diagonal):
    return jnp.where(diagonal == 0.0, 0.0, 1.0 / diagonal)


def begin_unshared(
    step, partial_ref, diagonal_ref, unshared_ref, field_ref, nodes_ref, hot_ref, shared_index_ref,
    inverse_out, update_out, field_out, gathered_out, hot_shared_ref,
):
    build_hot(shared_index_ref, hot_shared_ref, 128)
    unshared = jnp.concatenate([unshared_ref[...]] * 3, axis=0)
    inverse = jnp.where(unshared > 0.0, inverse_of(diagonal_ref[...]), 0.0)
    update = step[1] * (partial_ref[...] * inverse)
    inverse_out[...] = inverse
    update_out[...] = update
    field_out[...] = field_ref[...] + update
    gather_mixed(update_out, nodes_ref, hot_ref, gathered_out)


def begin_shared(
    step, message_in, near_in, other_in, shared_field, gathered_in, shared_index_ref, coefs_ref,
    hot_ref, high_ref, low_ref, residual_out, inverse_out, update_out, field_out, values_ref, message, gathered, value_high, value_low, sums,
):
    residual = message_in[0:24, :] + from_neighbours(near_in, other_in, 0)
    inverse = inverse_of(message_in[24:48, :] + from_neighbours(near_in, other_in, 24))
    update = step[1] * (residual * inverse)
    residual_out[...] = residual
    inverse_out[...] = inverse
    update_out[...] = update
    field_out[...] = shared_field[...] + update
    apply_operator(
        update_out, gathered_in, shared_index_ref, coefs_ref, hot_ref, high_ref, low_ref, values_ref,
        message, gathered, value_high, value_low, sums,
    )


def next_update(step, residual, inverse, update):
    changed = step[1] * (residual * inverse)
    return step[0] * update + changed if step[0] else changed


def step_unshared(
    step, values_ref, residual_ref, inverse_ref, update_ref, field_ref, nodes_ref, hot_ref,
    residual_out, update_out, field_out, gathered_out, value_high, value_low, sums,
):
    scatter_elements(nodes_ref, hot_ref, values_ref, value_high, value_low, sums, 3)
    residual = residual_ref[...] - add_parts(sums, 0, 3)
    update = next_update(step, residual, inverse_ref[...], update_ref[...])
    residual_out[...] = residual
    update_out[...] = update
    field_out[...] = field_ref[...] + update
    gather_mixed(update_out, nodes_ref, hot_ref, gathered_out)


def step_shared(
    step, message_in, near_in, other_in, residual_ref, inverse_ref, update_ref, field_ref,
    gathered_in, shared_index_ref, coefs_ref, hot_ref, high_ref, low_ref, residual_out, update_out,
    field_out, values_ref, message, gathered, value_high, value_low, sums,
):
    residual = residual_ref[...] - (message_in[...] + from_neighbours(near_in, other_in, 0))
    update = next_update(step, residual, inverse_ref[...], update_ref[...])
    residual_out[...] = residual
    update_out[...] = update
    field_out[...] = field_ref[...] + update
    apply_operator(
        update_out, gathered_in, shared_index_ref, coefs_ref, hot_ref, high_ref, low_ref, values_ref,
        message, gathered, value_high, value_low, sums,
    )


def last_unshared(
    step, values_ref, residual_ref, inverse_ref, update_ref, field_ref, nodes_ref, hot_ref, field_out,
    value_high, value_low, sums,
):
    scatter_elements(nodes_ref, hot_ref, values_ref, value_high, value_low, sums, 3)
    residual = residual_ref[...] - add_parts(sums, 0, 3)
    field_out[...] = field_ref[...] + next_update(step, residual, inverse_ref[...], update_ref[...])


def last_shared(
    step, message_in, near_in, other_in, residual_ref, inverse_ref, update_ref, shared_field,
    field_ref, unshared_ref, places_ref, out_ref,
):
    residual = residual_ref[...] - (message_in[...] + from_neighbours(near_in, other_in, 0))
    shared = shared_field[...] + next_update(step, residual, inverse_ref[...], update_ref[...])
    faces = expand_own_faces(places_ref[...], [shared[8 * c : 8 * c + 3] for c in range(3)], 3)
    unshared = jnp.concatenate([unshared_ref[...]] * 3, axis=0)
    field = jnp.where(unshared > 0.0, field_ref[...], faces)
    for c in range(3):
        for h in range(OWN_ROWS):
            out_ref[c : c + 1, 256 * h : 256 * h + 256] = field[32 * c + h : 32 * c + h + 1, :]


def shaped(*shape, dtype=F32):
    return jax.ShapeDtypeStruct(shape, dtype)


def steps():
    scaled_center = center / half_width
    found = []
    for _ in range(SWEEPS):
        found.append((0.0, 1.0 / center))
        ratio = 1.0 / scaled_center
        for _ in range(DEGREE - 1):
            ratio_next = 1.0 / (2.0 * scaled_center - ratio)
            found.append((ratio_next * ratio, 2.0 * ratio_next / half_width))
            ratio = ratio_next
    return found


NEAR_PAIRS = [(i, i ^ 1) for i in range(DEVICES)]
OTHER_PAIRS = [
    pair for i in range(1, DEVICES - 1, 2) for pair in ((i, i + 1), (i + 1, i))
]


def exchange(near_message, other_message):
    other = lax.ppermute(other_message, AXES, OTHER_PAIRS)
    near = lax.ppermute(near_message, AXES, NEAR_PAIRS)
    return near, other


def call(kernel, name, outs, scratch=(), **options):
    return pl.pallas_call(
        kernel,
        out_shape=outs,
        scratch_shapes=list(scratch),
        compiler_params=pltpu.CompilerParams(vmem_limit_bytes=20 << 20),
        name=name,
        **options,
    )


STATE = shaped(96, 256)
SHARED = shaped(24, 128)
ELEMENT_ROWS = shaped(DOFS, ELEM)


def rows(count):
    return pltpu.VMEM((count, ELEM), F32)


def local(
    start_field, element_loads, element_coefs, element_nodes, move_list, face_nodes, stiffness
):
    integers = functools.partial(shaped, dtype=jnp.int32)
    far, near, other, places, field, loads, coefs, moves, nodes, stiff = call(
        pack_kernel,
        "pack",
        (
            shaped(DEVICES, 1, 256),
            shaped(40, 256),
            shaped(40, 256),
            integers(8, 128),
            STATE,
            ELEMENT_ROWS,
            shaped(2, ELEM),
            integers(3, ELEM),
            integers(PER, ELEM),
            shaped(2, DOFS, DOFS),
        ),
        [
            pltpu.VMEM((2, FACE), jnp.int32),
            pltpu.VMEM((3, OWN), F32),
            pltpu.SemaphoreType.DMA((7,)),
        ],
        in_specs=[pl.BlockSpec(memory_space=pltpu.HBM)] * 7,
    )(*[pltpu.with_memory_space_constraint(x, pltpu.HBM) for x in (element_loads, element_coefs, move_list, face_nodes, start_field, element_nodes, stiffness)])
    field_message = near
    near, other = exchange(near, other)
    far = lax.all_to_all(far, AXES, split_axis=0, concat_axis=0, tiled=True)
    nodes, shared_index, unshared, high, low, gathered = call(
        index_kernel,
        "index",
        (
            integers(PER, ELEM),
            integers(PER, ELEM),
            shaped(32, 256),
            shaped(2 * DOFS, DOFS, dtype=BF16),
            shaped(2 * DOFS, DOFS, dtype=BF16),
            ELEMENT_ROWS,
        ),
        [rows(32), rows(PER)],
    )(field, places, nodes, stiff)
    hot, moved_loads, moved_coefs, coefs, partial, diagonal, shared_field, message = call(
        place_kernel,
        "place",
        (
            shaped(PER * ELEM, 256, dtype=BF16),
            ELEMENT_ROWS,
            shaped(2, ELEM),
            shaped(2, ELEM),
            STATE,
            STATE,
            SHARED,
            shaped(48, 128),
        ),
        [rows(DOFS), rows(2 * DOFS), rows(2 * DOFS), rows(2 * DOFS), rows(384)],
    )(
        loads, coefs, moves, far, near, other, field_message, stiff,
        gathered, nodes, shared_index, places, high, low,
    )
    near, other = exchange(message, message)
    plan = steps()
    scratch = [rows(DOFS)] * 3 + [pltpu.VMEM((48, 128), F32)]
    window_scratch = [rows(DOFS)] * 2 + [rows(192)]
    residual = partial
    inverse, update, field, gathered, hot_shared = call(
        functools.partial(begin_unshared, plan[0]),
        "begin_unshared",
        (STATE, STATE, STATE, ELEMENT_ROWS, shaped(PER * ELEM, 128, dtype=BF16)),
    )(partial, diagonal, unshared, field, nodes, hot, shared_index)
    fixed = (shared_index, coefs, hot_shared, high, low)
    shared_residual, shared_inverse, shared_update, shared_field, values, message = call(
        functools.partial(begin_shared, plan[0]),
        "begin_shared",
        (SHARED, SHARED, SHARED, SHARED, ELEMENT_ROWS, SHARED),
        scratch,
    )(message, near, other, shared_field, gathered, *fixed)
    for step in plan[1:-1]:
        near, other = exchange(message, message)
        residual, update, field, gathered = call(
            functools.partial(step_unshared, step),
            "unshared",
            (STATE, STATE, STATE, ELEMENT_ROWS),
            window_scratch,
        )(values, residual, inverse, update, field, nodes, hot)
        shared_residual, shared_update, shared_field, values, message = call(
            functools.partial(step_shared, step),
            "shared",
            (SHARED, SHARED, SHARED, ELEMENT_ROWS, SHARED),
            scratch,
        )(
            message, near, other, shared_residual, shared_inverse, shared_update, shared_field,
            gathered, *fixed,
        )
    near, other = exchange(message, message)
    field = call(
        functools.partial(last_unshared, plan[-1]), "last_unshared", STATE, window_scratch
    )(values, residual, inverse, update, field, nodes, hot)
    field = call(functools.partial(last_shared, plan[-1]), "last_shared", shaped(3, OWN))(
        message, near, other, shared_residual, shared_inverse, shared_update, shared_field, field,
        unshared, places,
    )
    return field, moved_loads, moved_coefs


def solution(mesh):
    split_columns = P(None, AXES)
    return jax.shard_map(
        local,
        mesh=mesh,
        in_specs=(split_columns,) * 6 + (P(),),
        out_specs=(split_columns,) * 3,
        check_vma=False,
    )
```

```python
import functools

import jax
import jax.numpy as jnp
from jax import lax
from jax.experimental import pallas as pl
from jax.experimental.pallas import tpu as pltpu
from jax.sharding import PartitionSpec as P


NEAR_CAP = 16
DEGREE = 4
SWEEPS = 2
DEVICES = 128
ELEM = 256
DOFS = 192
PER = 64
OWN = 6912
FACE = 192
OWN_ROWS = OWN // 256
OWN_CHUNKS = OWN // 128
SHARED_ROWS = 6
BLOCK = 32

center = 1.125
half_width = 0.875

AXES = ("seg", "sub")
F32 = jnp.float32
BF16 = jnp.bfloat16


def split(x):
    high = x.astype(BF16).astype(F32)
    return high, x - high


def iota(shape, dimension):
    return lax.broadcasted_iota(jnp.int32, shape, dimension)


def lane_pick(rows, lane):
    return jnp.take_along_axis(rows, lane, axis=1)


def gather_own(state_ref, nodes_ref, out_ref, extra_ref=None, extra_out=None):
    def block(b, carry):
        row = pl.multiple_of(b * 8, 8)
        for half in range(2):
            lanes = slice(half * 128, half * 128 + 128)
            index = nodes_ref[pl.ds(row, 8), lanes]
            lane = index & 127
            chunk = index >> 7
            found = [jnp.zeros((8, 128), F32)] * (3 if extra_ref is None else 4)
            for k in range(OWN_CHUNKS):
                here = chunk == k
                part = slice((k % 2) * 128, (k % 2) * 128 + 128)
                for c in range(len(found)):
                    source, line = (state_ref, 32 * c + k // 2) if c < 3 else (extra_ref, k // 2)
                    values = jnp.broadcast_to(source[line : line + 1, part], (8, 128))
                    found[c] = jnp.where(here, lane_pick(values, lane), found[c])
            for c in range(3):
                out_ref[pl.ds(c * PER + row, 8), lanes] = found[c]
            if extra_ref is not None:
                extra_out[pl.ds(row, 8), lanes] = found[3]
        return carry

    lax.fori_loop(0, PER // 8, block, 0)


def gather_mixed(state_ref, nodes_ref, hot_ref, out_ref):
    table = jnp.concatenate(split(state_ref[...]), axis=0).astype(BF16)
    line = iota((32, 256), 0)
    half_rows = PER // 2

    def block(b, carry):
        row = pl.multiple_of(b * 8, 8)
        for half in range(2):
            lanes = slice(half * 128, half * 128 + 128)
            index = nodes_ref[pl.ds(row, 8), lanes]
            lane = index & 127
            chunk = index >> 7
            found = [jnp.zeros((8, 128), F32)] * 3
            for k in range(OWN_CHUNKS):
                here = chunk == k
                part = slice((k % 2) * 128, (k % 2) * 128 + 128)
                for c in range(3):
                    source = 32 * c + k // 2
                    values = jnp.broadcast_to(state_ref[source : source + 1, part], (8, 128))
                    found[c] = jnp.where(here, lane_pick(values, lane), found[c])
            for c in range(3):
                out_ref[pl.ds(c * PER + row, 8), lanes] = found[c]
        other = pl.multiple_of(b * 8 + half_rows, 8)
        lines = nodes_ref[pl.ds(other, 8), :] >> 8
        for k in range(8):
            hot = hot_ref[pl.ds(pl.multiple_of((other + k) * 256, 256), 256), :]
            got = lax.dot_general(
                table, hot, (((1,), (1,)), ((), ())), preferred_element_type=F32
            )
            here = lines[k : k + 1, :] == line
            for c in range(3):
                both = got[32 * c : 32 * c + 32] + got[96 + 32 * c : 128 + 32 * c]
                out_ref[pl.ds(c * PER + other + k, 1), :] = jnp.sum(
                    jnp.where(here, both, 0.0), axis=0, keepdims=True
                )
        return carry

    lax.fori_loop(0, half_rows // 8, block, 0)


def gather_shared(shared_ref, index_ref, rows_ref, out_ref, first_row):
    tables = [
        [
            jnp.broadcast_to(shared_ref[8 * c + r : 8 * c + r + 1, :], (8, 128))
            for r in range(SHARED_ROWS)
        ]
        for c in range(3)
    ]
    for b in range(PER // 8):
        for half in range(2):
            lanes = slice(half * 128, half * 128 + 128)
            index = index_ref[8 * b : 8 * b + 8, lanes]
            lane = index & 127
            chunk = index >> 7
            masks = [chunk == r for r in range(first_row, SHARED_ROWS)]
            for c in range(3):
                rows = slice(c * PER + 8 * b, c * PER + 8 * b + 8)
                found = rows_ref[rows, lanes]
                for r in range(first_row, SHARED_ROWS):
                    found = jnp.where(masks[r - first_row], lane_pick(tables[c][r], lane), found)
                out_ref[rows, lanes] = found


def scatter_elements(nodes_ref, hot_ref, values_ref, high_ref, low_ref, sums_ref, channels):
    high, low = split(values_ref[...])
    high_ref[...] = high
    low_ref[...] = low
    sums_ref[...] = jnp.zeros_like(sums_ref)
    lines = iota((32, 256), 0).astype(F32).astype(BF16)
    zero = jnp.zeros((), BF16)

    def block(b, carry):
        row = pl.multiple_of(b * BLOCK, BLOCK)
        line = (nodes_ref[pl.ds(row, BLOCK), :] >> 8).astype(F32)
        left = []
        for k in range(BLOCK):
            here = line[k : k + 1, :].astype(BF16) == lines
            left.append(
                jnp.concatenate(
                    [
                        jnp.where(
                            here,
                            jnp.broadcast_to(ref[pl.ds(c * PER + row + k, 1), :], (32, 256)).astype(
                                BF16
                            ),
                            zero,
                        )
                        for ref in (high_ref, low_ref)
                        for c in range(channels)
                    ],
                    axis=0,
                )
            )
        left = jnp.concatenate(left, axis=1)
        right = hot_ref[pl.ds(pl.multiple_of(row * 256, 256), BLOCK * 256), :]
        sums_ref[...] += jnp.dot(left, right, preferred_element_type=F32)
        return carry

    lax.fori_loop(0, PER // BLOCK, block, 0)


def scatter_shared(index_ref, hot_ref, values_ref, high_ref, low_ref, out_ref):
    high, low = split(values_ref[...])
    high_ref[...] = high
    low_ref[...] = low
    lines = iota((8, 256), 0)
    line = index_ref[...] >> 7
    left = []
    for n in range(PER):
        here = line[n : n + 1, :] == lines
        left.append(
            jnp.concatenate(
                [
                    jnp.where(
                        here,
                        jnp.broadcast_to(ref[c * PER + n : c * PER + n + 1, :], (8, 256)),
                        0.0,
                    )
                    for ref in (high_ref, low_ref)
                    for c in range(3)
                ],
                axis=0,
            ).astype(BF16)
        )
    sums = jnp.dot(
        jnp.concatenate(left, axis=1), hot_ref[...], preferred_element_type=F32
    )
    out_ref[...] = sums[0:24, :] + sums[24:48, :]


def add_parts(sums_ref, first, channels):
    top = 32 * first
    low = top + 32 * channels
    return sums_ref[top : top + 96, :] + sums_ref[low : low + 96, :]


def expand_own_faces(places, channels, parts):
    lines = iota((32, 128), 0)
    lanes = iota((256, 128), 0)
    rows = []
    for values in channels:
        rest = values
        for _ in range(parts):
            high, rest = split(rest)
            rows.append(high)
    left, right = [], []
    for k in range(3):
        here = (places[k : k + 1, :] >> 8) == lines
        left.append(
            jnp.concatenate([jnp.where(here, r[k : k + 1, :], 0.0) for r in rows], axis=0).astype(BF16)
        )
        right.append(jnp.where((places[k : k + 1, :] & 255) == lanes, 1.0, 0.0).astype(BF16))
    sums = lax.dot_general(
        jnp.concatenate(left, axis=1),
        jnp.concatenate(right, axis=1),
        (((1,), (1,)), ((), ())),
        preferred_element_type=F32,
    )
    out = []
    for i in range(len(channels)):
        total = sums[32 * parts * i : 32 * parts * i + 32]
        for q in range(1, parts):
            start = 32 * (parts * i + q)
            total = total + sums[start : start + 32]
        out.append(total)
    return jnp.concatenate(out, axis=0)


def take_shared(state_ref, places, out_ref, base, ghosts):
    found = [[None] * 3 for _ in range(3)]
    line = iota((8, 128), 0)
    for r in range(3):
        place = jnp.broadcast_to(places[r : r + 1, :], (8, 128))
        lane = place & 127
        chunk = place >> 7
        masks = [
            [chunk == 2 * (8 * t + line) + half for half in range(2)] for t in range(4)
        ]
        for c in range(3):
            got = jnp.zeros((8, 128), F32)
            for t in range(4):
                for half in range(2):
                    values = state_ref[
                        32 * c + 8 * t : 32 * c + 8 * t + 8, half * 128 : half * 128 + 128
                    ]
                    got = jnp.where(masks[t][half], lane_pick(values, lane), got)
            found[c][r] = jnp.sum(got, axis=0, keepdims=True)
    for c in range(3):
        top = 32 * c + OWN_ROWS
        if ghosts:
            others = [
                state_ref[top : top + 1, 0:128],
                state_ref[top : top + 1, 128:256],
                state_ref[top + 1 : top + 2, 0:128],
                jnp.zeros((2, 128), F32),
            ]
        else:
            others = [jnp.zeros((5, 128), F32)]
        out_ref[base + 8 * c : base + 8 * c + 8, 0:128] = jnp.concatenate(found[c] + others, axis=0)


def from_neighbours(near_ref, far_ref, base):
    first_core = lax.axis_index("sub") == 0
    left = iota((1, 128), 1) < 64
    out = []
    for c in range(3):
        rows = slice(base + 8 * c, base + 8 * c + 8)
        near = near_ref[rows, 0:128]
        far = far_ref[rows, 0:128]
        before = jnp.where(first_core, far, near)
        after = jnp.where(first_core, near, far)
        before_turned = pltpu.roll(before, 64, 1)
        after_turned = pltpu.roll(after, 64, 1)
        out += [
            before[5:6],
            jnp.where(left, before_turned[4:5], after_turned[4:5]),
            after[3:4],
            before[2:3],
            jnp.where(left, before_turned[1:2], after_turned[1:2]),
            after[0:1],
            jnp.zeros((2, 128), F32),
        ]
    return jnp.concatenate(out, axis=0)


def pack_kernel(
    loads_hbm, coefs_hbm, move_hbm, face_hbm, field_hbm, nodes_hbm, stiff_hbm, far_hbm, near_out,
    other_out, places_ref, state_ref, loads_ref, coefs_ref, move_ref, nodes_ref, stiff_ref,
    face_ref, field_ref, far_rows, sems,
):
    pairs = (
        (move_hbm, move_ref),
        (coefs_hbm, coefs_ref),
        (loads_hbm, loads_ref),
        (face_hbm, face_ref),
        (field_hbm, field_ref),
        (nodes_hbm, nodes_ref),
        (stiff_hbm, stiff_ref),
    )
    copies = [
        pltpu.make_async_copy(source, target, sems.at[i]) for i, (source, target) in enumerate(pairs)
    ]
    for copy in copies:
        copy.start()
    for copy in copies[:3]:
        copy.wait()
    me = lax.axis_index(AXES)
    first_core = lax.axis_index("sub") == 0
    near = jnp.where(first_core, me + 1, me - 1)
    other = jnp.where(first_core, me - 1, me + 1)
    target = move_ref[0:1, :]
    place = move_ref[2:3, :]
    code = jnp.where(
        target == me,
        -1,
        jnp.where(
            target == near,
            DEVICES + place,
            jnp.where(target == other, DEVICES + NEAR_CAP + place, target),
        ),
    )
    rows = DEVICES + 2 * NEAR_CAP
    chosen = jnp.where(code == iota((rows, ELEM), 0), 1.0, 0.0)
    slot = (move_ref[1:2, :] + 1).astype(F32)
    records = jnp.concatenate(
        [loads_ref[...], coefs_ref[...], slot, jnp.zeros((61, ELEM), F32)], axis=0
    )
    packed = lax.dot_general(
        chosen,
        records,
        (((1,), (1,)), ((), ())),
        precision=lax.Precision.HIGHEST,
        preferred_element_type=F32,
    )
    far_rows[:, 0, :] = packed[:DEVICES]
    far_copy = pltpu.make_async_copy(far_rows, far_hbm, sems.at[7])
    far_copy.start()
    near_out[0:NEAR_CAP, :] = packed[DEVICES : DEVICES + NEAR_CAP]
    other_out[0:NEAR_CAP, :] = packed[DEVICES + NEAR_CAP :]
    near_out[NEAR_CAP:, :] = jnp.zeros((24, 256), F32)
    for copy in copies[3:5]:
        copy.wait()
    places_ref[...] = jnp.zeros((8, 128), jnp.int32)
    places_ref[0:1, :] = face_ref[0:1, 0:128]
    places_ref[1:2, 0:64] = face_ref[0:1, 128:192]
    places_ref[1:2, 64:128] = face_ref[1:2, 128:192]
    places_ref[2:3, :] = face_ref[1:2, 0:128]
    state_ref[...] = jnp.zeros_like(state_ref)
    for c in range(3):
        for h in range(OWN_ROWS):
            state_ref[32 * c + h : 32 * c + h + 1, :] = field_ref[c : c + 1, 256 * h : 256 * h + 256]
    take_shared(state_ref, places_ref[...], near_out, NEAR_CAP, False)
    other_out[NEAR_CAP:, :] = near_out[NEAR_CAP:, :]
    for copy in copies[5:]:
        copy.wait()
    far_copy.wait()


def index_kernel(
    state_ref,
    places_ref,
    nodes_ref,
    stiff_ref,
    index_ref,
    shared_index_ref,
    unshared_ref,
    blocks_ref,
    gathered_ref,
    positions,
    found,
):
    nodes = nodes_ref[...]
    ghost = nodes - OWN
    ahead = ghost - FACE
    shared = jnp.where(ahead < 0, ghost, jnp.where(ahead < 128, ahead + 256, ahead + 64))
    index_ref[...] = jnp.where(ghost < 0, nodes, OWN + shared)
    places = places_ref[...]
    numbers = (128 * iota((3, 128), 0) + iota((3, 128), 1) + 1).astype(F32)
    positions[...] = expand_own_faces(places, [numbers], 2)
    line = iota((32, 256), 0)
    unshared_ref[...] = jnp.where((positions[...] == 0.0) & (line < OWN_ROWS), 1.0, 0.0)
    gather_own(state_ref, index_ref, gathered_ref, positions, found)
    shared_index_ref[...] = jnp.where(
        ghost < 0, found[...].astype(jnp.int32) - 1, shared + 3 * 128
    )
    for i in range(2):
        high, low = split(stiff_ref[i])
        high = high.astype(BF16)
        blocks_ref[DOFS * i : DOFS * i + DOFS, :] = jnp.concatenate(
            [low.astype(BF16), high, high], axis=1
        )


def build_hot(index_ref, hot_ref, width):
    low = (index_ref[...] & (width - 1)).astype(F32)
    lanes = iota((16, width), 1).astype(F32).astype(BF16)
    one = jnp.ones((), BF16)
    zero = jnp.zeros((), BF16)
    for half in range(2):
        turned = low[:, half * 128 : half * 128 + 128].T.astype(BF16)
        for b in range(8):
            columns = turned[16 * b : 16 * b + 16]
            for n in range(PER):
                top = 256 * n + half * 128 + 16 * b
                column = jnp.broadcast_to(columns[:, n : n + 1], (16, width))
                hot_ref[top : top + 16, :] = jnp.where(column == lanes, one, zero)


def multiply_blocks(blocks_ref, rows_ref):
    high, low = split(rows_ref[...])
    high = high.astype(BF16)
    low = low.astype(BF16)
    return jnp.dot(
        blocks_ref[...], jnp.concatenate([high, low, high], axis=0), preferred_element_type=F32
    )


def place_kernel(
    loads_ref,
    coefs_ref,
    move_ref,
    far_ref,
    near_in,
    other_in,
    field_message,
    stiff_ref,
    gathered_in,
    nodes_ref,
    shared_index_ref,
    places_ref,
    blocks_ref,
    hot_ref,
    moved_loads,
    moved_coefs,
    coefs_out,
    partial_ref,
    diagonal_ref,
    shared_field,
    message,
    gathered,
    values,
    value_high,
    value_low,
    sums,
    kept_loads,
    sems,
):
    shared_field[...] = field_message[NEAR_CAP:, 0:128] + from_neighbours(near_in, other_in, NEAR_CAP)
    gather_shared(shared_field, shared_index_ref, gathered_in, gathered, 3)
    products = multiply_blocks(blocks_ref, gathered)
    me = lax.axis_index(AXES)
    received = jnp.concatenate(
        [far_ref[:, 0, :], near_in[0:NEAR_CAP, :], other_in[0:NEAR_CAP, :]], axis=0
    )
    rows = DEVICES + 2 * NEAR_CAP
    slot = received[:, DOFS + 2 : DOFS + 3].astype(jnp.int32)
    chosen = jnp.where(slot == iota((rows, ELEM), 1) + 1, 1.0, 0.0)
    arrived = lax.dot_general(
        received,
        chosen,
        (((0,), (0,)), ((), ())),
        precision=lax.Precision.HIGHEST,
        preferred_element_type=F32,
    )
    stays = move_ref[0:1, :] == me
    loads = jnp.where(stays, loads_ref[...], 0.0) + arrived[:DOFS]
    coefs = jnp.where(stays, coefs_ref[...], 0.0) + arrived[DOFS : DOFS + 2]
    kept_loads[...] = loads
    coefs_out[...] = coefs
    copies = (
        pltpu.make_async_copy(kept_loads, moved_loads, sems.at[0]),
        pltpu.make_async_copy(coefs_out, moved_coefs, sems.at[1]),
    )
    for copy in copies:
        copy.start()
    values[0:DOFS, :] = loads - (products[:DOFS] * coefs[0:1, :] + products[DOFS:] * coefs[1:2, :])
    eye = iota((DOFS, DOFS), 0) == iota((DOFS, DOFS), 1)
    first_diag = jnp.sum(jnp.where(eye, stiff_ref[0], 0.0), axis=1, keepdims=True)
    second_diag = jnp.sum(jnp.where(eye, stiff_ref[1], 0.0), axis=1, keepdims=True)
    values[DOFS:, :] = first_diag * coefs[0:1, :] + second_diag * coefs[1:2, :]
    build_hot(nodes_ref, hot_ref, 256)
    scatter_elements(nodes_ref, hot_ref, values, value_high, value_low, sums, 6)
    partial_ref[...] = add_parts(sums, 0, 6)
    diagonal_ref[...] = add_parts(sums, 3, 6)
    take_shared(partial_ref, places_ref[...], message, 0, True)
    take_shared(diagonal_ref, places_ref[...], message, 24, True)
    for copy in copies:
        copy.wait()


def apply_operator(
    shared_update, gathered_in, shared_index_ref, coefs_ref, hot_ref, blocks_ref, values_ref,
    message, gathered, value_high, value_low,
):
    gather_shared(shared_update, shared_index_ref, gathered_in, gathered, 0)
    products = multiply_blocks(blocks_ref, gathered)
    values_ref[...] = products[:DOFS] * coefs_ref[0:1, :] + products[DOFS:] * coefs_ref[1:2, :]
    scatter_shared(shared_index_ref, hot_ref, values_ref, value_high, value_low, message)


def inverse_of(diagonal):
    return jnp.where(diagonal == 0.0, 0.0, 1.0 / diagonal)


def begin_unshared(
    step, partial_ref, diagonal_ref, unshared_ref, field_ref, nodes_ref, hot_ref, shared_index_ref,
    inverse_out, update_out, field_out, gathered_out, hot_shared_ref,
):
    build_hot(shared_index_ref, hot_shared_ref, 128)
    unshared = jnp.concatenate([unshared_ref[...]] * 3, axis=0)
    inverse = jnp.where(unshared > 0.0, inverse_of(diagonal_ref[...]), 0.0)
    update = step[1] * (partial_ref[...] * inverse)
    inverse_out[...] = inverse
    update_out[...] = update
    field_out[...] = field_ref[...] + update
    gather_mixed(update_out, nodes_ref, hot_ref, gathered_out)


def begin_shared(
    step, message_in, near_in, other_in, shared_field, gathered_in, shared_index_ref, coefs_ref,
    hot_ref, blocks_ref, residual_out, inverse_out, update_out, field_out, values_ref, message,
    gathered, value_high, value_low,
):
    residual = message_in[0:24, :] + from_neighbours(near_in, other_in, 0)
    inverse = inverse_of(message_in[24:48, :] + from_neighbours(near_in, other_in, 24))
    update = step[1] * (residual * inverse)
    residual_out[...] = residual
    inverse_out[...] = inverse
    update_out[...] = update
    field_out[...] = shared_field[...] + update
    apply_operator(
        update_out, gathered_in, shared_index_ref, coefs_ref, hot_ref, blocks_ref, values_ref,
        message, gathered, value_high, value_low,
    )


def next_update(step, residual, inverse, update):
    changed = step[1] * (residual * inverse)
    return step[0] * update + changed if step[0] else changed


def step_unshared(
    step, values_ref, residual_ref, inverse_ref, update_ref, field_ref, nodes_ref, hot_ref,
    residual_out, update_out, field_out, gathered_out, value_high, value_low, sums,
):
    scatter_elements(nodes_ref, hot_ref, values_ref, value_high, value_low, sums, 3)
    residual = residual_ref[...] - add_parts(sums, 0, 3)
    update = next_update(step, residual, inverse_ref[...], update_ref[...])
    residual_out[...] = residual
    update_out[...] = update
    field_out[...] = field_ref[...] + update
    gather_mixed(update_out, nodes_ref, hot_ref, gathered_out)


def step_shared(
    step, message_in, near_in, other_in, residual_ref, inverse_ref, update_ref, field_ref,
    gathered_in, shared_index_ref, coefs_ref, hot_ref, blocks_ref, residual_out, update_out,
    field_out, values_ref, message, gathered, value_high, value_low,
):
    residual = residual_ref[...] - (message_in[...] + from_neighbours(near_in, other_in, 0))
    update = next_update(step, residual, inverse_ref[...], update_ref[...])
    residual_out[...] = residual
    update_out[...] = update
    field_out[...] = field_ref[...] + update
    apply_operator(
        update_out, gathered_in, shared_index_ref, coefs_ref, hot_ref, blocks_ref, values_ref,
        message, gathered, value_high, value_low,
    )


def last_unshared(
    step, values_ref, residual_ref, inverse_ref, update_ref, field_ref, nodes_ref, hot_ref, field_out,
    value_high, value_low, sums,
):
    scatter_elements(nodes_ref, hot_ref, values_ref, value_high, value_low, sums, 3)
    residual = residual_ref[...] - add_parts(sums, 0, 3)
    field_out[...] = field_ref[...] + next_update(step, residual, inverse_ref[...], update_ref[...])


def last_shared(
    step, message_in, near_in, other_in, residual_ref, inverse_ref, update_ref, shared_field,
    field_ref, unshared_ref, places_ref, out_ref,
):
    residual = residual_ref[...] - (message_in[...] + from_neighbours(near_in, other_in, 0))
    shared = shared_field[...] + next_update(step, residual, inverse_ref[...], update_ref[...])
    faces = expand_own_faces(places_ref[...], [shared[8 * c : 8 * c + 3] for c in range(3)], 3)
    unshared = jnp.concatenate([unshared_ref[...]] * 3, axis=0)
    field = jnp.where(unshared > 0.0, field_ref[...], faces)
    for c in range(3):
        for h in range(OWN_ROWS):
            out_ref[c : c + 1, 256 * h : 256 * h + 256] = field[32 * c + h : 32 * c + h + 1, :]


def shaped(*shape, dtype=F32):
    return jax.ShapeDtypeStruct(shape, dtype)


def steps():
    scaled_center = center / half_width
    found = []
    for _ in range(SWEEPS):
        found.append((0.0, 1.0 / center))
        ratio = 1.0 / scaled_center
        for _ in range(DEGREE - 1):
            ratio_next = 1.0 / (2.0 * scaled_center - ratio)
            found.append((ratio_next * ratio, 2.0 * ratio_next / half_width))
            ratio = ratio_next
    return found


NEAR_PAIRS = [(i, i ^ 1) for i in range(DEVICES)]
OTHER_PAIRS = [
    pair for i in range(1, DEVICES - 1, 2) for pair in ((i, i + 1), (i + 1, i))
]


def exchange(near_message, other_message):
    other = lax.ppermute(other_message, AXES, OTHER_PAIRS)
    near = lax.ppermute(near_message, AXES, NEAR_PAIRS)
    return near, other


def call(kernel, outs, scratch=(), **options):
    return pl.pallas_call(
        kernel,
        out_shape=outs,
        scratch_shapes=list(scratch),
        compiler_params=pltpu.CompilerParams(vmem_limit_bytes=20 << 20),
        **options,
    )


STATE = shaped(96, 256)
SHARED = shaped(24, 128)
ELEMENT_ROWS = shaped(DOFS, ELEM)


def rows(count):
    return pltpu.VMEM((count, ELEM), F32)


def local(
    start_field, element_loads, element_coefs, element_nodes, move_list, face_nodes, stiffness
):
    integers = functools.partial(shaped, dtype=jnp.int32)
    far, near, other, places, field, loads, coefs, moves, nodes, stiff = call(
        pack_kernel,
        (
            shaped(DEVICES, 1, 256),
            shaped(40, 256),
            shaped(40, 256),
            integers(8, 128),
            STATE,
            ELEMENT_ROWS,
            shaped(2, ELEM),
            integers(3, ELEM),
            integers(PER, ELEM),
            shaped(2, DOFS, DOFS),
        ),
        [
            pltpu.VMEM((2, FACE), jnp.int32),
            pltpu.VMEM((3, OWN), F32),
            pltpu.VMEM((DEVICES, 1, 256), F32),
            pltpu.SemaphoreType.DMA((8,)),
        ],
        in_specs=[pl.BlockSpec(memory_space=pltpu.HBM)] * 7,
        out_specs=[pl.BlockSpec(memory_space=pltpu.HBM)]
        + [pl.BlockSpec(memory_space=pltpu.VMEM)] * 9,
    )(*[pltpu.with_memory_space_constraint(x, pltpu.HBM) for x in (element_loads, element_coefs, move_list, face_nodes, start_field, element_nodes, stiffness)])
    field_message = near
    near, other = exchange(near, other)
    far = lax.all_to_all(far, AXES, split_axis=0, concat_axis=0, tiled=True)
    nodes, shared_index, unshared, blocks, gathered = call(
        index_kernel,
        (
            integers(PER, ELEM),
            integers(PER, ELEM),
            shaped(32, 256),
            shaped(2 * DOFS, 3 * DOFS, dtype=BF16),
            ELEMENT_ROWS,
        ),
        [rows(32), rows(PER)],
    )(field, places, nodes, stiff)
    hot, moved_loads, moved_coefs, coefs, partial, diagonal, shared_field, message = call(
        place_kernel,
        (
            shaped(PER * ELEM, 256, dtype=BF16),
            ELEMENT_ROWS,
            shaped(2, ELEM),
            shaped(2, ELEM),
            STATE,
            STATE,
            SHARED,
            shaped(48, 128),
        ),
        [rows(DOFS), rows(2 * DOFS), rows(2 * DOFS), rows(2 * DOFS), rows(384), rows(DOFS)]
        + [pltpu.SemaphoreType.DMA((2,))],
        out_specs=[
            pl.BlockSpec(memory_space=pltpu.HBM if i in (1, 2) else pltpu.VMEM) for i in range(8)
        ],
    )(
        loads, coefs, moves, far, near, other, field_message, stiff,
        gathered, nodes, shared_index, places, blocks,
    )
    near, other = exchange(message, message)
    plan = steps()
    scratch = [rows(DOFS)] * 3
    window_scratch = [rows(DOFS)] * 2 + [rows(192)]
    residual = partial
    inverse, update, field, gathered, hot_shared = call(
        functools.partial(begin_unshared, plan[0]),
        (STATE, STATE, STATE, ELEMENT_ROWS, shaped(PER * ELEM, 128, dtype=BF16)),
    )(partial, diagonal, unshared, field, nodes, hot, shared_index)
    fixed = (shared_index, coefs, hot_shared, blocks)
    shared_residual, shared_inverse, shared_update, shared_field, values, message = call(
        functools.partial(begin_shared, plan[0]),
        (SHARED, SHARED, SHARED, SHARED, ELEMENT_ROWS, SHARED),
        scratch,
    )(message, near, other, shared_field, gathered, *fixed)
    for step in plan[1:-1]:
        near, other = exchange(message, message)
        residual, update, field, gathered = call(
            functools.partial(step_unshared, step),
            (STATE, STATE, STATE, ELEMENT_ROWS),
            window_scratch,
        )(values, residual, inverse, update, field, nodes, hot)
        shared_residual, shared_update, shared_field, values, message = call(
            functools.partial(step_shared, step),
            (SHARED, SHARED, SHARED, ELEMENT_ROWS, SHARED),
            scratch,
        )(
            message, near, other, shared_residual, shared_inverse, shared_update, shared_field,
            gathered, *fixed,
        )
    near, other = exchange(message, message)
    field = call(
        functools.partial(last_unshared, plan[-1]), STATE, window_scratch
    )(values, residual, inverse, update, field, nodes, hot)
    field = call(functools.partial(last_shared, plan[-1]), shaped(3, OWN))(
        message, near, other, shared_residual, shared_inverse, shared_update, shared_field, field,
        unshared, places,
    )
    return field, moved_loads, moved_coefs


def solution(mesh):
    split_columns = P(None, AXES)
    return jax.shard_map(
        local,
        mesh=mesh,
        in_specs=(split_columns,) * 6 + (P(),),
        out_specs=(split_columns,) * 3,
        check_vma=False,
    )
```

```python
import functools

import jax
import jax.numpy as jnp
from jax import lax
from jax.experimental import pallas as pl
from jax.experimental.pallas import tpu as pltpu
from jax.sharding import PartitionSpec as P


NEAR_CAP = 16
DEGREE = 4
SWEEPS = 2
DEVICES = 128
ELEM = 256
DOFS = 192
PER = 64
OWN = 6912
FACE = 192
OWN_ROWS = OWN // 256
OWN_CHUNKS = OWN // 128
SHARED_ROWS = 6
BLOCK = 32

center = 1.125
half_width = 0.875

AXES = ("seg", "sub")
F32 = jnp.float32
BF16 = jnp.bfloat16


def split(x):
    high = x.astype(BF16).astype(F32)
    return high, x - high


def iota(shape, dimension):
    return lax.broadcasted_iota(jnp.int32, shape, dimension)


def lane_pick(rows, lane):
    return jnp.take_along_axis(rows, lane, axis=1)


def gather_own(state_ref, nodes_ref, out_ref, extra_ref=None, extra_out=None):
    def block(b, carry):
        row = pl.multiple_of(b * 8, 8)
        for half in range(2):
            lanes = slice(half * 128, half * 128 + 128)
            index = nodes_ref[pl.ds(row, 8), lanes]
            lane = index & 127
            chunk = index >> 7
            found = [jnp.zeros((8, 128), F32)] * (3 if extra_ref is None else 4)
            for k in range(OWN_CHUNKS):
                here = chunk == k
                part = slice((k % 2) * 128, (k % 2) * 128 + 128)
                for c in range(len(found)):
                    source, line = (state_ref, 32 * c + k // 2) if c < 3 else (extra_ref, k // 2)
                    values = jnp.broadcast_to(source[line : line + 1, part], (8, 128))
                    found[c] = jnp.where(here, lane_pick(values, lane), found[c])
            for c in range(3):
                out_ref[pl.ds(c * PER + row, 8), lanes] = found[c]
            if extra_ref is not None:
                extra_out[pl.ds(row, 8), lanes] = found[3]
        return carry

    lax.fori_loop(0, PER // 8, block, 0)


def gather_mixed(state_ref, nodes_ref, hot_ref, out_ref):
    table = jnp.concatenate(split(state_ref[...]), axis=0).astype(BF16)
    line = iota((32, 256), 0)
    half_rows = PER // 2

    def block(b, carry):
        row = pl.multiple_of(b * 8, 8)
        for half in range(2):
            lanes = slice(half * 128, half * 128 + 128)
            index = nodes_ref[pl.ds(row, 8), lanes]
            lane = index & 127
            chunk = index >> 7
            found = [jnp.zeros((8, 128), F32)] * 3
            for k in range(OWN_CHUNKS):
                here = chunk == k
                part = slice((k % 2) * 128, (k % 2) * 128 + 128)
                for c in range(3):
                    source = 32 * c + k // 2
                    values = jnp.broadcast_to(state_ref[source : source + 1, part], (8, 128))
                    found[c] = jnp.where(here, lane_pick(values, lane), found[c])
            for c in range(3):
                out_ref[pl.ds(c * PER + row, 8), lanes] = found[c]
        other = pl.multiple_of(b * 8 + half_rows, 8)
        lines = nodes_ref[pl.ds(other, 8), :] >> 8
        for k in range(8):
            hot = hot_ref[pl.ds(pl.multiple_of((other + k) * 256, 256), 256), :]
            got = lax.dot_general(
                table, hot, (((1,), (1,)), ((), ())), preferred_element_type=F32
            )
            here = lines[k : k + 1, :] == line
            for c in range(3):
                both = got[32 * c : 32 * c + 32] + got[96 + 32 * c : 128 + 32 * c]
                out_ref[pl.ds(c * PER + other + k, 1), :] = jnp.sum(
                    jnp.where(here, both, 0.0), axis=0, keepdims=True
                )
        return carry

    lax.fori_loop(0, half_rows // 8, block, 0)


def gather_shared(shared_ref, index_ref, rows_ref, out_ref, first_row):
    tables = [
        [
            jnp.broadcast_to(shared_ref[8 * c + r : 8 * c + r + 1, :], (8, 128))
            for r in range(SHARED_ROWS)
        ]
        for c in range(3)
    ]
    for b in range(PER // 8):
        for half in range(2):
            lanes = slice(half * 128, half * 128 + 128)
            index = index_ref[8 * b : 8 * b + 8, lanes]
            lane = index & 127
            chunk = index >> 7
            masks = [chunk == r for r in range(first_row, SHARED_ROWS)]
            for c in range(3):
                rows = slice(c * PER + 8 * b, c * PER + 8 * b + 8)
                found = rows_ref[rows, lanes]
                for r in range(first_row, SHARED_ROWS):
                    found = jnp.where(masks[r - first_row], lane_pick(tables[c][r], lane), found)
                out_ref[rows, lanes] = found


def scatter_elements(nodes_ref, hot_ref, values_ref, high_ref, low_ref, sums_ref, channels):
    high, low = split(values_ref[...])
    high_ref[...] = high
    low_ref[...] = low
    sums_ref[...] = jnp.zeros_like(sums_ref)
    lines = iota((32, 256), 0).astype(F32).astype(BF16)
    zero = jnp.zeros((), BF16)

    def block(b, carry):
        row = pl.multiple_of(b * BLOCK, BLOCK)
        line = (nodes_ref[pl.ds(row, BLOCK), :] >> 8).astype(F32)
        left = []
        for k in range(BLOCK):
            here = line[k : k + 1, :].astype(BF16) == lines
            left.append(
                jnp.concatenate(
                    [
                        jnp.where(
                            here,
                            jnp.broadcast_to(ref[pl.ds(c * PER + row + k, 1), :], (32, 256)).astype(
                                BF16
                            ),
                            zero,
                        )
                        for ref in (high_ref, low_ref)
                        for c in range(channels)
                    ],
                    axis=0,
                )
            )
        left = jnp.concatenate(left, axis=1)
        right = hot_ref[pl.ds(pl.multiple_of(row * 256, 256), BLOCK * 256), :]
        sums_ref[...] += jnp.dot(left, right, preferred_element_type=F32)
        return carry

    lax.fori_loop(0, PER // BLOCK, block, 0)


def scatter_shared(index_ref, hot_ref, values_ref, high_ref, low_ref, sums_ref, out_ref):
    high, low = split(values_ref[...])
    high_ref[...] = high
    low_ref[...] = low
    sums_ref[...] = jnp.zeros_like(sums_ref)
    lines = iota((8, 256), 0)

    def block(b, carry):
        row = pl.multiple_of(b * BLOCK, BLOCK)
        line = index_ref[pl.ds(row, BLOCK), :] >> 7
        left = []
        for k in range(BLOCK):
            here = line[k : k + 1, :] == lines
            left.append(
                jnp.concatenate(
                    [
                        jnp.where(
                            here,
                            jnp.broadcast_to(ref[pl.ds(c * PER + row + k, 1), :], (8, 256)),
                            0.0,
                        )
                        for ref in (high_ref, low_ref)
                        for c in range(3)
                    ],
                    axis=0,
                ).astype(BF16)
            )
        left = jnp.concatenate(left, axis=1)
        right = hot_ref[pl.ds(pl.multiple_of(row * 256, 256), BLOCK * 256), :]
        sums_ref[...] += jnp.dot(left, right, preferred_element_type=F32)
        return carry

    lax.fori_loop(0, PER // BLOCK, block, 0)
    out_ref[...] = sums_ref[0:24, :] + sums_ref[24:48, :]


def add_parts(sums_ref, first, channels):
    top = 32 * first
    low = top + 32 * channels
    return sums_ref[top : top + 96, :] + sums_ref[low : low + 96, :]


def expand_own_faces(places, channels, parts):
    lines = iota((32, 128), 0)
    lanes = iota((256, 128), 0)
    rows = []
    for values in channels:
        rest = values
        for _ in range(parts):
            high, rest = split(rest)
            rows.append(high)
    left, right = [], []
    for k in range(3):
        here = (places[k : k + 1, :] >> 8) == lines
        left.append(
            jnp.concatenate([jnp.where(here, r[k : k + 1, :], 0.0) for r in rows], axis=0).astype(BF16)
        )
        right.append(jnp.where((places[k : k + 1, :] & 255) == lanes, 1.0, 0.0).astype(BF16))
    sums = lax.dot_general(
        jnp.concatenate(left, axis=1),
        jnp.concatenate(right, axis=1),
        (((1,), (1,)), ((), ())),
        preferred_element_type=F32,
    )
    out = []
    for i in range(len(channels)):
        total = sums[32 * parts * i : 32 * parts * i + 32]
        for q in range(1, parts):
            start = 32 * (parts * i + q)
            total = total + sums[start : start + 32]
        out.append(total)
    return jnp.concatenate(out, axis=0)


def take_shared(state_ref, places, out_ref, base, ghosts):
    found = [[None] * 3 for _ in range(3)]
    line = iota((8, 128), 0)
    for r in range(3):
        place = jnp.broadcast_to(places[r : r + 1, :], (8, 128))
        lane = place & 127
        chunk = place >> 7
        masks = [
            [chunk == 2 * (8 * t + line) + half for half in range(2)] for t in range(4)
        ]
        for c in range(3):
            got = jnp.zeros((8, 128), F32)
            for t in range(4):
                for half in range(2):
                    values = state_ref[
                        32 * c + 8 * t : 32 * c + 8 * t + 8, half * 128 : half * 128 + 128
                    ]
                    got = jnp.where(masks[t][half], lane_pick(values, lane), got)
            found[c][r] = jnp.sum(got, axis=0, keepdims=True)
    for c in range(3):
        top = 32 * c + OWN_ROWS
        if ghosts:
            others = [
                state_ref[top : top + 1, 0:128],
                state_ref[top : top + 1, 128:256],
                state_ref[top + 1 : top + 2, 0:128],
                jnp.zeros((2, 128), F32),
            ]
        else:
            others = [jnp.zeros((5, 128), F32)]
        out_ref[base + 8 * c : base + 8 * c + 8, 0:128] = jnp.concatenate(found[c] + others, axis=0)


def from_neighbours(near_ref, far_ref, base):
    first_core = lax.axis_index("sub") == 0
    left = iota((1, 128), 1) < 64
    out = []
    for c in range(3):
        rows = slice(base + 8 * c, base + 8 * c + 8)
        near = near_ref[rows, 0:128]
        far = far_ref[rows, 0:128]
        before = jnp.where(first_core, far, near)
        after = jnp.where(first_core, near, far)
        before_turned = pltpu.roll(before, 64, 1)
        after_turned = pltpu.roll(after, 64, 1)
        out += [
            before[5:6],
            jnp.where(left, before_turned[4:5], after_turned[4:5]),
            after[3:4],
            before[2:3],
            jnp.where(left, before_turned[1:2], after_turned[1:2]),
            after[0:1],
            jnp.zeros((2, 128), F32),
        ]
    return jnp.concatenate(out, axis=0)


def pack_kernel(
    loads_hbm, coefs_hbm, move_hbm, face_hbm, field_hbm, nodes_hbm, stiff_hbm, far_hbm, near_out,
    other_out, places_ref, state_ref, loads_ref, coefs_ref, move_ref, nodes_ref, stiff_ref,
    face_ref, field_ref, far_rows, sems,
):
    pairs = (
        (move_hbm, move_ref),
        (coefs_hbm, coefs_ref),
        (loads_hbm, loads_ref),
        (face_hbm, face_ref),
        (field_hbm, field_ref),
        (nodes_hbm, nodes_ref),
        (stiff_hbm, stiff_ref),
    )
    copies = [
        pltpu.make_async_copy(source, target, sems.at[i]) for i, (source, target) in enumerate(pairs)
    ]
    for copy in copies:
        copy.start()
    for copy in copies[:3]:
        copy.wait()
    me = lax.axis_index(AXES)
    first_core = lax.axis_index("sub") == 0
    near = jnp.where(first_core, me + 1, me - 1)
    other = jnp.where(first_core, me - 1, me + 1)
    target = move_ref[0:1, :]
    place = move_ref[2:3, :]
    code = jnp.where(
        target == me,
        -1,
        jnp.where(
            target == near,
            DEVICES + place,
            jnp.where(target == other, DEVICES + NEAR_CAP + place, target),
        ),
    )
    rows = DEVICES + 2 * NEAR_CAP
    chosen = jnp.where(code == iota((rows, ELEM), 0), 1.0, 0.0)
    slot = (move_ref[1:2, :] + 1).astype(F32)
    records = jnp.concatenate(
        [loads_ref[...], coefs_ref[...], slot, jnp.zeros((61, ELEM), F32)], axis=0
    )
    packed = lax.dot_general(
        chosen,
        records,
        (((1,), (1,)), ((), ())),
        precision=lax.Precision.HIGHEST,
        preferred_element_type=F32,
    )
    far_rows[:, 0, :] = packed[:DEVICES]
    far_copy = pltpu.make_async_copy(far_rows, far_hbm, sems.at[7])
    far_copy.start()
    near_out[0:NEAR_CAP, :] = packed[DEVICES : DEVICES + NEAR_CAP]
    other_out[0:NEAR_CAP, :] = packed[DEVICES + NEAR_CAP :]
    near_out[NEAR_CAP:, :] = jnp.zeros((24, 256), F32)
    for copy in copies[3:5]:
        copy.wait()
    places_ref[...] = jnp.zeros((8, 128), jnp.int32)
    places_ref[0:1, :] = face_ref[0:1, 0:128]
    places_ref[1:2, 0:64] = face_ref[0:1, 128:192]
    places_ref[1:2, 64:128] = face_ref[1:2, 128:192]
    places_ref[2:3, :] = face_ref[1:2, 0:128]
    state_ref[...] = jnp.zeros_like(state_ref)
    for c in range(3):
        for h in range(OWN_ROWS):
            state_ref[32 * c + h : 32 * c + h + 1, :] = field_ref[c : c + 1, 256 * h : 256 * h + 256]
    take_shared(state_ref, places_ref[...], near_out, NEAR_CAP, False)
    other_out[NEAR_CAP:, :] = near_out[NEAR_CAP:, :]
    for copy in copies[5:]:
        copy.wait()
    far_copy.wait()


def index_kernel(
    state_ref,
    places_ref,
    nodes_ref,
    stiff_ref,
    index_ref,
    shared_index_ref,
    unshared_ref,
    blocks_ref,
    gathered_ref,
    positions,
    found,
):
    nodes = nodes_ref[...]
    ghost = nodes - OWN
    ahead = ghost - FACE
    shared = jnp.where(ahead < 0, ghost, jnp.where(ahead < 128, ahead + 256, ahead + 64))
    index_ref[...] = jnp.where(ghost < 0, nodes, OWN + shared)
    places = places_ref[...]
    numbers = (128 * iota((3, 128), 0) + iota((3, 128), 1) + 1).astype(F32)
    positions[...] = expand_own_faces(places, [numbers], 2)
    line = iota((32, 256), 0)
    unshared_ref[...] = jnp.where((positions[...] == 0.0) & (line < OWN_ROWS), 1.0, 0.0)
    gather_own(state_ref, index_ref, gathered_ref, positions, found)
    shared_index_ref[...] = jnp.where(
        ghost < 0, found[...].astype(jnp.int32) - 1, shared + 3 * 128
    )
    for i in range(2):
        high, low = split(stiff_ref[i])
        high = high.astype(BF16)
        blocks_ref[DOFS * i : DOFS * i + DOFS, :] = high
        blocks_ref[DOFS * (2 + i) : DOFS * (3 + i), :] = low.astype(BF16)


def build_hot(index_ref, hot_ref, width):
    low = (index_ref[...] & (width - 1)).astype(F32)
    lanes = iota((16, width), 1).astype(F32).astype(BF16)
    one = jnp.ones((), BF16)
    zero = jnp.zeros((), BF16)
    for half in range(2):
        turned = low[:, half * 128 : half * 128 + 128].T.astype(BF16)
        for b in range(8):
            columns = turned[16 * b : 16 * b + 16]
            for n in range(PER):
                top = 256 * n + half * 128 + 16 * b
                column = jnp.broadcast_to(columns[:, n : n + 1], (16, width))
                hot_ref[top : top + 16, :] = jnp.where(column == lanes, one, zero)


def multiply_blocks(blocks_ref, rows):
    high, low = split(rows)
    high = high.astype(BF16)
    low = low.astype(BF16)
    block_high = blocks_ref[: 2 * DOFS]
    block_low = blocks_ref[2 * DOFS :]
    return (
        jnp.dot(block_low, high, preferred_element_type=F32)
        + jnp.dot(block_high, low, preferred_element_type=F32)
        + jnp.dot(block_high, high, preferred_element_type=F32)
    )


def place_kernel(
    loads_ref,
    coefs_ref,
    move_ref,
    far_ref,
    near_in,
    other_in,
    field_message,
    stiff_ref,
    gathered_in,
    nodes_ref,
    shared_index_ref,
    places_ref,
    blocks_ref,
    hot_ref,
    moved_loads,
    moved_coefs,
    coefs_out,
    partial_ref,
    diagonal_ref,
    shared_field,
    message,
    gathered,
    values,
    value_high,
    value_low,
    sums,
    kept_loads,
    sems,
):
    shared_field[...] = field_message[NEAR_CAP:, 0:128] + from_neighbours(near_in, other_in, NEAR_CAP)
    gather_shared(shared_field, shared_index_ref, gathered_in, gathered, 3)
    products = multiply_blocks(blocks_ref, gathered[...])
    me = lax.axis_index(AXES)
    received = jnp.concatenate(
        [far_ref[:, 0, :], near_in[0:NEAR_CAP, :], other_in[0:NEAR_CAP, :]], axis=0
    )
    rows = DEVICES + 2 * NEAR_CAP
    slot = received[:, DOFS + 2 : DOFS + 3].astype(jnp.int32)
    chosen = jnp.where(slot == iota((rows, ELEM), 1) + 1, 1.0, 0.0)
    arrived = lax.dot_general(
        received,
        chosen,
        (((0,), (0,)), ((), ())),
        precision=lax.Precision.HIGHEST,
        preferred_element_type=F32,
    )
    stays = move_ref[0:1, :] == me
    loads = jnp.where(stays, loads_ref[...], 0.0) + arrived[:DOFS]
    coefs = jnp.where(stays, coefs_ref[...], 0.0) + arrived[DOFS : DOFS + 2]
    kept_loads[...] = loads
    coefs_out[...] = coefs
    copies = (
        pltpu.make_async_copy(kept_loads, moved_loads, sems.at[0]),
        pltpu.make_async_copy(coefs_out, moved_coefs, sems.at[1]),
    )
    for copy in copies:
        copy.start()
    values[0:DOFS, :] = loads - (products[:DOFS] * coefs[0:1, :] + products[DOFS:] * coefs[1:2, :])
    eye = iota((DOFS, DOFS), 0) == iota((DOFS, DOFS), 1)
    first_diag = jnp.sum(jnp.where(eye, stiff_ref[0], 0.0), axis=1, keepdims=True)
    second_diag = jnp.sum(jnp.where(eye, stiff_ref[1], 0.0), axis=1, keepdims=True)
    values[DOFS:, :] = first_diag * coefs[0:1, :] + second_diag * coefs[1:2, :]
    build_hot(nodes_ref, hot_ref, 256)
    scatter_elements(nodes_ref, hot_ref, values, value_high, value_low, sums, 6)
    partial_ref[...] = add_parts(sums, 0, 6)
    diagonal_ref[...] = add_parts(sums, 3, 6)
    take_shared(partial_ref, places_ref[...], message, 0, True)
    take_shared(diagonal_ref, places_ref[...], message, 24, True)
    for copy in copies:
        copy.wait()


def apply_operator(
    shared_update, gathered_in, shared_index_ref, coefs_ref, hot_ref, blocks_ref, values_ref,
    message, gathered, value_high, value_low, sums,
):
    gather_shared(shared_update, shared_index_ref, gathered_in, gathered, 0)
    products = multiply_blocks(blocks_ref, gathered[...])
    values_ref[...] = products[:DOFS] * coefs_ref[0:1, :] + products[DOFS:] * coefs_ref[1:2, :]
    scatter_shared(shared_index_ref, hot_ref, values_ref, value_high, value_low, sums, message)


def inverse_of(diagonal):
    return jnp.where(diagonal == 0.0, 0.0, 1.0 / diagonal)


def begin_unshared(
    step, partial_ref, diagonal_ref, unshared_ref, field_ref, nodes_ref, hot_ref, shared_index_ref,
    inverse_out, update_out, field_out, gathered_out, hot_shared_ref,
):
    build_hot(shared_index_ref, hot_shared_ref, 128)
    unshared = jnp.concatenate([unshared_ref[...]] * 3, axis=0)
    inverse = jnp.where(unshared > 0.0, inverse_of(diagonal_ref[...]), 0.0)
    update = step[1] * (partial_ref[...] * inverse)
    inverse_out[...] = inverse
    update_out[...] = update
    field_out[...] = field_ref[...] + update
    gather_mixed(update_out, nodes_ref, hot_ref, gathered_out)


def begin_shared(
    step, message_in, near_in, other_in, shared_field, gathered_in, shared_index_ref, coefs_ref,
    hot_ref, blocks_ref, residual_out, inverse_out, update_out, field_out, values_ref, message,
    gathered, value_high, value_low, sums,
):
    residual = message_in[0:24, :] + from_neighbours(near_in, other_in, 0)
    inverse = inverse_of(message_in[24:48, :] + from_neighbours(near_in, other_in, 24))
    update = step[1] * (residual * inverse)
    residual_out[...] = residual
    inverse_out[...] = inverse
    update_out[...] = update
    field_out[...] = shared_field[...] + update
    apply_operator(
        update_out, gathered_in, shared_index_ref, coefs_ref, hot_ref, blocks_ref, values_ref,
        message, gathered, value_high, value_low, sums,
    )


def next_update(step, residual, inverse, update):
    changed = step[1] * (residual * inverse)
    return step[0] * update + changed if step[0] else changed


def step_unshared(
    step, values_ref, residual_ref, inverse_ref, update_ref, field_ref, nodes_ref, hot_ref,
    residual_out, update_out, field_out, gathered_out, value_high, value_low, sums,
):
    scatter_elements(nodes_ref, hot_ref, values_ref, value_high, value_low, sums, 3)
    residual = residual_ref[...] - add_parts(sums, 0, 3)
    update = next_update(step, residual, inverse_ref[...], update_ref[...])
    residual_out[...] = residual
    update_out[...] = update
    field_out[...] = field_ref[...] + update
    gather_mixed(update_out, nodes_ref, hot_ref, gathered_out)


def step_shared(
    step, message_in, near_in, other_in, residual_ref, inverse_ref, update_ref, field_ref,
    gathered_in, shared_index_ref, coefs_ref, hot_ref, blocks_ref, residual_out, update_out,
    field_out, values_ref, message, gathered, value_high, value_low, sums,
):
    residual = residual_ref[...] - (message_in[...] + from_neighbours(near_in, other_in, 0))
    update = next_update(step, residual, inverse_ref[...], update_ref[...])
    residual_out[...] = residual
    update_out[...] = update
    field_out[...] = field_ref[...] + update
    apply_operator(
        update_out, gathered_in, shared_index_ref, coefs_ref, hot_ref, blocks_ref, values_ref,
        message, gathered, value_high, value_low, sums,
    )


def last_unshared(
    step, values_ref, residual_ref, inverse_ref, update_ref, field_ref, nodes_ref, hot_ref, field_out,
    value_high, value_low, sums,
):
    scatter_elements(nodes_ref, hot_ref, values_ref, value_high, value_low, sums, 3)
    residual = residual_ref[...] - add_parts(sums, 0, 3)
    field_out[...] = field_ref[...] + next_update(step, residual, inverse_ref[...], update_ref[...])


def last_shared(
    step, message_in, near_in, other_in, residual_ref, inverse_ref, update_ref, shared_field,
    field_ref, unshared_ref, places_ref, out_ref,
):
    residual = residual_ref[...] - (message_in[...] + from_neighbours(near_in, other_in, 0))
    shared = shared_field[...] + next_update(step, residual, inverse_ref[...], update_ref[...])
    faces = expand_own_faces(places_ref[...], [shared[8 * c : 8 * c + 3] for c in range(3)], 3)
    unshared = jnp.concatenate([unshared_ref[...]] * 3, axis=0)
    field = jnp.where(unshared > 0.0, field_ref[...], faces)
    for c in range(3):
        for h in range(OWN_ROWS):
            out_ref[c : c + 1, 256 * h : 256 * h + 256] = field[32 * c + h : 32 * c + h + 1, :]


def shaped(*shape, dtype=F32):
    return jax.ShapeDtypeStruct(shape, dtype)


def steps():
    scaled_center = center / half_width
    found = []
    for _ in range(SWEEPS):
        found.append((0.0, 1.0 / center))
        ratio = 1.0 / scaled_center
        for _ in range(DEGREE - 1):
            ratio_next = 1.0 / (2.0 * scaled_center - ratio)
            found.append((ratio_next * ratio, 2.0 * ratio_next / half_width))
            ratio = ratio_next
    return found


NEAR_PAIRS = [(i, i ^ 1) for i in range(DEVICES)]
OTHER_PAIRS = [
    pair for i in range(1, DEVICES - 1, 2) for pair in ((i, i + 1), (i + 1, i))
]


def exchange(near_message, other_message):
    other = lax.ppermute(other_message, AXES, OTHER_PAIRS)
    near = lax.ppermute(near_message, AXES, NEAR_PAIRS)
    return near, other


def call(kernel, outs, scratch=(), **options):
    return pl.pallas_call(
        kernel,
        out_shape=outs,
        scratch_shapes=list(scratch),
        compiler_params=pltpu.CompilerParams(vmem_limit_bytes=20 << 20),
        **options,
    )


STATE = shaped(96, 256)
SHARED = shaped(24, 128)
ELEMENT_ROWS = shaped(DOFS, ELEM)


def rows(count):
    return pltpu.VMEM((count, ELEM), F32)


def local(
    start_field, element_loads, element_coefs, element_nodes, move_list, face_nodes, stiffness
):
    integers = functools.partial(shaped, dtype=jnp.int32)
    far, near, other, places, field, loads, coefs, moves, nodes, stiff = call(
        pack_kernel,
        (
            shaped(DEVICES, 1, 256),
            shaped(40, 256),
            shaped(40, 256),
            integers(8, 128),
            STATE,
            ELEMENT_ROWS,
            shaped(2, ELEM),
            integers(3, ELEM),
            integers(PER, ELEM),
            shaped(2, DOFS, DOFS),
        ),
        [
            pltpu.VMEM((2, FACE), jnp.int32),
            pltpu.VMEM((3, OWN), F32),
            pltpu.VMEM((DEVICES, 1, 256), F32),
            pltpu.SemaphoreType.DMA((8,)),
        ],
        in_specs=[pl.BlockSpec(memory_space=pltpu.HBM)] * 7,
        out_specs=[pl.BlockSpec(memory_space=pltpu.HBM)]
        + [pl.BlockSpec(memory_space=pltpu.VMEM)] * 9,
    )(*[pltpu.with_memory_space_constraint(x, pltpu.HBM) for x in (element_loads, element_coefs, move_list, face_nodes, start_field, element_nodes, stiffness)])
    field_message = near
    near, other = exchange(near, other)
    far = lax.all_to_all(far, AXES, split_axis=0, concat_axis=0, tiled=True)
    nodes, shared_index, unshared, blocks, gathered = call(
        index_kernel,
        (
            integers(PER, ELEM),
            integers(PER, ELEM),
            shaped(32, 256),
            shaped(4 * DOFS, DOFS, dtype=BF16),
            ELEMENT_ROWS,
        ),
        [rows(32), rows(PER)],
    )(field, places, nodes, stiff)
    hot, moved_loads, moved_coefs, coefs, partial, diagonal, shared_field, message = call(
        place_kernel,
        (
            shaped(PER * ELEM, 256, dtype=BF16),
            ELEMENT_ROWS,
            shaped(2, ELEM),
            shaped(2, ELEM),
            STATE,
            STATE,
            SHARED,
            shaped(48, 128),
        ),
        [rows(DOFS), rows(2 * DOFS), rows(2 * DOFS), rows(2 * DOFS), rows(384), rows(DOFS)]
        + [pltpu.SemaphoreType.DMA((2,))],
        out_specs=[
            pl.BlockSpec(memory_space=pltpu.HBM if i in (1, 2) else pltpu.VMEM) for i in range(8)
        ],
    )(
        loads, coefs, moves, far, near, other, field_message, stiff,
        gathered, nodes, shared_index, places, blocks,
    )
    near, other = exchange(message, message)
    plan = steps()
    scratch = [rows(DOFS)] * 3 + [pltpu.VMEM((48, 128), F32)]
    window_scratch = [rows(DOFS)] * 2 + [rows(192)]
    residual = partial
    inverse, update, field, gathered, hot_shared = call(
        functools.partial(begin_unshared, plan[0]),
        (STATE, STATE, STATE, ELEMENT_ROWS, shaped(PER * ELEM, 128, dtype=BF16)),
    )(partial, diagonal, unshared, field, nodes, hot, shared_index)
    fixed = (shared_index, coefs, hot_shared, blocks)
    shared_residual, shared_inverse, shared_update, shared_field, values, message = call(
        functools.partial(begin_shared, plan[0]),
        (SHARED, SHARED, SHARED, SHARED, ELEMENT_ROWS, SHARED),
        scratch,
    )(message, near, other, shared_field, gathered, *fixed)
    for step in plan[1:-1]:
        near, other = exchange(message, message)
        residual, update, field, gathered = call(
            functools.partial(step_unshared, step),
            (STATE, STATE, STATE, ELEMENT_ROWS),
            window_scratch,
        )(values, residual, inverse, update, field, nodes, hot)
        shared_residual, shared_update, shared_field, values, message = call(
            functools.partial(step_shared, step),
            (SHARED, SHARED, SHARED, ELEMENT_ROWS, SHARED),
            scratch,
        )(
            message, near, other, shared_residual, shared_inverse, shared_update, shared_field,
            gathered, *fixed,
        )
    near, other = exchange(message, message)
    field = call(
        functools.partial(last_unshared, plan[-1]), STATE, window_scratch
    )(values, residual, inverse, update, field, nodes, hot)
    field = call(functools.partial(last_shared, plan[-1]), shaped(3, OWN))(
        message, near, other, shared_residual, shared_inverse, shared_update, shared_field, field,
        unshared, places,
    )
    return field, moved_loads, moved_coefs


def solution(mesh):
    split_columns = P(None, AXES)
    return jax.shard_map(
        local,
        mesh=mesh,
        in_specs=(split_columns,) * 6 + (P(),),
        out_specs=(split_columns,) * 3,
        check_vma=False,
    )
```

```python
import functools

import jax
import jax.numpy as jnp
from jax import lax
from jax.experimental import pallas as pl
from jax.experimental.pallas import tpu as pltpu
from jax.sharding import PartitionSpec as P


NEAR_CAP = 16
DEGREE = 4
SWEEPS = 2
DEVICES = 128
ELEM = 256
DOFS = 192
PER = 64
OWN = 6912
FACE = 192
OWN_ROWS = OWN // 256
OWN_CHUNKS = OWN // 128
SHARED_ROWS = 6
BLOCK = 32

center = 1.125
half_width = 0.875

AXES = ("seg", "sub")
F32 = jnp.float32
BF16 = jnp.bfloat16


def split(x):
    high = x.astype(BF16).astype(F32)
    return high, x - high


def iota(shape, dimension):
    return lax.broadcasted_iota(jnp.int32, shape, dimension)


def lane_pick(rows, lane):
    return jnp.take_along_axis(rows, lane, axis=1)


def gather_own(state_ref, nodes_ref, out_ref, extra_ref=None, extra_out=None):
    def block(b, carry):
        row = pl.multiple_of(b * 8, 8)
        for half in range(2):
            lanes = slice(half * 128, half * 128 + 128)
            index = nodes_ref[pl.ds(row, 8), lanes]
            lane = index & 127
            chunk = index >> 7
            found = [jnp.zeros((8, 128), F32)] * (3 if extra_ref is None else 4)
            for k in range(OWN_CHUNKS):
                here = chunk == k
                part = slice((k % 2) * 128, (k % 2) * 128 + 128)
                for c in range(len(found)):
                    source, line = (state_ref, 32 * c + k // 2) if c < 3 else (extra_ref, k // 2)
                    values = jnp.broadcast_to(source[line : line + 1, part], (8, 128))
                    found[c] = jnp.where(here, lane_pick(values, lane), found[c])
            for c in range(3):
                out_ref[pl.ds(c * PER + row, 8), lanes] = found[c]
            if extra_ref is not None:
                extra_out[pl.ds(row, 8), lanes] = found[3]
        return carry

    lax.fori_loop(0, PER // 8, block, 0)


def gather_mixed(state_ref, nodes_ref, hot_ref, out_ref):
    table = jnp.concatenate(split(state_ref[...]), axis=0).astype(BF16)
    line = iota((32, 256), 0)
    half_rows = PER // 2

    def block(b, carry):
        row = pl.multiple_of(b * 8, 8)
        for half in range(2):
            lanes = slice(half * 128, half * 128 + 128)
            index = nodes_ref[pl.ds(row, 8), lanes]
            lane = index & 127
            chunk = index >> 7
            found = [jnp.zeros((8, 128), F32)] * 3
            for k in range(OWN_CHUNKS):
                here = chunk == k
                part = slice((k % 2) * 128, (k % 2) * 128 + 128)
                for c in range(3):
                    source = 32 * c + k // 2
                    values = jnp.broadcast_to(state_ref[source : source + 1, part], (8, 128))
                    found[c] = jnp.where(here, lane_pick(values, lane), found[c])
            for c in range(3):
                out_ref[pl.ds(c * PER + row, 8), lanes] = found[c]
        other = pl.multiple_of(b * 8 + half_rows, 8)
        lines = nodes_ref[pl.ds(other, 8), :] >> 8
        for k in range(8):
            hot = hot_ref[pl.ds(pl.multiple_of((other + k) * 256, 256), 256), :]
            got = lax.dot_general(
                table, hot, (((1,), (1,)), ((), ())), preferred_element_type=F32
            )
            here = lines[k : k + 1, :] == line
            for c in range(3):
                both = got[32 * c : 32 * c + 32] + got[96 + 32 * c : 128 + 32 * c]
                out_ref[pl.ds(c * PER + other + k, 1), :] = jnp.sum(
                    jnp.where(here, both, 0.0), axis=0, keepdims=True
                )
        return carry

    lax.fori_loop(0, half_rows // 8, block, 0)


def gather_shared(shared_ref, index_ref, rows_ref, out_ref, first_row):
    tables = [
        [
            jnp.broadcast_to(shared_ref[8 * c + r : 8 * c + r + 1, :], (8, 128))
            for r in range(SHARED_ROWS)
        ]
        for c in range(3)
    ]
    for b in range(PER // 8):
        for half in range(2):
            lanes = slice(half * 128, half * 128 + 128)
            index = index_ref[8 * b : 8 * b + 8, lanes]
            lane = index & 127
            chunk = index >> 7
            masks = [chunk == r for r in range(first_row, SHARED_ROWS)]
            for c in range(3):
                rows = slice(c * PER + 8 * b, c * PER + 8 * b + 8)
                found = rows_ref[rows, lanes]
                for r in range(first_row, SHARED_ROWS):
                    found = jnp.where(masks[r - first_row], lane_pick(tables[c][r], lane), found)
                out_ref[rows, lanes] = found


def scatter_elements(nodes_ref, hot_ref, values_ref, high_ref, low_ref, sums_ref, channels):
    high, low = split(values_ref[...])
    high_ref[...] = high
    low_ref[...] = low
    sums_ref[...] = jnp.zeros_like(sums_ref)
    lines = iota((32, 256), 0).astype(F32).astype(BF16)
    zero = jnp.zeros((), BF16)

    def block(b, carry):
        row = pl.multiple_of(b * BLOCK, BLOCK)
        line = (nodes_ref[pl.ds(row, BLOCK), :] >> 8).astype(F32)
        left = []
        for k in range(BLOCK):
            here = line[k : k + 1, :].astype(BF16) == lines
            left.append(
                jnp.concatenate(
                    [
                        jnp.where(
                            here,
                            jnp.broadcast_to(ref[pl.ds(c * PER + row + k, 1), :], (32, 256)).astype(
                                BF16
                            ),
                            zero,
                        )
                        for ref in (high_ref, low_ref)
                        for c in range(channels)
                    ],
                    axis=0,
                )
            )
        left = jnp.concatenate(left, axis=1)
        right = hot_ref[pl.ds(pl.multiple_of(row * 256, 256), BLOCK * 256), :]
        sums_ref[...] += jnp.dot(left, right, preferred_element_type=F32)
        return carry

    lax.fori_loop(0, PER // BLOCK, block, 0)


def scatter_shared(index_ref, hot_ref, values_ref, high_ref, low_ref, sums_ref, out_ref):
    high, low = split(values_ref[...])
    high_ref[...] = high
    low_ref[...] = low
    sums_ref[...] = jnp.zeros_like(sums_ref)
    lines = iota((8, 256), 0)

    def block(b, carry):
        row = pl.multiple_of(b * BLOCK, BLOCK)
        line = index_ref[pl.ds(row, BLOCK), :] >> 7
        left = []
        for k in range(BLOCK):
            here = line[k : k + 1, :] == lines
            left.append(
                jnp.concatenate(
                    [
                        jnp.where(
                            here,
                            jnp.broadcast_to(ref[pl.ds(c * PER + row + k, 1), :], (8, 256)),
                            0.0,
                        )
                        for ref in (high_ref, low_ref)
                        for c in range(3)
                    ],
                    axis=0,
                ).astype(BF16)
            )
        left = jnp.concatenate(left, axis=1)
        right = hot_ref[pl.ds(pl.multiple_of(row * 256, 256), BLOCK * 256), :]
        sums_ref[...] += jnp.dot(left, right, preferred_element_type=F32)
        return carry

    lax.fori_loop(0, PER // BLOCK, block, 0)
    out_ref[...] = sums_ref[0:24, :] + sums_ref[24:48, :]


def add_parts(sums_ref, first, channels):
    top = 32 * first
    low = top + 32 * channels
    return sums_ref[top : top + 96, :] + sums_ref[low : low + 96, :]


def expand_own_faces(places, channels, parts):
    lines = iota((32, 128), 0)
    lanes = iota((256, 128), 0)
    rows = []
    for values in channels:
        rest = values
        for _ in range(parts):
            high, rest = split(rest)
            rows.append(high)
    left, right = [], []
    for k in range(3):
        here = (places[k : k + 1, :] >> 8) == lines
        left.append(
            jnp.concatenate([jnp.where(here, r[k : k + 1, :], 0.0) for r in rows], axis=0).astype(BF16)
        )
        right.append(jnp.where((places[k : k + 1, :] & 255) == lanes, 1.0, 0.0).astype(BF16))
    sums = lax.dot_general(
        jnp.concatenate(left, axis=1),
        jnp.concatenate(right, axis=1),
        (((1,), (1,)), ((), ())),
        preferred_element_type=F32,
    )
    out = []
    for i in range(len(channels)):
        total = sums[32 * parts * i : 32 * parts * i + 32]
        for q in range(1, parts):
            start = 32 * (parts * i + q)
            total = total + sums[start : start + 32]
        out.append(total)
    return jnp.concatenate(out, axis=0)


def take_shared(state_ref, places, out_ref, base, ghosts):
    found = [[None] * 3 for _ in range(3)]
    line = iota((8, 128), 0)
    for r in range(3):
        place = jnp.broadcast_to(places[r : r + 1, :], (8, 128))
        lane = place & 127
        chunk = place >> 7
        masks = [
            [chunk == 2 * (8 * t + line) + half for half in range(2)] for t in range(4)
        ]
        for c in range(3):
            got = jnp.zeros((8, 128), F32)
            for t in range(4):
                for half in range(2):
                    values = state_ref[
                        32 * c + 8 * t : 32 * c + 8 * t + 8, half * 128 : half * 128 + 128
                    ]
                    got = jnp.where(masks[t][half], lane_pick(values, lane), got)
            found[c][r] = jnp.sum(got, axis=0, keepdims=True)
    for c in range(3):
        top = 32 * c + OWN_ROWS
        if ghosts:
            others = [
                state_ref[top : top + 1, 0:128],
                state_ref[top : top + 1, 128:256],
                state_ref[top + 1 : top + 2, 0:128],
                jnp.zeros((2, 128), F32),
            ]
        else:
            others = [jnp.zeros((5, 128), F32)]
        out_ref[base + 8 * c : base + 8 * c + 8, 0:128] = jnp.concatenate(found[c] + others, axis=0)


def from_neighbours(near_ref, far_ref, base):
    first_core = lax.axis_index("sub") == 0
    left = iota((1, 128), 1) < 64
    out = []
    for c in range(3):
        rows = slice(base + 8 * c, base + 8 * c + 8)
        near = near_ref[rows, 0:128]
        far = far_ref[rows, 0:128]
        before = jnp.where(first_core, far, near)
        after = jnp.where(first_core, near, far)
        before_turned = pltpu.roll(before, 64, 1)
        after_turned = pltpu.roll(after, 64, 1)
        out += [
            before[5:6],
            jnp.where(left, before_turned[4:5], after_turned[4:5]),
            after[3:4],
            before[2:3],
            jnp.where(left, before_turned[1:2], after_turned[1:2]),
            after[0:1],
            jnp.zeros((2, 128), F32),
        ]
    return jnp.concatenate(out, axis=0)


def pack_kernel(
    loads_hbm, coefs_hbm, move_hbm, face_hbm, field_hbm, nodes_hbm, stiff_hbm, far_hbm, near_out,
    other_out, places_ref, state_ref, loads_ref, coefs_ref, move_ref, nodes_ref, stiff_ref,
    face_ref, field_ref, far_rows, sems,
):
    pairs = (
        (move_hbm, move_ref),
        (coefs_hbm, coefs_ref),
        (loads_hbm, loads_ref),
        (face_hbm, face_ref),
        (field_hbm, field_ref),
        (nodes_hbm, nodes_ref),
        (stiff_hbm, stiff_ref),
    )
    copies = [
        pltpu.make_async_copy(source, target, sems.at[i]) for i, (source, target) in enumerate(pairs)
    ]
    for copy in copies:
        copy.start()
    for copy in copies[:3]:
        copy.wait()
    me = lax.axis_index(AXES)
    first_core = lax.axis_index("sub") == 0
    near = jnp.where(first_core, me + 1, me - 1)
    other = jnp.where(first_core, me - 1, me + 1)
    target = move_ref[0:1, :]
    place = move_ref[2:3, :]
    code = jnp.where(
        target == me,
        -1,
        jnp.where(
            target == near,
            DEVICES + place,
            jnp.where(target == other, DEVICES + NEAR_CAP + place, target),
        ),
    )
    rows = DEVICES + 2 * NEAR_CAP
    chosen = jnp.where(code == iota((rows, ELEM), 0), 1.0, 0.0)
    slot = (move_ref[1:2, :] + 1).astype(F32)
    records = jnp.concatenate(
        [loads_ref[...], coefs_ref[...], slot, jnp.zeros((61, ELEM), F32)], axis=0
    )
    packed = lax.dot_general(
        chosen,
        records,
        (((1,), (1,)), ((), ())),
        precision=lax.Precision.HIGHEST,
        preferred_element_type=F32,
    )
    far_rows[:, 0, :] = packed[:DEVICES]
    far_copy = pltpu.make_async_copy(far_rows, far_hbm, sems.at[7])
    far_copy.start()
    near_out[0:NEAR_CAP, :] = packed[DEVICES : DEVICES + NEAR_CAP]
    other_out[0:NEAR_CAP, :] = packed[DEVICES + NEAR_CAP :]
    near_out[NEAR_CAP:, :] = jnp.zeros((24, 256), F32)
    for copy in copies[3:5]:
        copy.wait()
    places_ref[...] = jnp.zeros((8, 128), jnp.int32)
    places_ref[0:1, :] = face_ref[0:1, 0:128]
    places_ref[1:2, 0:64] = face_ref[0:1, 128:192]
    places_ref[1:2, 64:128] = face_ref[1:2, 128:192]
    places_ref[2:3, :] = face_ref[1:2, 0:128]
    state_ref[...] = jnp.zeros_like(state_ref)
    for c in range(3):
        for h in range(OWN_ROWS):
            state_ref[32 * c + h : 32 * c + h + 1, :] = field_ref[c : c + 1, 256 * h : 256 * h + 256]
    take_shared(state_ref, places_ref[...], near_out, NEAR_CAP, False)
    other_out[NEAR_CAP:, :] = near_out[NEAR_CAP:, :]
    for copy in copies[5:]:
        copy.wait()
    far_copy.wait()


def index_kernel(
    state_ref,
    places_ref,
    nodes_ref,
    stiff_ref,
    index_ref,
    shared_index_ref,
    unshared_ref,
    blocks_ref,
    gathered_ref,
    positions,
    found,
):
    nodes = nodes_ref[...]
    ghost = nodes - OWN
    ahead = ghost - FACE
    shared = jnp.where(ahead < 0, ghost, jnp.where(ahead < 128, ahead + 256, ahead + 64))
    index_ref[...] = jnp.where(ghost < 0, nodes, OWN + shared)
    places = places_ref[...]
    numbers = (128 * iota((3, 128), 0) + iota((3, 128), 1) + 1).astype(F32)
    positions[...] = expand_own_faces(places, [numbers], 2)
    line = iota((32, 256), 0)
    unshared_ref[...] = jnp.where((positions[...] == 0.0) & (line < OWN_ROWS), 1.0, 0.0)
    gather_own(state_ref, index_ref, gathered_ref, positions, found)
    shared_index_ref[...] = jnp.where(
        ghost < 0, found[...].astype(jnp.int32) - 1, shared + 3 * 128
    )
    for i in range(2):
        high, low = split(stiff_ref[i])
        high = high.astype(BF16)
        blocks_ref[DOFS * i : DOFS * i + DOFS, :] = high
        blocks_ref[DOFS * (2 + i) : DOFS * (3 + i), :] = low.astype(BF16)


def build_hot(index_ref, hot_ref, width):
    low = (index_ref[...] & (width - 1)).astype(F32)
    lanes = iota((16, width), 1).astype(F32).astype(BF16)
    one = jnp.ones((), BF16)
    zero = jnp.zeros((), BF16)
    for half in range(2):
        turned = low[:, half * 128 : half * 128 + 128].T.astype(BF16)
        for b in range(8):
            columns = turned[16 * b : 16 * b + 16]
            for n in range(PER):
                top = 256 * n + half * 128 + 16 * b
                column = jnp.broadcast_to(columns[:, n : n + 1], (16, width))
                hot_ref[top : top + 16, :] = jnp.where(column == lanes, one, zero)


def multiply_blocks(blocks_ref, rows):
    high, low = split(rows)
    high = high.astype(BF16)
    low = low.astype(BF16)
    block_high = blocks_ref[: 2 * DOFS]
    block_low = blocks_ref[2 * DOFS :]
    return (
        jnp.dot(block_low, high, preferred_element_type=F32)
        + jnp.dot(block_high, low, preferred_element_type=F32)
        + jnp.dot(block_high, high, preferred_element_type=F32)
    )


def products_kernel(
    near_in,
    other_in,
    field_message,
    gathered_in,
    shared_index_ref,
    blocks_ref,
    shared_field,
    products_ref,
    gathered,
):
    shared_field[...] = field_message[NEAR_CAP:, 0:128] + from_neighbours(near_in, other_in, NEAR_CAP)
    gather_shared(shared_field, shared_index_ref, gathered_in, gathered, 3)
    products_ref[...] = multiply_blocks(blocks_ref, gathered[...])


def place_kernel(
    loads_ref,
    coefs_ref,
    move_ref,
    far_ref,
    near_in,
    other_in,
    stiff_ref,
    products_ref,
    nodes_ref,
    places_ref,
    hot_ref,
    moved_loads,
    moved_coefs,
    coefs_out,
    partial_ref,
    diagonal_ref,
    message,
    values,
    value_high,
    value_low,
    sums,
    kept_loads,
    sems,
):
    me = lax.axis_index(AXES)
    received = jnp.concatenate(
        [far_ref[:, 0, :], near_in[0:NEAR_CAP, :], other_in[0:NEAR_CAP, :]], axis=0
    )
    rows = DEVICES + 2 * NEAR_CAP
    slot = received[:, DOFS + 2 : DOFS + 3].astype(jnp.int32)
    chosen = jnp.where(slot == iota((rows, ELEM), 1) + 1, 1.0, 0.0)
    arrived = lax.dot_general(
        received,
        chosen,
        (((0,), (0,)), ((), ())),
        precision=lax.Precision.HIGHEST,
        preferred_element_type=F32,
    )
    stays = move_ref[0:1, :] == me
    loads = jnp.where(stays, loads_ref[...], 0.0) + arrived[:DOFS]
    coefs = jnp.where(stays, coefs_ref[...], 0.0) + arrived[DOFS : DOFS + 2]
    kept_loads[...] = loads
    coefs_out[...] = coefs
    copies = (
        pltpu.make_async_copy(kept_loads, moved_loads, sems.at[0]),
        pltpu.make_async_copy(coefs_out, moved_coefs, sems.at[1]),
    )
    for copy in copies:
        copy.start()
    values[0:DOFS, :] = loads - (
        products_ref[0:DOFS, :] * coefs[0:1, :] + products_ref[DOFS:, :] * coefs[1:2, :]
    )
    eye = iota((DOFS, DOFS), 0) == iota((DOFS, DOFS), 1)
    first_diag = jnp.sum(jnp.where(eye, stiff_ref[0], 0.0), axis=1, keepdims=True)
    second_diag = jnp.sum(jnp.where(eye, stiff_ref[1], 0.0), axis=1, keepdims=True)
    values[DOFS:, :] = first_diag * coefs[0:1, :] + second_diag * coefs[1:2, :]
    build_hot(nodes_ref, hot_ref, 256)
    scatter_elements(nodes_ref, hot_ref, values, value_high, value_low, sums, 6)
    partial_ref[...] = add_parts(sums, 0, 6)
    diagonal_ref[...] = add_parts(sums, 3, 6)
    take_shared(partial_ref, places_ref[...], message, 0, True)
    take_shared(diagonal_ref, places_ref[...], message, 24, True)
    for copy in copies:
        copy.wait()


def apply_operator(
    shared_update, gathered_in, shared_index_ref, coefs_ref, hot_ref, blocks_ref, values_ref,
    message, gathered, value_high, value_low, sums,
):
    gather_shared(shared_update, shared_index_ref, gathered_in, gathered, 0)
    products = multiply_blocks(blocks_ref, gathered[...])
    values_ref[...] = products[:DOFS] * coefs_ref[0:1, :] + products[DOFS:] * coefs_ref[1:2, :]
    scatter_shared(shared_index_ref, hot_ref, values_ref, value_high, value_low, sums, message)


def inverse_of(diagonal):
    return jnp.where(diagonal == 0.0, 0.0, 1.0 / diagonal)


def begin_unshared(
    step, partial_ref, diagonal_ref, unshared_ref, field_ref, nodes_ref, hot_ref, shared_index_ref,
    inverse_out, update_out, field_out, gathered_out, hot_shared_ref,
):
    build_hot(shared_index_ref, hot_shared_ref, 128)
    unshared = jnp.concatenate([unshared_ref[...]] * 3, axis=0)
    inverse = jnp.where(unshared > 0.0, inverse_of(diagonal_ref[...]), 0.0)
    update = step[1] * (partial_ref[...] * inverse)
    inverse_out[...] = inverse
    update_out[...] = update
    field_out[...] = field_ref[...] + update
    gather_mixed(update_out, nodes_ref, hot_ref, gathered_out)


def begin_shared(
    step, message_in, near_in, other_in, shared_field, gathered_in, shared_index_ref, coefs_ref,
    hot_ref, blocks_ref, residual_out, inverse_out, update_out, field_out, values_ref, message,
    gathered, value_high, value_low, sums,
):
    residual = message_in[0:24, :] + from_neighbours(near_in, other_in, 0)
    inverse = inverse_of(message_in[24:48, :] + from_neighbours(near_in, other_in, 24))
    update = step[1] * (residual * inverse)
    residual_out[...] = residual
    inverse_out[...] = inverse
    update_out[...] = update
    field_out[...] = shared_field[...] + update
    apply_operator(
        update_out, gathered_in, shared_index_ref, coefs_ref, hot_ref, blocks_ref, values_ref,
        message, gathered, value_high, value_low, sums,
    )


def next_update(step, residual, inverse, update):
    changed = step[1] * (residual * inverse)
    return step[0] * update + changed if step[0] else changed


def step_unshared(
    step, values_ref, residual_ref, inverse_ref, update_ref, field_ref, nodes_ref, hot_ref,
    residual_out, update_out, field_out, gathered_out, value_high, value_low, sums,
):
    scatter_elements(nodes_ref, hot_ref, values_ref, value_high, value_low, sums, 3)
    residual = residual_ref[...] - add_parts(sums, 0, 3)
    update = next_update(step, residual, inverse_ref[...], update_ref[...])
    residual_out[...] = residual
    update_out[...] = update
    field_out[...] = field_ref[...] + update
    gather_mixed(update_out, nodes_ref, hot_ref, gathered_out)


def step_shared(
    step, message_in, near_in, other_in, residual_ref, inverse_ref, update_ref, field_ref,
    gathered_in, shared_index_ref, coefs_ref, hot_ref, blocks_ref, residual_out, update_out,
    field_out, values_ref, message, gathered, value_high, value_low, sums,
):
    residual = residual_ref[...] - (message_in[...] + from_neighbours(near_in, other_in, 0))
    update = next_update(step, residual, inverse_ref[...], update_ref[...])
    residual_out[...] = residual
    update_out[...] = update
    field_out[...] = field_ref[...] + update
    apply_operator(
        update_out, gathered_in, shared_index_ref, coefs_ref, hot_ref, blocks_ref, values_ref,
        message, gathered, value_high, value_low, sums,
    )


def last_unshared(
    step, values_ref, residual_ref, inverse_ref, update_ref, field_ref, nodes_ref, hot_ref, field_out,
    value_high, value_low, sums,
):
    scatter_elements(nodes_ref, hot_ref, values_ref, value_high, value_low, sums, 3)
    residual = residual_ref[...] - add_parts(sums, 0, 3)
    field_out[...] = field_ref[...] + next_update(step, residual, inverse_ref[...], update_ref[...])


def last_shared(
    step, message_in, near_in, other_in, residual_ref, inverse_ref, update_ref, shared_field,
    field_ref, unshared_ref, places_ref, out_ref,
):
    residual = residual_ref[...] - (message_in[...] + from_neighbours(near_in, other_in, 0))
    shared = shared_field[...] + next_update(step, residual, inverse_ref[...], update_ref[...])
    faces = expand_own_faces(places_ref[...], [shared[8 * c : 8 * c + 3] for c in range(3)], 3)
    unshared = jnp.concatenate([unshared_ref[...]] * 3, axis=0)
    field = jnp.where(unshared > 0.0, field_ref[...], faces)
    for c in range(3):
        for h in range(OWN_ROWS):
            out_ref[c : c + 1, 256 * h : 256 * h + 256] = field[32 * c + h : 32 * c + h + 1, :]


def shaped(*shape, dtype=F32):
    return jax.ShapeDtypeStruct(shape, dtype)


def steps():
    scaled_center = center / half_width
    found = []
    for _ in range(SWEEPS):
        found.append((0.0, 1.0 / center))
        ratio = 1.0 / scaled_center
        for _ in range(DEGREE - 1):
            ratio_next = 1.0 / (2.0 * scaled_center - ratio)
            found.append((ratio_next * ratio, 2.0 * ratio_next / half_width))
            ratio = ratio_next
    return found


NEAR_PAIRS = [(i, i ^ 1) for i in range(DEVICES)]
OTHER_PAIRS = [
    pair for i in range(1, DEVICES - 1, 2) for pair in ((i, i + 1), (i + 1, i))
]


def exchange(near_message, other_message):
    other = lax.ppermute(other_message, AXES, OTHER_PAIRS)
    near = lax.ppermute(near_message, AXES, NEAR_PAIRS)
    return near, other


def call(kernel, outs, scratch=(), **options):
    return pl.pallas_call(
        kernel,
        out_shape=outs,
        scratch_shapes=list(scratch),
        compiler_params=pltpu.CompilerParams(vmem_limit_bytes=20 << 20),
        **options,
    )


STATE = shaped(96, 256)
SHARED = shaped(24, 128)
ELEMENT_ROWS = shaped(DOFS, ELEM)


def rows(count):
    return pltpu.VMEM((count, ELEM), F32)


def local(
    start_field, element_loads, element_coefs, element_nodes, move_list, face_nodes, stiffness
):
    integers = functools.partial(shaped, dtype=jnp.int32)
    far, near, other, places, field, loads, coefs, moves, nodes, stiff = call(
        pack_kernel,
        (
            shaped(DEVICES, 1, 256),
            shaped(40, 256),
            shaped(40, 256),
            integers(8, 128),
            STATE,
            ELEMENT_ROWS,
            shaped(2, ELEM),
            integers(3, ELEM),
            integers(PER, ELEM),
            shaped(2, DOFS, DOFS),
        ),
        [
            pltpu.VMEM((2, FACE), jnp.int32),
            pltpu.VMEM((3, OWN), F32),
            pltpu.VMEM((DEVICES, 1, 256), F32),
            pltpu.SemaphoreType.DMA((8,)),
        ],
        in_specs=[pl.BlockSpec(memory_space=pltpu.HBM)] * 7,
        out_specs=[pl.BlockSpec(memory_space=pltpu.HBM)]
        + [pl.BlockSpec(memory_space=pltpu.VMEM)] * 9,
    )(*[pltpu.with_memory_space_constraint(x, pltpu.HBM) for x in (element_loads, element_coefs, move_list, face_nodes, start_field, element_nodes, stiffness)])
    field_message = near
    near, other = exchange(near, other)
    far = lax.all_to_all(far, AXES, split_axis=0, concat_axis=0, tiled=True)
    nodes, shared_index, unshared, blocks, gathered = call(
        index_kernel,
        (
            integers(PER, ELEM),
            integers(PER, ELEM),
            shaped(32, 256),
            shaped(4 * DOFS, DOFS, dtype=BF16),
            ELEMENT_ROWS,
        ),
        [rows(32), rows(PER)],
    )(field, places, nodes, stiff)
    shared_field, products = call(
        products_kernel, (SHARED, shaped(2 * DOFS, ELEM)), [rows(DOFS)]
    )(near, other, field_message, gathered, shared_index, blocks)
    hot, moved_loads, moved_coefs, coefs, partial, diagonal, message = call(
        place_kernel,
        (
            shaped(PER * ELEM, 256, dtype=BF16),
            ELEMENT_ROWS,
            shaped(2, ELEM),
            shaped(2, ELEM),
            STATE,
            STATE,
            shaped(48, 128),
        ),
        [rows(2 * DOFS), rows(2 * DOFS), rows(2 * DOFS), rows(384), rows(DOFS)]
        + [pltpu.SemaphoreType.DMA((2,))],
        out_specs=[
            pl.BlockSpec(memory_space=pltpu.HBM if i in (1, 2) else pltpu.VMEM) for i in range(7)
        ],
    )(loads, coefs, moves, far, near, other, stiff, products, nodes, places)
    near, other = exchange(message, message)
    plan = steps()
    scratch = [rows(DOFS)] * 3 + [pltpu.VMEM((48, 128), F32)]
    window_scratch = [rows(DOFS)] * 2 + [rows(192)]
    residual = partial
    inverse, update, field, gathered, hot_shared = call(
        functools.partial(begin_unshared, plan[0]),
        (STATE, STATE, STATE, ELEMENT_ROWS, shaped(PER * ELEM, 128, dtype=BF16)),
    )(partial, diagonal, unshared, field, nodes, hot, shared_index)
    fixed = (shared_index, coefs, hot_shared, blocks)
    shared_residual, shared_inverse, shared_update, shared_field, values, message = call(
        functools.partial(begin_shared, plan[0]),
        (SHARED, SHARED, SHARED, SHARED, ELEMENT_ROWS, SHARED),
        scratch,
    )(message, near, other, shared_field, gathered, *fixed)
    for step in plan[1:-1]:
        near, other = exchange(message, message)
        residual, update, field, gathered = call(
            functools.partial(step_unshared, step),
            (STATE, STATE, STATE, ELEMENT_ROWS),
            window_scratch,
        )(values, residual, inverse, update, field, nodes, hot)
        shared_residual, shared_update, shared_field, values, message = call(
            functools.partial(step_shared, step),
            (SHARED, SHARED, SHARED, ELEMENT_ROWS, SHARED),
            scratch,
        )(
            message, near, other, shared_residual, shared_inverse, shared_update, shared_field,
            gathered, *fixed,
        )
    near, other = exchange(message, message)
    field = call(
        functools.partial(last_unshared, plan[-1]), STATE, window_scratch
    )(values, residual, inverse, update, field, nodes, hot)
    field = call(functools.partial(last_shared, plan[-1]), shaped(3, OWN))(
        message, near, other, shared_residual, shared_inverse, shared_update, shared_field, field,
        unshared, places,
    )
    return field, moved_loads, moved_coefs


def solution(mesh):
    split_columns = P(None, AXES)
    return jax.shard_map(
        local,
        mesh=mesh,
        in_specs=(split_columns,) * 6 + (P(),),
        out_specs=(split_columns,) * 3,
        check_vma=False,
    )
```
